32 devices in a mesh: wide: 8 (over z, x), narrow: 4 (over y, core).
Axes of the slice: x: 2, y: 2, z: 4, core: 2. Of those that a mesh axis runs over, the one named last changes fastest.
Arguments:
- tokens: bfloat16 [32768, 384], P(('wide', 'narrow')), may hold values from -6 to 6
- conditions: bfloat16 [128, 384], P(('wide', 'narrow')), may hold values from -6 to 6
- routes: int32 [32768, 2], P(('wide', 'narrow')), may hold values from 0 to 7, all different within a row; in each aligned block of 1024 rows (0 to 1023, 1024 to 2047, ...) at most 384 rows name the same one
- resolution: int32 [32], P(('wide', 'narrow')), may hold values from 0 to 1
- step_count: int32 [1], replicated, may hold values from 1 to 20
- cotangent: bfloat16 [32768, 384], P(('wide', 'narrow')), may hold values from -6 to 6
- w_square: float32 [9, 384, 384], P(None, 'narrow', 'wide'), may hold values from -0.3125 to 0.3125
- w_out: float32 [384, 384], P('narrow', 'wide'), may hold values from -0.875 to 0.875
- w_router: float32 [8, 384], P('narrow', 'wide'), may hold values from -0.21875 to 0.21875
- w_up: float32 [10, 1536, 384], P(None, 'narrow', 'wide'), may hold values from -0.3125 to 0.3125
- w_down: float32 [10, 1536, 384], P(None, 'narrow', 'wide'), may hold values from -0.15625 to 0.15625
- b_ada: float32 [2304], P(('wide', 'narrow')), may hold values from -1.2 to 1.2
- moment_square: float32 [9, 384, 384], P(None, 'narrow', 'wide'), may hold values from -112 to 112
- moment_out: float32 [384, 384], P('narrow', 'wide'), may hold values from -112 to 112
- moment_router: float32 [8, 384], P('narrow', 'wide'), may hold values from -56 to 56
- moment_up: float32 [10, 1536, 384], P(None, 'narrow', 'wide'), may hold values from -56 to 56
- moment_down: float32 [10, 1536, 384], P(None, 'narrow', 'wide'), may hold values from -112 to 112
- moment_bias: float32 [2304], P(('wide', 'narrow')), may hold values from -512 to 512
- ema_square: float32 [9, 384, 384], P(None, 'narrow', 'wide'), may hold values from -0.3125 to 0.3125
- ema_out: float32 [384, 384], P('narrow', 'wide'), may hold values from -0.875 to 0.875
- ema_router: float32 [8, 384], P('narrow', 'wide'), may hold values from -0.21875 to 0.21875
- ema_up: float32 [10, 1536, 384], P(None, 'narrow', 'wide'), may hold values from -0.3125 to 0.3125
- ema_down: float32 [10, 1536, 384], P(None, 'narrow', 'wide'), may hold values from -0.15625 to 0.15625
- ema_bias: float32 [2304], P(('wide', 'narrow')), may hold values from -1.2 to 1.2
Outputs:
- output: bfloat16 [32768, 384], P(('wide', 'narrow'))
- grad_in: float32 [32768, 384], P(('wide', 'narrow'))
- state_square: float32 [9, 384, 384], P(None, 'narrow', 'wide')
- master_square: float32 [9, 384, 384], P(None, 'narrow', 'wide')
- average_square: float32 [9, 384, 384], P(None, 'narrow', 'wide')
- state_out: float32 [384, 384], P('narrow', 'wide')
- master_out: float32 [384, 384], P('narrow', 'wide')
- average_out: float32 [384, 384], P('narrow', 'wide')
- state_router: float32 [8, 384], P('narrow', 'wide')
- master_router: float32 [8, 384], P('narrow', 'wide')
- average_router: float32 [8, 384], P('narrow', 'wide')
- state_up: float32 [10, 1536, 384], P(None, 'narrow', 'wide')
- master_up: float32 [10, 1536, 384], P(None, 'narrow', 'wide')
- average_up: float32 [10, 1536, 384], P(None, 'narrow', 'wide')
- state_down: float32 [10, 1536, 384], P(None, 'narrow', 'wide')
- master_down: float32 [10, 1536, 384], P(None, 'narrow', 'wide')
- average_down: float32 [10, 1536, 384], P(None, 'narrow', 'wide')
- state_bias: float32 [2304], P(('wide', 'narrow'))
- master_bias: float32 [2304], P(('wide', 'narrow'))
- average_bias: float32 [2304], P(('wide', 'narrow'))
The draws below stay inside these ranges and needn't reach their ends.
Inputs may be any that keep to these rules, and one draw needn't show every extreme that they name: `routes`: the 2 experts of a row differ. In the rows of one device no expert is named by more than 384 rows, a bound that some block reaches. `resolution`: 1 marks a device whose tokens are images of 1024 consecutive rows, 0 one whose tokens are images of 256 consecutive rows.
All inputs are finite; a program needn't handle non-finite values.
Results may differ from the reference program's by a relative error of at most 0.02.
The reference program's roundings to bfloat16 on the way count: a program that leaves them out, or rounds other values in their place, can miss the bound.
Values may be sent and summed in bfloat16 or wider, within the bound.
No kernel may reach another device: no remote copies, remote signals or barrier semaphores. Data moves between devices by JAX's collectives and lax.ppermute only.
A program may use at most 256 MiB of HBM per device.

```python
import math
from functools import partial
import jax
import jax.numpy as jnp
import numpy as np
from jax import lax

D = 384
HEADS = 6
HEAD = 64
FF = 1536
TOP = 2
ROUTED = 8
SHORT = 256
LONG = 1024
TOK_DEV = 1024
TOKENS = 32768
EXPERTS = 10
CAP = 384
DEVICES = 32


def set_ends(array, own_key, low, top_value):
    index_at = [jax.random.randint(jax.random.fold_in(own_key, axis), (), 0, length) for axis, length in enumerate(array.shape)]
    longest = array.shape.index(max(array.shape))
    neighbour = index_at[:longest] + [(index_at[longest] + 1) % array.shape[longest]] + index_at[longest + 1:]
    return array.at[tuple(index_at)].set(low).at[tuple(neighbour)].set(top_value)


def levels(rng, dims, cuts, low, high):
    level = 1.0
    for position, blocks in cuts:
        draws = jax.random.uniform(jax.random.fold_in(jax.random.fold_in(rng, 6), position), (blocks,), jnp.float32, low / len(cuts), high / len(cuts))
        level = level * jnp.repeat(jnp.exp(draws), dims[position] // blocks).reshape((-1,) + (1,) * (len(dims) - 1 - position))
    return level


def assign_block(key, own, number, rows, amount, top, most, slope):
    sequence = jax.random.permutation(key, amount)
    heavy_load, ordinary = load_shares(amount, rows * top, most, slope, True), load_shares(amount, rows * top, most, slope, False)
    places = jnp.arange(amount)

    def named(lengths, offset_by):
        used = int((lengths > 0).sum())
        fixed = max(1, used // 4)
        shifted = fixed + (places - fixed + offset_by * (used - fixed)) % max(1, amount - fixed)
        return jnp.zeros((amount,), jnp.int32).at[sequence[jnp.where(places < fixed, places, shifted)]].set(jnp.asarray(lengths, jnp.int32))

    lengths = jnp.where(number % 4 == 0, named(heavy_load, number // 4), named(ordinary, number - number // 4 - 1))
    mixed = jax.random.permutation(jax.random.fold_in(own, 3), amount)
    source_of, sink = mixed[0:amount // 2 * 2:2], mixed[1:amount // 2 * 2:2]
    slack = jnp.minimum(lengths[source_of] - 1, most - lengths[sink]) // 2
    slack = jnp.where((source_of == sequence[0]) | (sink == sequence[0]) | (lengths[sink] == 0), 0, jnp.maximum(slack, 0))
    shifted = jax.random.randint(jax.random.fold_in(own, 4), (amount // 2,), 0, 1 << 20) % (slack + 1)
    lengths = lengths.at[source_of].add(-shifted).at[sink].add(shifted)
    items = jnp.searchsorted(jnp.cumsum(lengths), jnp.arange(rows * top), side="right").astype(jnp.int32)
    listing = items.reshape(top, rows).T
    listing = listing[jax.random.permutation(jax.random.fold_in(own, 1), rows)]
    offset_by = jax.random.randint(jax.random.fold_in(own, 2), (rows, 1), 0, top)
    return jnp.take_along_axis(listing, (jnp.arange(top)[None, :] + offset_by) % top, axis=1)


def load_shares(count, total, most, skew, full):
    portions = [(1 << 20) // math.isqrt(standing ** skew) + 1 for standing in range(1, count + 1)]
    largest = most if full else min(most, max(-(-total // count), total * portions[0] // sum(portions)))
    least = 1 if total - largest >= count - 1 else 0
    given, rest = [largest] + [least] * (count - 1), total - largest - least * (count - 1)
    while rest > 0:
        free = [i for i in range(1, count) if given[i] < largest] or [i for i in range(1, count) if given[i] < most]
        mass, remaining = sum([portions[i] for i in free]), rest
        for i in free:
            extra = min(most - given[i], max(1, remaining * portions[i] // mass), rest)
            given[i] = given[i] + extra
            rest = rest - extra
    return np.array(given)


def normal_values(rng, extent, width, reach, cuts=(), kind=jnp.bfloat16):
    array = jax.random.normal(rng, extent, jnp.float32) * width
    if len(cuts) > 0:
        array = levels(rng, extent, cuts, -0.22, 0.18) * array
    return jnp.clip(array, min=-reach, max=reach).astype(kind)


def setup_inputs(seed: int = 0) -> dict:
    splits = jax.random.split(jax.random.key(seed), 25)
    tokens = normal_values(splits[0], (TOKENS, D), 1.0, 6.0, ((0, 32),))
    conditions = normal_values(splits[1], (TOKENS // SHORT, D), 1.0, 6.0, ((0, 32),))
    routes_keys = jax.random.split(jax.random.fold_in(splits[2], 1), TOKENS // TOK_DEV)
    routes_turns = jax.random.permutation(jax.random.fold_in(splits[2], 3), TOKENS // TOK_DEV)
    routes = jax.vmap(lambda own, number: assign_block(jax.random.fold_in(splits[2], 2), own, number, TOK_DEV, ROUTED, TOP, CAP, 1))(routes_keys, routes_turns).reshape((TOKENS, TOP))
    resolution = set_ends(jax.random.randint(splits[3], (DEVICES,), 0, 2), jax.random.fold_in(splits[3], 1), 0, 1).astype(jnp.int32)
    step_count = jax.random.randint(splits[4], (1,), 1, 21).astype(jnp.int32)
    cotangent = normal_values(splits[5], (TOKENS, D), 1.0, 6.0, ((0, 32),))
    w_square = normal_values(splits[6], (9, D, D), D ** -0.5, 0.3125, ((1, 4), (2, 8)), jnp.float32)
    w_out = normal_values(splits[7], (D, D), (D // 8) ** -0.5, 0.875, ((0, 4), (1, 8)), jnp.float32)
    w_router = normal_values(splits[8], (ROUTED, D), (2 * D) ** -0.5, 0.21875, ((0, 4), (1, 8)), jnp.float32)
    w_up = normal_values(splits[9], (EXPERTS, FF, D), D ** -0.5, 0.3125, ((1, 4), (2, 8)), jnp.float32)
    w_down = normal_values(splits[10], (EXPERTS, FF, D), FF ** -0.5, 0.15625, ((1, 4), (2, 8)), jnp.float32)
    b_ada = normal_values(splits[11], (6 * D,), 0.2, 1.2, ((0, 32),), jnp.float32)
    moment_square = normal_values(splits[12], (9, D, D), (0.1 * TOKENS ** 0.5), 112.0, ((1, 4), (2, 8)), jnp.float32)
    moment_out = normal_values(splits[13], (D, D), (0.1 * TOKENS ** 0.5), 112.0, ((0, 4), (1, 8)), jnp.float32)
    moment_router = normal_values(splits[14], (ROUTED, D), (0.05 * TOKENS ** 0.5), 56.0, ((0, 4), (1, 8)), jnp.float32)
    moment_up = normal_values(splits[15], (EXPERTS, FF, D), (0.05 * TOKENS ** 0.5), 56.0, ((1, 4), (2, 8)), jnp.float32)
    moment_down = normal_values(splits[16], (EXPERTS, FF, D), (0.1 * TOKENS ** 0.5), 112.0, ((1, 4), (2, 8)), jnp.float32)
    moment_bias = normal_values(splits[17], (6 * D,), (0.5 * TOKENS ** 0.5), 512.0, ((0, 32),), jnp.float32)
    ema_square = normal_values(splits[18], (9, D, D), D ** -0.5, 0.3125, ((1, 4), (2, 8)), jnp.float32)
    ema_out = normal_values(splits[19], (D, D), (D // 8) ** -0.5, 0.875, ((0, 4), (1, 8)), jnp.float32)
    ema_router = normal_values(splits[20], (ROUTED, D), (2 * D) ** -0.5, 0.21875, ((0, 4), (1, 8)), jnp.float32)
    ema_up = normal_values(splits[21], (EXPERTS, FF, D), D ** -0.5, 0.3125, ((1, 4), (2, 8)), jnp.float32)
    ema_down = normal_values(splits[22], (EXPERTS, FF, D), FF ** -0.5, 0.15625, ((1, 4), (2, 8)), jnp.float32)
    ema_bias = normal_values(splits[23], (6 * D,), 0.2, 1.2, ((0, 32),), jnp.float32)
    return dict(tokens=tokens, conditions=conditions, routes=routes, resolution=resolution, step_count=step_count, cotangent=cotangent, w_square=w_square, w_out=w_out, w_router=w_router, w_up=w_up, w_down=w_down, b_ada=b_ada, moment_square=moment_square, moment_out=moment_out, moment_router=moment_router, moment_up=moment_up, moment_down=moment_down, moment_bias=moment_bias, ema_square=ema_square, ema_out=ema_out, ema_router=ema_router, ema_up=ema_up, ema_down=ema_down, ema_bias=ema_bias)


PRECISE = lax.Precision.HIGHEST
EPSILON = 1e-06
NS_FIRST = 3.4445
NS_SECOND = -4.775
NS_THIRD = 2.0315
MOMENTUM = 0.95
MOMENTUM_VECTOR = 0.5
RATE = 0.25
RATE_VECTOR = 0.05

@jax.custom_vjp
def low(v):
    return lax.optimization_barrier(v.astype(jnp.bfloat16)).astype(jnp.float32)

@jax.custom_vjp
def low_back(v):
    return v

def low_keep(v):
    return (low(v), None)

def low_pass(kept, grad):
    return (grad,)

def back_keep(v):
    return (v, None)

def back_low(kept, grad):
    return (low(grad),)
low.defvjp(low_keep, low_pass)
low_back.defvjp(back_keep, back_low)

def modulate(seg_rows, shift_by, scale_by):
    center = seg_rows - lax.optimization_barrier(jnp.mean(seg_rows, axis=-1, keepdims=True))
    normed = center * lax.rsqrt(lax.optimization_barrier(jnp.mean(center * center, axis=-1, keepdims=True)) + EPSILON)
    return normed * (1.0 + scale_by) + shift_by

def slot_table(route_rows):
    flat_routes = route_rows.reshape(-1)
    hot_table = (flat_routes[:, None] == jnp.arange(ROUTED, dtype=jnp.int32)[None, :]).astype(jnp.int32)
    earlier = jnp.cumsum(hot_table, axis=0, dtype=jnp.int32) - hot_table
    place_in = lax.optimization_barrier(jnp.sum(earlier * hot_table, axis=1, dtype=jnp.int32))
    slot_ids = flat_routes * CAP + place_in
    sources = jnp.arange(slot_ids.shape[0], dtype=jnp.int32) // TOP
    slot_owner = jnp.zeros((ROUTED * CAP,), jnp.int32).at[slot_ids].set(sources)
    return (slot_ids, slot_owner)

def attention(projected, length):
    image_count = projected.shape[1] // length
    split_parts = projected.reshape(3, image_count, length, HEADS, HEAD)
    scores = low_back(jnp.einsum('bqhe,bkhe->bhqk', split_parts[0], split_parts[1], precision=PRECISE) * HEAD ** (-0.5))
    weights = low(jax.nn.softmax(scores, axis=-1))
    mixed_heads = jnp.einsum('bhqk,bkhe->bqhe', weights, split_parts[2], precision=PRECISE)
    return low(low_back(mixed_heads.reshape(-1, D)))

def device_layer(tokens, conditions, route_rows, res_group, rounded):
    square, outward, router, upward, downward, bias_vec = rounded
    segments = tokens.shape[0] // SHORT
    seg_ratio = LONG // SHORT
    first_seg = jnp.arange(segments, dtype=jnp.int32) // seg_ratio * seg_ratio
    chosen = jnp.where(res_group == 1, conditions[first_seg], conditions)
    cond_low = low(jax.nn.silu(chosen))
    modulation = jnp.einsum('sd,jde->sje', cond_low, square[3:], precision=PRECISE) + bias_vec.reshape(6, D)
    seg_rows = tokens.reshape(segments, SHORT, D)
    hidden_one = low(modulate(seg_rows, modulation[:, 0:1], modulation[:, 1:2]).reshape(-1, D))
    projected = low(low_back(jnp.einsum('td,jde->jte', hidden_one, square[:3], precision=PRECISE)))
    attended = lax.cond(res_group == 1, partial(attention, length=LONG), partial(attention, length=SHORT), projected)
    attn_out = low_back(jnp.dot(attended, outward, precision=PRECISE))
    mid_state = tokens + (attn_out.reshape(segments, SHORT, D) * modulation[:, 2:3]).reshape(-1, D)
    hidden_two = low(modulate(mid_state.reshape(segments, SHORT, D), modulation[:, 3:4], modulation[:, 4:5]).reshape(-1, D))
    logits = low_back(jnp.einsum('td,rd->tr', hidden_two, router, precision=PRECISE))
    gate_probs = jax.nn.softmax(jnp.take_along_axis(logits, route_rows, axis=1), axis=1)
    slot_ids, slot_owner = slot_table(route_rows)
    inputs = hidden_two[slot_owner].reshape(ROUTED, CAP, D)
    pre_act = low_back(jnp.einsum('ecd,efd->ecf', inputs, upward[:ROUTED], precision=PRECISE))
    act_low = low(jax.nn.gelu(pre_act, approximate=True))
    produced = low_back(jnp.einsum('ecf,efd->ecd', act_low, downward[:ROUTED], precision=PRECISE)).reshape(-1, D)
    routed = lax.optimization_barrier(jnp.sum(produced[slot_ids].reshape(-1, TOP, D) * gate_probs[:, :, None], axis=1))
    shared_pre = low_back(jnp.einsum('td,sfd->stf', hidden_two, upward[ROUTED:], precision=PRECISE))
    shared_act = low(jax.nn.gelu(shared_pre, approximate=True))
    shared_out = low_back(jnp.einsum('stf,sfd->std', shared_act, downward[ROUTED:], precision=PRECISE))
    mixture = routed + lax.optimization_barrier(jnp.sum(shared_out, axis=0))
    return mid_state + (mixture.reshape(segments, SHORT, D) * modulation[:, 5:6]).reshape(-1, D)

def orthogonal(matrix):
    current = matrix / (jnp.sqrt(jnp.sum(matrix * matrix)) + 1e-07)
    for sweep_num in range(5):
        gram_mat = jnp.dot(current.T, current, precision=PRECISE)
        polynomial = NS_SECOND * gram_mat + NS_THIRD * jnp.dot(gram_mat, gram_mat, precision=PRECISE)
        current = NS_FIRST * current + jnp.dot(current, polynomial, precision=PRECISE)
    return current

def reference(tokens, conditions, routes, resolution, step_count, cotangent, w_square, w_out, w_router, w_up, w_down, b_ada, moment_square, moment_out, moment_router, moment_up, moment_down, moment_bias, ema_square, ema_out, ema_router, ema_up, ema_down, ema_bias):
    dev_count = resolution.shape[0]
    token_blocks = tokens.astype(jnp.float32).reshape(dev_count, -1, D)
    cond_blocks = conditions.astype(jnp.float32).reshape(dev_count, -1, D)
    route_blocks = routes.reshape(dev_count, -1, TOP)

    def forward(token_all, square, outward, router, upward, downward, bias_vec):
        rounded = (low(square), low(outward), low(router), low(upward), low(downward), low(bias_vec))

        def one_device(carry, pieces):
            return (carry, device_layer(pieces[0], pieces[1], pieces[2], pieces[3], rounded))
        _, results = lax.scan(jax.checkpoint(one_device), None, (token_all, cond_blocks, route_blocks, resolution))
        return results
    results, pullback = jax.vjp(forward, token_blocks, w_square, w_out, w_router, w_up, w_down, b_ada)
    grads = pullback(cotangent.astype(jnp.float32).reshape(dev_count, -1, D))
    output = results.reshape(-1, D).astype(jnp.bfloat16)
    grad_in = grads[0].reshape(-1, D)
    small_factor = RATE * 0.2 * D ** 0.5
    large_factor = RATE * 0.2 * FF ** 0.5
    state_square = MOMENTUM * moment_square + grads[1]
    master_square = w_square - small_factor * jax.vmap(orthogonal)(state_square)
    state_out = MOMENTUM * moment_out + grads[2]
    master_out = w_out - small_factor * orthogonal(state_out)
    state_router = MOMENTUM * moment_router + grads[3]
    master_router = w_router - small_factor * orthogonal(state_router)
    state_up = MOMENTUM * moment_up + grads[4]
    master_up = w_up - large_factor * jax.vmap(orthogonal)(state_up)
    state_down = MOMENTUM * moment_down + grads[5]
    master_down = w_down - large_factor * jax.vmap(orthogonal)(state_down)
    state_bias = MOMENTUM_VECTOR * moment_bias + grads[6]
    root_mean = jnp.sqrt(jnp.mean(state_bias * state_bias) + 1e-05)
    master_bias = b_ada - RATE_VECTOR * state_bias / root_mean
    step_value = step_count[0].astype(jnp.float32)
    decay = jnp.minimum(0.9999, (1.0 + step_value) / (10.0 + step_value))
    average_square = decay * ema_square + (1.0 - decay) * master_square
    average_out = decay * ema_out + (1.0 - decay) * master_out
    average_router = decay * ema_router + (1.0 - decay) * master_router
    average_up = decay * ema_up + (1.0 - decay) * master_up
    average_down = decay * ema_down + (1.0 - decay) * master_down
    average_bias = decay * ema_bias + (1.0 - decay) * master_bias
    return (output, grad_in, state_square, master_square, average_square, state_out, master_out, average_out, state_router, master_router, average_router, state_up, master_up, average_up, state_down, master_down, average_down, state_bias, master_bias, average_bias)
```

```python
from functools import partial

import jax
import jax.numpy as jnp
from jax import lax
from jax.experimental import pallas as pl
from jax.experimental.pallas import tpu as pltpu
from jax.sharding import PartitionSpec as P

WIDE, NARROW = "wide", "narrow"
D = 384
HEADS = 6
HEAD = 64
FF = 1536
TOP = 2
ROUTED = 8
SHORT = 256
LONG = 1024
CAP = 384


PRECISE = lax.Precision.HIGHEST
EPSILON = 1e-06
NS_FIRST = 3.4445
NS_SECOND = -4.775
NS_THIRD = 2.0315
MOMENTUM = 0.95
MOMENTUM_VECTOR = 0.5
RATE = 0.25
RATE_VECTOR = 0.05


def as_sent(array):

    def short(part):
        return part.astype(jnp.bfloat16) if part.dtype == jnp.float32 else part

    return jax.tree.map(short, array)


def modulate(seg_rows, shift_by, scale_by):
    center = seg_rows - jnp.mean(seg_rows, axis=-1, keepdims=True)
    normed = center * lax.rsqrt(jnp.mean(center * center, axis=-1, keepdims=True) + EPSILON)
    return normed * (1.0 + scale_by) + shift_by


def gelu_tanh(values):
    return jax.nn.gelu(values, approximate=True)


def gelu_grad(pre_act, upstream):
    _, pull_back = jax.vjp(gelu_tanh, pre_act)
    return pull_back(upstream)[0]


def slot_table(route_rows):
    flat_routes = route_rows.reshape(-1)
    hot_table = (flat_routes[:, None] == jnp.arange(ROUTED, dtype=jnp.int32)[None, :]).astype(
        jnp.int32
    )
    earlier = jnp.cumsum(hot_table, axis=0, dtype=jnp.int32) - hot_table
    place_in = jnp.sum(earlier * hot_table, axis=1, dtype=jnp.int32)
    slot_ids = flat_routes * CAP + place_in
    sources = jnp.arange(slot_ids.shape[0], dtype=jnp.int32) // TOP
    slot_owner = jnp.zeros((ROUTED * CAP,), jnp.int32).at[slot_ids].set(sources)
    return (slot_ids, slot_owner)


def attend(projected, length):
    image_count = projected.shape[1] // length
    split_parts = projected.reshape(3, image_count, length, HEADS, HEAD)
    scores = jnp.einsum(
        "bqhe,bkhe->bhqk", split_parts[0], split_parts[1], preferred_element_type=jnp.float32
    ) * HEAD ** (-0.5)
    highest = jnp.max(scores, axis=-1, keepdims=True)
    expo = jnp.exp(scores - highest)
    totals = jnp.sum(expo, axis=-1, keepdims=True)
    weights_low = (expo / totals).astype(jnp.bfloat16)
    mixed_heads = jnp.einsum(
        "bhqk,bkhe->bqhe", weights_low, split_parts[2], preferred_element_type=jnp.float32
    )
    log_total = (highest + jnp.log(totals))[..., 0]
    return (
        mixed_heads.reshape(-1, D).astype(jnp.bfloat16),
        jnp.transpose(log_total, (0, 2, 1)).reshape(-1, HEADS),
    )


def attend_back(projected, log_total, d_attended, length):
    image_count = projected.shape[1] // length
    split_parts = projected.reshape(3, image_count, length, HEADS, HEAD)
    scale_qk = HEAD ** (-0.5)
    scores = (
        jnp.einsum(
            "bqhe,bkhe->bhqk", split_parts[0], split_parts[1], preferred_element_type=jnp.float32
        )
        * scale_qk
    )
    log_four = jnp.transpose(log_total.reshape(image_count, length, HEADS), (0, 2, 1))[..., None]
    probs = jnp.exp(scores - log_four)
    weights_low = probs.astype(jnp.bfloat16)
    d_heads = d_attended.reshape(image_count, length, HEADS, HEAD)
    d_weights = jnp.einsum(
        "bqhe,bkhe->bhqk", d_heads, split_parts[2], preferred_element_type=jnp.float32
    )
    d_values = jnp.einsum(
        "bhqk,bqhe->bkhe", weights_low, d_heads, preferred_element_type=jnp.float32
    )
    d_scores = (probs * (d_weights - jnp.sum(d_weights * probs, axis=-1, keepdims=True))).astype(
        jnp.bfloat16
    )
    d_queries = (
        jnp.einsum("bhqk,bkhe->bqhe", d_scores, split_parts[1], preferred_element_type=jnp.float32)
        * scale_qk
    )
    d_keys = (
        jnp.einsum("bhqk,bqhe->bkhe", d_scores, split_parts[0], preferred_element_type=jnp.float32)
        * scale_qk
    )
    return jnp.stack([d_queries, d_keys, d_values]).reshape(3, -1, D).astype(jnp.bfloat16)


def on_device(
    tokens,
    conditions,
    routes,
    resolution,
    step_count,
    cotangent,
    w_square,
    w_out,
    w_router,
    w_up,
    w_down,
    b_ada,
    moment_square,
    moment_out,
    moment_router,
    moment_up,
    moment_down,
    moment_bias,
    ema_square,
    ema_out,
    ema_router,
    ema_up,
    ema_down,
    ema_bias,
):
    bf_type = jnp.bfloat16
    fl_type = jnp.float32
    row_pieces = (
        lax.all_gather(w_square.astype(bf_type), NARROW, axis=1, tiled=True),
        lax.all_gather(w_out.astype(bf_type), NARROW, axis=0, tiled=True),
        lax.all_gather(w_router.astype(bf_type), NARROW, axis=0, tiled=True),
        lax.all_gather(w_up.astype(bf_type), NARROW, axis=1, tiled=True),
        lax.all_gather(w_down.astype(bf_type), NARROW, axis=1, tiled=True),
        lax.all_gather(b_ada.astype(bf_type), NARROW, axis=0, tiled=True),
    )
    whole_low = (
        lax.all_gather(row_pieces[0], WIDE, axis=2, tiled=True),
        lax.all_gather(row_pieces[1], WIDE, axis=1, tiled=True),
        lax.all_gather(row_pieces[2], WIDE, axis=1, tiled=True),
        lax.all_gather(row_pieces[3], WIDE, axis=2, tiled=True),
        lax.all_gather(row_pieces[4], WIDE, axis=2, tiled=True),
        lax.all_gather(row_pieces[5], WIDE, axis=0, tiled=True),
    )
    square_low, out_low, router_low, up_low, down_low, bias_low = whole_low
    res_group = resolution[0]
    token_f = tokens.astype(fl_type)
    segments = tokens.shape[0] // SHORT
    seg_ratio = LONG // SHORT
    first_seg = jnp.arange(segments, dtype=jnp.int32) // seg_ratio * seg_ratio
    chosen = jnp.where(res_group == 1, conditions[first_seg], conditions)
    cond_low = jax.nn.silu(chosen.astype(fl_type)).astype(bf_type)
    modulation = jnp.einsum(
        "sd,jde->sje", cond_low, square_low[3:], preferred_element_type=fl_type
    ) + bias_low.astype(fl_type).reshape(6, D)
    seg_rows = token_f.reshape(segments, SHORT, D)
    first_mod, first_back = jax.vjp(modulate, seg_rows, modulation[:, 0:1], modulation[:, 1:2])
    hidden_one = first_mod.reshape(-1, D).astype(bf_type)
    projected = jnp.einsum(
        "td,jde->jte", hidden_one, square_low[:3], preferred_element_type=fl_type
    ).astype(bf_type)
    attended, log_total = lax.cond(
        res_group == 1, partial(attend, length=LONG), partial(attend, length=SHORT), projected
    )
    attn_out = jnp.dot(attended, out_low, preferred_element_type=fl_type)
    mid_state = token_f + (attn_out.reshape(segments, SHORT, D) * modulation[:, 2:3]).reshape(-1, D)
    second_mod, second_back = jax.vjp(
        modulate, mid_state.reshape(segments, SHORT, D), modulation[:, 3:4], modulation[:, 4:5]
    )
    hidden_two = second_mod.reshape(-1, D).astype(bf_type)
    logits = jnp.einsum("td,rd->tr", hidden_two, router_low, preferred_element_type=fl_type)
    gate_probs = jax.nn.softmax(jnp.take_along_axis(logits, routes, axis=1), axis=1)
    slot_ids, slot_owner = slot_table(routes)
    inputs = hidden_two[slot_owner].reshape(ROUTED, CAP, D)
    pre_act = jnp.einsum("ecd,efd->ecf", inputs, up_low[:ROUTED], preferred_element_type=fl_type)
    act_low = gelu_tanh(pre_act).astype(bf_type)
    produced = jnp.einsum(
        "ecf,efd->ecd", act_low, down_low[:ROUTED], preferred_element_type=fl_type
    ).reshape(-1, D)
    chosen_out = produced[slot_ids].reshape(-1, TOP, D)
    routed = jnp.sum(chosen_out * gate_probs[:, :, None], axis=1)
    shared_pre = jnp.einsum(
        "td,sfd->stf", hidden_two, up_low[ROUTED:], preferred_element_type=fl_type
    )
    shared_act = gelu_tanh(shared_pre).astype(bf_type)
    shared_out = jnp.einsum(
        "stf,sfd->std", shared_act, down_low[ROUTED:], preferred_element_type=fl_type
    )
    mixture = routed + jnp.sum(shared_out, axis=0)
    output = (
        mid_state + (mixture.reshape(segments, SHORT, D) * modulation[:, 5:6]).reshape(-1, D)
    ).astype(bf_type)
    again_rows = (
        lax.all_gather(w_square.astype(bf_type), NARROW, axis=1, tiled=True),
        lax.all_gather(w_out.astype(bf_type), NARROW, axis=0, tiled=True),
        lax.all_gather(w_router.astype(bf_type), NARROW, axis=0, tiled=True),
        lax.all_gather(w_up.astype(bf_type), NARROW, axis=1, tiled=True),
        lax.all_gather(w_down.astype(bf_type), NARROW, axis=1, tiled=True),
    )
    again_whole = (
        lax.all_gather(again_rows[0], WIDE, axis=2, tiled=True),
        lax.all_gather(again_rows[1], WIDE, axis=1, tiled=True),
        lax.all_gather(again_rows[2], WIDE, axis=1, tiled=True),
        lax.all_gather(again_rows[3], WIDE, axis=2, tiled=True),
        lax.all_gather(again_rows[4], WIDE, axis=2, tiled=True),
    )
    square_low, out_low, router_low, up_low, down_low = again_whole
    grad_out = cotangent.astype(fl_type)
    grad_seg = grad_out.reshape(segments, SHORT, D)
    d_gate_two = jnp.sum(grad_seg * mixture.reshape(segments, SHORT, D), axis=1)
    d_mixture = (grad_seg * modulation[:, 5:6]).reshape(-1, D)
    d_shared = d_mixture.astype(bf_type)
    d_shared_act = jnp.einsum(
        "td,sfd->stf", d_shared, down_low[ROUTED:], preferred_element_type=fl_type
    )
    d_shared_pre = gelu_grad(shared_pre, d_shared_act).astype(bf_type)
    g_shared_down = jnp.einsum("stf,td->sfd", shared_act, d_shared, preferred_element_type=fl_type)
    g_shared_up = jnp.einsum(
        "stf,td->sfd", d_shared_pre, hidden_two, preferred_element_type=fl_type
    )
    d_hidden = jnp.einsum(
        "stf,sfd->td", d_shared_pre, up_low[ROUTED:], preferred_element_type=fl_type
    )
    d_gates = jnp.sum(d_mixture[:, None, :] * chosen_out, axis=2)
    gate_slot = jnp.zeros((ROUTED * CAP,), fl_type).at[slot_ids].set(gate_probs.reshape(-1))
    d_produced = (
        (gate_slot[:, None] * d_mixture[slot_owner]).astype(bf_type).reshape(ROUTED, CAP, D)
    )
    d_act = jnp.einsum(
        "ecd,efd->ecf", d_produced, down_low[:ROUTED], preferred_element_type=fl_type
    )
    d_pre = gelu_grad(pre_act, d_act).astype(bf_type)
    g_routed_down = jnp.einsum("ecf,ecd->efd", act_low, d_produced, preferred_element_type=fl_type)
    g_routed_up = jnp.einsum("ecf,ecd->efd", d_pre, inputs, preferred_element_type=fl_type)
    d_inputs = jnp.einsum(
        "ecf,efd->ecd", d_pre, up_low[:ROUTED], preferred_element_type=fl_type
    ).reshape(-1, D)
    d_hidden = d_hidden + jnp.sum(d_inputs[slot_ids].reshape(-1, TOP, D), axis=1)
    d_picked = gate_probs * (d_gates - jnp.sum(gate_probs * d_gates, axis=1, keepdims=True))
    route_hot = (routes[:, :, None] == jnp.arange(ROUTED, dtype=jnp.int32)[None, None, :]).astype(
        fl_type
    )
    d_logits = jnp.sum(route_hot * d_picked[:, :, None], axis=1).astype(bf_type)
    g_router = jnp.einsum("tr,td->rd", d_logits, hidden_two, preferred_element_type=fl_type)
    d_hidden = d_hidden + jnp.einsum(
        "tr,rd->td", d_logits, router_low, preferred_element_type=fl_type
    )
    d_mid_norm, d_shift_two, d_scale_two = second_back(d_hidden.reshape(segments, SHORT, D))
    d_mid = grad_out + d_mid_norm.reshape(-1, D)
    d_gate_one = jnp.sum(
        d_mid.reshape(segments, SHORT, D) * attn_out.reshape(segments, SHORT, D), axis=1
    )
    d_attn = (d_mid.reshape(segments, SHORT, D) * modulation[:, 2:3]).reshape(-1, D).astype(bf_type)
    g_out = jnp.einsum("td,te->de", attended, d_attn, preferred_element_type=fl_type)
    d_attended = jnp.einsum("te,de->td", d_attn, out_low, preferred_element_type=fl_type).astype(
        bf_type
    )
    d_projected = lax.cond(
        res_group == 1,
        partial(attend_back, length=LONG),
        partial(attend_back, length=SHORT),
        projected,
        log_total,
        d_attended,
    )
    g_qkv = jnp.einsum("td,jte->jde", hidden_one, d_projected, preferred_element_type=fl_type)
    d_hidden_one = jnp.einsum(
        "jte,jde->td", d_projected, square_low[:3], preferred_element_type=fl_type
    )
    d_rows, d_shift_one, d_scale_one = first_back(d_hidden_one.reshape(segments, SHORT, D))
    grad_in = d_mid + d_rows.reshape(-1, D)
    d_modulation = jnp.stack(
        [
            d_shift_one[:, 0],
            d_scale_one[:, 0],
            d_gate_one,
            d_shift_two[:, 0],
            d_scale_two[:, 0],
            d_gate_two,
        ],
        axis=1,
    )
    g_ada = jnp.einsum("sd,sje->jde", cond_low.astype(fl_type), d_modulation, precision=PRECISE)
    g_bias = jnp.sum(d_modulation, axis=0).reshape(-1)
    g_square = jnp.concatenate([g_qkv, g_ada], axis=0)
    g_up = jnp.concatenate([g_routed_up, g_shared_up], axis=0)
    g_down = jnp.concatenate([g_routed_down, g_shared_down], axis=0)
    by_columns = (
        lax.psum_scatter(g_square, WIDE, scatter_dimension=2, tiled=True),
        lax.psum_scatter(g_out, WIDE, scatter_dimension=1, tiled=True),
        lax.psum_scatter(g_router, WIDE, scatter_dimension=1, tiled=True),
        lax.psum_scatter(g_up, WIDE, scatter_dimension=2, tiled=True),
        lax.psum_scatter(g_down, WIDE, scatter_dimension=2, tiled=True),
        lax.psum_scatter(g_bias, WIDE, scatter_dimension=0, tiled=True),
    )
    summed = (
        lax.psum_scatter(by_columns[0], NARROW, scatter_dimension=1, tiled=True),
        lax.psum_scatter(by_columns[1], NARROW, scatter_dimension=0, tiled=True),
        lax.psum_scatter(by_columns[2], NARROW, scatter_dimension=0, tiled=True),
        lax.psum_scatter(by_columns[3], NARROW, scatter_dimension=1, tiled=True),
        lax.psum_scatter(by_columns[4], NARROW, scatter_dimension=1, tiled=True),
        lax.psum_scatter(by_columns[5], NARROW, scatter_dimension=0, tiled=True),
    )
    state_square = MOMENTUM * moment_square + summed[0]
    state_out = MOMENTUM * moment_out + summed[1]
    state_router = MOMENTUM * moment_router + summed[2]
    state_up = MOMENTUM * moment_up + summed[3]
    state_down = MOMENTUM * moment_down + summed[4]
    local_rows = w_up.shape[1]

    def padded(block):
        return jnp.pad(block, ((0, 0), (0, local_rows - block.shape[1]), (0, 0)))

    stacked = jnp.concatenate(
        [
            padded(state_square),
            padded(state_out[None]),
            padded(state_router[None]),
            state_up,
            state_down,
        ],
        axis=0,
    )
    wide_count = lax.axis_size(WIDE)
    matrices = stacked.shape[0]
    per_owner = -(-matrices // wide_count)
    stacked = jnp.pad(stacked, ((0, per_owner * wide_count - matrices), (0, 0), (0, 0)))
    current = lax.all_to_all(stacked, WIDE, split_axis=0, concat_axis=2, tiled=True)
    for sweep_num in range(5):
        gram_mat = lax.psum(
            jnp.einsum("mrc,mrd->mcd", current, current, precision=PRECISE).astype(jnp.bfloat16),
            NARROW,
        ).astype(jnp.float32)
        if sweep_num == 0:
            factor = 1.0 / (jnp.sqrt(jnp.trace(gram_mat, axis1=1, axis2=2)) + 1e-07)
            current = current * factor[:, None, None]
            gram_mat = gram_mat * (factor * factor)[:, None, None]
        polynomial = NS_SECOND * gram_mat + NS_THIRD * jnp.einsum(
            "mcd,mde->mce", gram_mat, gram_mat, precision=PRECISE
        )
        current = NS_FIRST * current + jnp.einsum(
            "mrc,mcd->mrd", current, polynomial, precision=PRECISE
        )
    spread_back = lax.all_to_all(
        as_sent(current), WIDE, split_axis=2, concat_axis=0, tiled=True
    ).astype(current.dtype)[:matrices]
    expert_total = w_up.shape[0]
    small_factor = RATE * 0.2 * D**0.5
    large_factor = RATE * 0.2 * FF**0.5
    master_square = w_square - small_factor * spread_back[0:9, : w_square.shape[1]]
    master_out = w_out - small_factor * spread_back[9, : w_out.shape[0]]
    master_router = w_router - small_factor * spread_back[10, : w_router.shape[0]]
    master_up = w_up - large_factor * spread_back[11 : 11 + expert_total]
    master_down = w_down - large_factor * spread_back[11 + expert_total : 11 + 2 * expert_total]
    state_bias = MOMENTUM_VECTOR * moment_bias + summed[5]
    square_total = lax.psum(jnp.sum(state_bias * state_bias), (WIDE, NARROW))
    root_mean = jnp.sqrt(square_total / (6 * D) + 1e-05)
    master_bias = b_ada - RATE_VECTOR * state_bias / root_mean
    step_value = step_count[0].astype(fl_type)
    decay = jnp.minimum(0.9999, (1.0 + step_value) / (10.0 + step_value))
    average_square = decay * ema_square + (1.0 - decay) * master_square
    average_out = decay * ema_out + (1.0 - decay) * master_out
    average_router = decay * ema_router + (1.0 - decay) * master_router
    average_up = decay * ema_up + (1.0 - decay) * master_up
    average_down = decay * ema_down + (1.0 - decay) * master_down
    average_bias = decay * ema_bias + (1.0 - decay) * master_bias
    return (
        output,
        grad_in,
        state_square,
        master_square,
        average_square,
        state_out,
        master_out,
        average_out,
        state_router,
        master_router,
        average_router,
        state_up,
        master_up,
        average_up,
        state_down,
        master_down,
        average_down,
        state_bias,
        master_bias,
        average_bias,
    )


bf = jnp.bfloat16
f32 = jnp.float32
TOK = 1024
NN=(((1,),(0,)),((),())); NT=(((1,),(1,)),((),())); TN=(((0,),(0,)),((),()))
def dot(a,b,dims=NN): return lax.dot_general(a,b,dims,preferred_element_type=f32)

def gelu_pair(v):
    sq=v*v
    th=jnp.tanh(v*(0.7978845608028654+0.035677408136300125*sq))
    half=0.5*th+0.5
    act=v*half
    slope=half+act*(1.0-half)*(1.5957691216057308+0.21406444881780075*sq)
    return act,slope

def moe_kernel(ids, t0,t1,t2,t3,m0,m1,m2,m3,ga,gb, p0,p1,p2,p3,dg_out,g_send,g_keep,g_b1,g_b2,g_sh,
               tok,meta,up,dn,ups,dns,gup,gdn,gups,gdns,acc,part,dgs,gst,tsem,wsem,osem,gsem, *, RB, FC):
    n=ids[0]; z=ids[1]; x=ids[2]
    tin=(t0,t1,t2,t3); mins=(m0,m1,m2,m3)
    tcop=[pltpu.make_async_copy(tin[i],tok.at[i],tsem.at[i,0]) for i in range(4)]
    mcop=[pltpu.make_async_copy(mins[i],meta.at[i],tsem.at[i,1]) for i in range(4)]
    tcop[0].start(); mcop[0].start()
    wc=[]
    for src,xx in ((ga,x),(gb,1-x)):
        for d in range(4):
            row=pl.multiple_of((2*lax.rem(z-d+4,4)+xx)*48,16)
            for m in range(4):
                tgt=(ups,dns)[m%2]
                wc.append(pltpu.make_async_copy(src.at[d,4,m],tgt.at[pl.ds(row,48),pl.ds((m//2)*384,384)],wsem.at[0]))
                for k in range(4):
                    tgt=(up,dn)[m%2]
                    wc.append(pltpu.make_async_copy(src.at[d,k,m],tgt.at[m//2,pl.ds(row,48),pl.ds(k*384,384)],wsem.at[1]))
    for c in wc: c.start()
    for i in range(1,4): tcop[i].start(); mcop[i].start()
    gup[...]=jnp.zeros_like(gup); gdn[...]=jnp.zeros_like(gdn); gups[...]=jnp.zeros_like(gups); gdns[...]=jnp.zeros_like(gdns)
    for c in wc: c.wait()

    def per_src(s,_):
        pltpu.make_async_copy(t0,tok.at[s],tsem.at[s,0]).wait()
        pltpu.make_async_copy(m0,meta.at[s],tsem.at[s,1]).wait()
        def shared(r,_):
            rows=pl.ds(pl.multiple_of(r*RB,RB),RB)
            xs=tok[s,rows,:D]; ds=tok[s,rows,D:]
            out=jnp.zeros((RB,D),f32); dx=jnp.zeros((RB,D),f32)
            for f in range(0,768,FC):
                fs=slice(f,f+FC)
                pre=dot(xs,ups[:,fs]); da=dot(ds,dns[:,fs])
                act,slope=gelu_pair(pre)
                ab=act.astype(bf); pb=(slope*da).astype(bf)
                out=out+dot(ab,dns[:,fs],NT); dx=dx+dot(pb,ups[:,fs],NT)
                gups[:,fs]+=dot(xs,pb,TN); gdns[:,fs]+=dot(ds,ab,TN)
            acc[rows,:D]=out; acc[rows,D:]=dx
            return 0
        lax.fori_loop(0,TOK//RB,shared,0)
        def routed(e,_):
            ex=2*n+e
            pos=meta[s,pl.ds(ex,1),:]; gat=meta[s,pl.ds(8+ex,1),:]
            slot=lax.broadcasted_iota(jnp.int32,(CAP,TOK),0).astype(f32)
            hit=slot==pos
            hot=hit.astype(f32).astype(bf)
            gsl=jnp.sum(jnp.where(hit,gat,0.0),axis=1,keepdims=True)
            xd=dot(hot,tok[s])
            xs=xd[:,:D].astype(bf); dmx=xd[:,D:]
            ds=(dmx*gsl).astype(bf)
            out=jnp.zeros((CAP,D),f32); dx=jnp.zeros((CAP,D),f32)
            for f in range(0,FF,FC):
                fs=slice(f,f+FC)
                pre=dot(xs,up[e,:,fs]); da=dot(ds,dn[e,:,fs])
                act,slope=gelu_pair(pre)
                ab=act.astype(bf); pb=(slope*da).astype(bf)
                out=out+dot(ab,dn[e,:,fs],NT); dx=dx+dot(pb,up[e,:,fs],NT)
                gup[e,:,fs]+=dot(xs,pb,TN); gdn[e,:,fs]+=dot(ds,ab,TN)
            dgate=jnp.sum(out*dmx,axis=1,keepdims=True)
            dgs[s,pl.ds(e,1),:]=jnp.sum(jnp.where(hit,dgate,0.0),axis=0,keepdims=True)
            both=jnp.concatenate([(out*gsl).astype(bf),dx.astype(bf)],axis=1)
            acc[...]+=dot(hot,both,TN)
            return 0
        lax.fori_loop(0,2,routed,0)
        part[s]=acc[...].astype(bf)
        for i,dst in enumerate((p0,p1,p2,p3)):
            @pl.when(s==i)
            def _():
                pltpu.make_async_copy(part.at[i],dst,osem.at[i]).start()
        return 0
    lax.fori_loop(0,4,per_src,0)
    outs=[pltpu.make_async_copy(part.at[i],dst,osem.at[i]) for i,dst in enumerate((p0,p1,p2,p3))]
    cd=pltpu.make_async_copy(dgs,dg_out,osem.at[4]); cd.start(); outs.append(cd)
    def to(slot,dst): return pltpu.make_async_copy(gst.at[slot],dst,gsem.at[slot])
    for e in range(2):
        for m,src in ((0,gup),(1,gdn)):
            gst[2*e+m]=src[e].astype(bf)
    for sh in range(2):
        for m,src in ((0,gups),(1,gdns)):
            gst[4,:,pl.ds((2*sh+m)*384,384)]=src[:,sh*384:(sh+1)*384].astype(bf)
    @pl.when(x==0)
    def _():
        to(0,g_keep).start(); to(3,g_send).start()
    @pl.when(x!=0)
    def _():
        to(0,g_send).start(); to(3,g_keep).start()
    to(1,g_b1).start(); to(2,g_b2).start(); to(4,g_sh).start()
    for slot,dst in ((0,g_keep),(3,g_send),(1,g_b1),(2,g_b2),(4,g_sh)): to(slot,dst).wait()
    for c in outs: c.wait()

def moe(ids,toks,metas,ga,gb,RB=512,FC=512):
    anyspec=pl.BlockSpec(memory_space=pl.ANY)
    return pl.pallas_call(
        partial(moe_kernel,RB=RB,FC=FC),
        out_shape=[jax.ShapeDtypeStruct((TOK,2*D),bf)]*4+[jax.ShapeDtypeStruct((4,8,TOK),f32)]+[jax.ShapeDtypeStruct((D,FF),bf)]*5,
        in_specs=[pl.BlockSpec(memory_space=pltpu.SMEM)]+[anyspec]*10,
        out_specs=[anyspec]*10,
        scratch_shapes=[pltpu.VMEM((4,TOK,2*D),bf),pltpu.VMEM((4,16,TOK),f32),
            pltpu.VMEM((2,D,FF),bf),pltpu.VMEM((2,D,FF),bf),pltpu.VMEM((D,768),bf),pltpu.VMEM((D,768),bf),
            pltpu.VMEM((2,D,FF),f32),pltpu.VMEM((2,D,FF),f32),pltpu.VMEM((D,768),f32),pltpu.VMEM((D,768),f32),
            pltpu.VMEM((TOK,2*D),f32),pltpu.VMEM((4,TOK,2*D),bf),pltpu.VMEM((4,8,TOK),f32),pltpu.VMEM((5,D,FF),bf),
            pltpu.SemaphoreType.DMA((4,2)),pltpu.SemaphoreType.DMA((2,)),pltpu.SemaphoreType.DMA((5,)),pltpu.SemaphoreType.DMA((5,))],
        compiler_params=pltpu.CompilerParams(vmem_limit_bytes=63*1024*1024),
        name="moe",
    )(ids,*toks,*metas,ga,gb)


def head_only(block, head):
    lane = lax.broadcasted_iota(jnp.int32, block.shape, 1)
    return jnp.where((lane >= 64) == (head == 1), block, jnp.zeros_like(block))


def attend_kernel(res, q_ref, k_ref, v_ref, o_ref, lse_ref, vt_ref):
    qb = pl.program_id(1)

    @pl.when(qb == 0)
    def _():
        vt_ref[...] = v_ref[...].T

    def work(rows):
        q = q_ref[...] * 0.125
        outs = []
        for head in range(2):
            scores = dot(k_ref[rows, :], head_only(q, head), NT)
            top = jnp.max(scores, axis=0, keepdims=True)
            expo = jnp.exp(scores - top)
            total = jnp.sum(expo, axis=0, keepdims=True)
            weights = (expo * (1.0 / total)).astype(bf)
            outs.append(dot(vt_ref[head * 64 : head * 64 + 64, rows], weights))
            lse_ref[0, head : head + 1, :] = top + jnp.log(total)
        o_ref[...] = jnp.concatenate(outs, axis=0).T.astype(bf)

    @pl.when(res[0] == 1)
    def _():
        work(pl.ds(0, TOK))

    @pl.when(res[0] != 1)
    def _():
        work(pl.ds(pl.multiple_of(qb * 256, 256), 256))


def attend_fast(resolution, projected):
    return pl.pallas_call(
        attend_kernel,
        grid_spec=pltpu.PrefetchScalarGridSpec(
            num_scalar_prefetch=1,
            grid=(3, 4),
            in_specs=[
                pl.BlockSpec((256, 128), lambda h, i, r: (i, h)),
                pl.BlockSpec((TOK, 128), lambda h, i, r: (0, 3 + h)),
                pl.BlockSpec((TOK, 128), lambda h, i, r: (0, 6 + h)),
            ],
            out_specs=[
                pl.BlockSpec((256, 128), lambda h, i, r: (i, h)),
                pl.BlockSpec((1, 8, 256), lambda h, i, r: (h, 0, i)),
            ],
            scratch_shapes=[pltpu.VMEM((128, TOK), bf)],
        ),
        out_shape=(
            jax.ShapeDtypeStruct((TOK, D), bf),
            jax.ShapeDtypeStruct((3, 8, TOK), f32),
        ),
        compiler_params=pltpu.CompilerParams(vmem_limit_bytes=48 * 1024 * 1024),
        name="attend_fast",
    )(resolution, projected, projected, projected)


def attend_back_kernel(
    res, q_ref, k_ref, v_ref, do_ref, lse_ref, dq_ref, dk_ref, dv_ref, kt_ref, dk_acc, dv_acc
):
    qb = pl.program_id(1)

    @pl.when(qb == 0)
    def _():
        kt_ref[...] = k_ref[...].T

    def work(rows, whole):
        q = q_ref[...] * 0.125
        grads = []
        dk = dv = None
        for head in range(2):
            qh = head_only(q, head)
            doh = head_only(do_ref[...], head)
            scores = dot(k_ref[rows, :], qh, NT)
            probs = jnp.exp(scores - lse_ref[0, head : head + 1, :])
            d_weights = dot(v_ref[rows, :], doh, NT)
            delta = jnp.sum(d_weights * probs, axis=0, keepdims=True)
            d_scores = (probs * (d_weights - delta)).astype(bf)
            dv_one = dot(probs.astype(bf), doh)
            dk_one = dot(d_scores, qh)
            dv = dv_one if dv is None else dv + dv_one
            dk = dk_one if dk is None else dk + dk_one
            grads.append(dot(kt_ref[head * 64 : head * 64 + 64, rows], d_scores))
        dq_ref[...] = (jnp.concatenate(grads, axis=0).T * 0.125).astype(bf)
        if not whole:
            dk_ref[rows, :] = dk.astype(bf)
            dv_ref[rows, :] = dv.astype(bf)
            return

        @pl.when(qb == 0)
        def _():
            dk_acc[...] = dk
            dv_acc[...] = dv

        @pl.when(qb != 0)
        def _():
            dk_acc[...] += dk
            dv_acc[...] += dv

        @pl.when(qb == 3)
        def _():
            dk_ref[...] = dk_acc[...].astype(bf)
            dv_ref[...] = dv_acc[...].astype(bf)

    @pl.when(res[0] == 1)
    def _():
        work(pl.ds(0, TOK), True)

    @pl.when(res[0] != 1)
    def _():
        work(pl.ds(pl.multiple_of(qb * 256, 256), 256), False)


def attend_back_fast(resolution, projected, lse, d_attended):
    return pl.pallas_call(
        attend_back_kernel,
        grid_spec=pltpu.PrefetchScalarGridSpec(
            num_scalar_prefetch=1,
            grid=(3, 4),
            in_specs=[
                pl.BlockSpec((256, 128), lambda h, i, r: (i, h)),
                pl.BlockSpec((TOK, 128), lambda h, i, r: (0, 3 + h)),
                pl.BlockSpec((TOK, 128), lambda h, i, r: (0, 6 + h)),
                pl.BlockSpec((256, 128), lambda h, i, r: (i, h)),
                pl.BlockSpec((1, 8, 256), lambda h, i, r: (h, 0, i)),
            ],
            out_specs=[
                pl.BlockSpec((256, 128), lambda h, i, r: (i, h)),
                pl.BlockSpec((TOK, 128), lambda h, i, r: (0, h)),
                pl.BlockSpec((TOK, 128), lambda h, i, r: (0, h)),
            ],
            scratch_shapes=[
                pltpu.VMEM((128, TOK), bf),
                pltpu.VMEM((TOK, 128), f32),
                pltpu.VMEM((TOK, 128), f32),
            ],
        ),
        out_shape=[jax.ShapeDtypeStruct((TOK, D), bf)] * 3,
        compiler_params=pltpu.CompilerParams(vmem_limit_bytes=48 * 1024 * 1024),
        name="attend_back_fast",
    )(resolution, projected, projected, projected, d_attended, lse)


def halves(value):
    high = value.astype(bf)
    return high, (value - high.astype(f32)).astype(bf)


def dot_three(a, b, dims=NN):
    return dot(a[0], b[0], dims) + dot(a[0], b[1], dims) + dot(a[1], b[0], dims)


def up_owner(e):
    return (24 if e % 2 else 0) + e // 2 if e < 8 else 20 + 2 * (e - 8)


def down_owner(e):
    return (4 if e % 2 else 16) + e // 2 if e < 8 else 21 + 2 * (e - 8)


def square_owner(j):
    return 8 + j if j < 3 else (9 + j if j < 7 else 21 + j)


OUT_OWNER, ROUTER_OWNER = 11, 30


def pack_kernel(square, out, router, up, down, packed):
    for e in range(10):
        packed[up_owner(e)] = up[e]
        packed[down_owner(e)] = down[e]
    rest = jnp.zeros((48, D - 96), f32)
    for j in range(9):
        packed[square_owner(j)] = jnp.concatenate([square[j], rest], axis=1)
    packed[OUT_OWNER] = jnp.concatenate([out[...], rest], axis=1)
    packed[ROUTER_OWNER] = router[...]
    packed[31] = jnp.zeros((48, D), f32)


def pack_owned(square, out, router, up, down):
    vmem = pl.BlockSpec(memory_space=pltpu.VMEM)
    return pl.pallas_call(
        pack_kernel,
        out_shape=jax.ShapeDtypeStruct((32, 48, D), f32),
        in_specs=[vmem] * 5,
        out_specs=vmem,
        name="pack_owned",
    )(square, out, router, up, down)


def owned_grad_kernel(ids, *refs):
    held, received = refs[:3], refs[3:12]
    dense, small, full_out, cut_out, buf, sems = refs[12:]
    n, z, x = ids[0], ids[1], ids[2]
    is_small = (z == 1) | ((z == 3) & (x == 1))

    def fetch(group):
        sources = [held[group]] + list(received[3 * group : 3 * group + 3])
        return [
            pltpu.make_async_copy(source, buf.at[i], sems.at[i])
            for i, source in enumerate(sources)
        ]

    for group, owner in enumerate((0, 2, 3)):

        @pl.when((z == owner) & jnp.logical_not(is_small))
        def _():
            for copy in fetch(group):
                copy.start()
            for copy in fetch(group):
                copy.wait()

    @pl.when(jnp.logical_not(is_small))
    def _():
        for k in range(4):
            lanes = slice(k * D, k * D + D)
            total = buf[0, :, lanes].astype(f32) + buf[1, :, lanes].astype(f32)
            full_out[k] = total + buf[2, :, lanes].astype(f32) + buf[3, :, lanes].astype(f32)

    @pl.when(is_small)
    def _():
        rows = small[...].reshape(32, 8, 512)

        def place(matrix, width):
            rest = jnp.zeros((D, D - width), f32)
            for m in range(4):
                part = matrix[:, m * width : m * width + width]
                full_out[m ^ n] = jnp.concatenate([part, rest], axis=1)

        @pl.when(z == 1)
        def _():
            @pl.when(x == 0)
            def _():
                place(dense[...], 96)

        @pl.when(jnp.logical_not((z == 1) & (x == 0)))
        def _():
            is_router = (z == 3) & (n == 2)

            @pl.when(is_router)
            def _():
                summed = jnp.sum(rows[:, :, :D], axis=0)
                place(jnp.concatenate([summed, jnp.zeros((120, D), f32)], axis=0).T[:, :8], 2)

            @pl.when(jnp.logical_not(is_router))
            def _():
                first = (lax.broadcasted_iota(jnp.int32, (256, D), 0) % 8) < 4
                both = small[:, :D]
                mods = jnp.where(first, both, 0.0)
                conds = pltpu.roll(both, 252, 0)
                conds = jnp.where(first, conds, 0.0)
                place(dot_three(halves(mods), halves(conds), TN), 96)

    for w in range(8):
        for m in range(4):
            cut_out[4 * w + m] = full_out[m ^ n, 48 * w : 48 * w + 48, :].astype(bf)


def owned_grad(ids, held, received, dense, small):
    anyspec, vmem = pl.BlockSpec(memory_space=pl.ANY), pl.BlockSpec(memory_space=pltpu.VMEM)
    return pl.pallas_call(
        owned_grad_kernel,
        out_shape=(
            jax.ShapeDtypeStruct((4, D, D), f32),
            jax.ShapeDtypeStruct((32, 48, D), bf),
        ),
        in_specs=[pl.BlockSpec(memory_space=pltpu.SMEM)] + [anyspec] * 12 + [vmem] * 2,
        out_specs=[vmem, vmem],
        scratch_shapes=[pltpu.VMEM((4, D, FF), bf), pltpu.SemaphoreType.DMA((4,))],
        compiler_params=pltpu.CompilerParams(vmem_limit_bytes=40 * 1024 * 1024),
        name="owned_grad",
    )(ids, *held, *received, dense, small)


def ortho_kernel(ids, grad, moment, extra, cut_out, cur, poly):
    n = ids[0]
    for k in range(4):
        cur[k] = grad[k]
    for w in range(8):
        rows = slice(48 * w, 48 * w + 48)
        for m in range(4):
            cur[m ^ n, rows, :] += MOMENTUM * moment[4 * w + m]
    total = jnp.zeros((1, D), f32)
    for k in range(4):
        total = total + jnp.sum(cur[k] * cur[k], axis=0, keepdims=True)
    factor = 1.0 / (jnp.sqrt(jnp.sum(total, axis=1, keepdims=True)) + 1e-07)
    for k in range(4):
        cur[k] = cur[k] * factor

    def sweep(_, carry):
        gram = jnp.zeros((D, D), f32)
        for k in range(4):
            part = halves(cur[k])
            gram = gram + dot_three(part, part, NT)
        split = halves(gram)
        poly[...] = NS_SECOND * gram + NS_THIRD * dot_three(split, split)
        split = halves(poly[...])
        for k in range(4):
            block = cur[k]
            cur[k] = NS_FIRST * block + dot_three(split, halves(block))
        return carry

    lax.fori_loop(0, 5, sweep, 0)
    for w in range(8):
        for m in range(4):
            cut_out[4 * w + m, :48] = cur[m ^ n, 48 * w : 48 * w + 48, :].astype(bf)
            cut_out[4 * w + m, 48:] = extra[...]


def ortho_owned(ids, grad, moment, extra):
    vmem = pl.BlockSpec(memory_space=pltpu.VMEM)
    return pl.pallas_call(
        ortho_kernel,
        out_shape=jax.ShapeDtypeStruct((32, 56, D), bf),
        in_specs=[pl.BlockSpec(memory_space=pltpu.SMEM), vmem, vmem, vmem],
        out_specs=vmem,
        scratch_shapes=[pltpu.VMEM((4, D, D), f32), pltpu.VMEM((D, D), f32)],
        compiler_params=pltpu.CompilerParams(vmem_limit_bytes=40 * 1024 * 1024),
        name="ortho_owned",
    )(ids, grad, moment, extra)


def update_kernel(decay_ref, grads, orthos, *refs):
    decay = decay_ref[0]
    weights, moments, emas = refs[0:5], refs[5:10], refs[10:15]
    states, masters, averages = refs[15:20], refs[20:25], refs[25:30]
    small_rate, large_rate = RATE * 0.2 * D**0.5, RATE * 0.2 * FF**0.5

    def step(which, at, grad, ortho, rate):
        states[which][at] = MOMENTUM * moments[which][at] + grad.astype(f32)
        master = weights[which][at] - rate * ortho.astype(f32)
        masters[which][at] = master
        averages[which][at] = decay * emas[which][at] + (1.0 - decay) * master

    for j in range(9):
        own = square_owner(j)
        step(0, j, grads[own, :, :96], orthos[own, :48, :96], small_rate)
    step(1, slice(None), grads[OUT_OWNER, :, :96], orthos[OUT_OWNER, :48, :96], small_rate)

    def router_rows(source):
        return source[ROUTER_OWNER, :48, :128].astype(f32).T[:2]

    step(2, slice(None), router_rows(grads), router_rows(orthos), small_rate)
    for e in range(10):
        step(3, e, grads[up_owner(e)], orthos[up_owner(e), :48], large_rate)
        step(4, e, grads[down_owner(e)], orthos[down_owner(e), :48], large_rate)


def update(decay, grads, orthos, weights, moments, emas):
    vmem = pl.BlockSpec(memory_space=pltpu.VMEM)
    shapes = [jax.ShapeDtypeStruct(weight.shape, f32) for weight in weights]
    return pl.pallas_call(
        update_kernel,
        out_shape=shapes * 3,
        in_specs=[pl.BlockSpec(memory_space=pltpu.SMEM)] + [vmem] * 17,
        out_specs=[vmem] * 15,
        compiler_params=pltpu.CompilerParams(vmem_limit_bytes=48 * 1024 * 1024),
        name="update",
    )(decay, grads, orthos, *weights, *moments, *emas)


AXES = (WIDE, NARROW)


def route_pairs(move):
    pairs = []
    for index in range(32):
        w, n = divmod(index, 4)
        target = move(w // 2, w % 2, n // 2, n % 2)
        if target is not None:
            z, x, y, c = target
            pairs.append((index, (z * 2 + x) * 4 + y * 2 + c))
    return pairs


def send(array, move):
    return lax.ppermute(array, AXES, route_pairs(move))


def to_core(z, x, y, c):
    return (z, x, y, 1 - c)


def to_y(z, x, y, c):
    return (z, x, 1 - y, c)


def to_diag(z, x, y, c):
    return (z, x, 1 - y, 1 - c)


def to_x(z, x, y, c):
    return (z, 1 - x, y, c)


def to_z(step):
    return lambda z, x, y, c: ((z + step) % 4, x, y, c)


NARROW_MOVES = (None, to_core, to_y, to_diag)


def pick(array, index, axis=0):
    return lax.dynamic_index_in_dim(array, index, axis, keepdims=False)


def in_order(mine, other, flag):
    return jnp.where(flag == 0, mine, other), jnp.where(flag == 0, other, mine)


def xor_blocks(array, axis, y, c):
    parts = [lax.index_in_dim(array, i, axis, keepdims=True) for i in range(4)]
    parts = [jnp.where(c == 0, parts[i], parts[i ^ 1]) for i in range(4)]
    parts = [jnp.where(y == 0, parts[i], parts[i ^ 2]) for i in range(4)]
    return jnp.concatenate(parts, axis=axis)


def gather_rows(rows, z, x, c):
    pieces = [send(rows, to_z(step)) for step in (3, 2, 1)] + [rows]
    pieces = [pieces[2], pieces[1], pieces[0]]
    recv = {step: send_piece for step, send_piece in zip((1, 2, 3), pieces)}
    ring = jnp.stack([recv[3], recv[2], recv[1], rows])
    doubled = jnp.concatenate([ring, ring])
    by_z = lax.dynamic_slice_in_dim(doubled, (3 - z) % 4, 4, 0)
    by_zx = jnp.stack(in_order(by_z, send(by_z, to_x), x), axis=1)
    return jnp.stack(in_order(by_zx, send(by_zx, to_core), c), axis=2)


def lanes_to(block, width):
    return jnp.pad(block, [(0, 0)] * (block.ndim - 1) + [(0, width - block.shape[-1])])


def turned(array):
    return jnp.swapaxes(array, -1, -2)


def fast_device(
    tokens,
    conditions,
    routes,
    resolution,
    step_count,
    cotangent,
    w_square,
    w_out,
    w_router,
    w_up,
    w_down,
    b_ada,
    moment_square,
    moment_out,
    moment_router,
    moment_up,
    moment_down,
    moment_bias,
    ema_square,
    ema_out,
    ema_router,
    ema_up,
    ema_down,
    ema_bias,
):
    wide = lax.axis_index(WIDE)
    narrow = lax.axis_index(NARROW)
    z, x = wide // 2, wide % 2
    y, c = narrow // 2, narrow % 2

    square_t = turned(w_square).astype(bf)
    out_t = turned(w_out).astype(bf)[None]
    misc = jnp.concatenate(
        [
            lanes_to(b_ada.astype(bf)[None], 96),
            lanes_to(w_router.astype(bf), 96),
            jnp.zeros((5, 96), bf),
        ]
    )
    flat = jnp.concatenate(
        [
            square_t[:5].reshape(-1, 96),
            misc,
            square_t[5:].reshape(-1, 96),
            out_t.reshape(-1, 96),
        ]
    )
    by_y = jnp.stack(in_order(flat, send(flat, to_y), y))
    by_yc = in_order(by_y, send(by_y, to_core), c)
    rows = jnp.concatenate([by_yc[0][0], by_yc[1][0], by_yc[0][1], by_yc[1][1]], axis=1)

    def my_half(block):
        return pick(block.reshape(5, 2, 24, D), c, 1).reshape(120, D)

    first_rows = jnp.concatenate([my_half(rows[:240]), rows[240:248]])
    first_all = gather_rows(first_rows, z, x, c)
    second_all = gather_rows(my_half(rows[248:]), z, x, c)

    def assemble(gathered):
        parts = gathered[..., :120, :].reshape(8, 2, 5, 24, D)
        return jnp.transpose(parts, (2, 0, 1, 3, 4)).reshape(5, D, D)

    first_maps = assemble(first_all)
    second_maps = assemble(second_all)
    misc_all = first_all[:, :, 0, 120:, :].reshape(8, 8, 4, 96)
    bias_low = misc_all[:, 0, :, :72].reshape(-1)
    router_low = jnp.transpose(misc_all[:, 1:3, :, :48], (2, 1, 0, 3)).reshape(ROUTED, D)

    up_t = turned(w_up).astype(bf)
    down_t = turned(w_down).astype(bf)
    routed_t = jnp.stack([up_t[:8], down_t[:8]], axis=1).reshape(4, 4, 48, D)
    shared_t = jnp.stack([up_t[8:], down_t[8:]], axis=1).reshape(4, 48, D)
    mine = [pick(routed_t, narrow)]
    mine += [send(pick(routed_t, narrow ^ k), NARROW_MOVES[k]) for k in (1, 2, 3)]
    blocks = jnp.stack(mine + [shared_t])
    near = jnp.stack([blocks] + [send(blocks, to_z(step)) for step in (1, 2, 3)])
    far = send(near, to_x)

    moment_parts = (
        turned(moment_square),
        turned(moment_out),
        moment_router,
        turned(moment_up),
        turned(moment_down),
    )
    router_block = lanes_to(turned(moment_router), D)
    moments = pack_owned(*moment_parts[:2], router_block, *moment_parts[3:])

    res_group = resolution[0]
    token_f = tokens.astype(f32)
    segments = tokens.shape[0] // SHORT
    seg_ratio = LONG // SHORT
    first_seg = jnp.arange(segments, dtype=jnp.int32) // seg_ratio * seg_ratio
    chosen = jnp.where(res_group == 1, conditions[first_seg], conditions)
    cond_low = jax.nn.silu(chosen.astype(f32)).astype(bf)
    bias_rows = bias_low.astype(f32).reshape(6, D)

    def modulation_of(maps, bias):
        return dot(cond_low, maps.reshape(-1, D), NT).reshape(segments, -1, D) + bias

    first_two = modulation_of(first_maps[3:], bias_rows[:2])
    last_four = modulation_of(second_maps[:4], bias_rows[2:])
    out_map = second_maps[4]
    seg_rows = token_f.reshape(segments, SHORT, D)
    first_mod, first_back = jax.vjp(modulate, seg_rows, first_two[:, 0:1], first_two[:, 1:2])
    hidden_one = first_mod.reshape(-1, D).astype(bf)
    query_maps = first_maps[:3].reshape(3 * D, D)
    projected = dot(hidden_one, query_maps, NT).astype(bf)
    attended, log_total = attend_fast(resolution, projected)
    attn_out = dot(attended, out_map, NT)
    gate_one, gate_two = last_four[:, 0:1], last_four[:, 3:4]
    mid_state = token_f + (attn_out.reshape(segments, SHORT, D) * gate_one).reshape(-1, D)
    second_mod, second_back = jax.vjp(
        modulate, mid_state.reshape(segments, SHORT, D), last_four[:, 1:2], last_four[:, 2:3]
    )
    hidden_two = second_mod.reshape(-1, D).astype(bf)

    logits = dot(router_low, hidden_two, NT)
    experts = jnp.arange(ROUTED, dtype=jnp.int32)[:, None]
    named = (routes[:, 0][None] == experts) | (routes[:, 1][None] == experts)
    index = jnp.arange(TOK, dtype=jnp.int32)
    earlier = (index[:, None] < index[None, :]).astype(bf)
    place = jnp.dot(named.astype(bf), earlier, preferred_element_type=f32)
    masked = jnp.where(named, logits, -jnp.inf)
    expo = jnp.where(named, jnp.exp(logits - jnp.max(masked, axis=0, keepdims=True)), 0.0)
    gates = expo / jnp.sum(expo, axis=0, keepdims=True)
    meta = jnp.concatenate([jnp.where(named, place, -1.0), gates])

    grad_out = cotangent.astype(f32)
    grad_seg = grad_out.reshape(segments, SHORT, D)
    d_mixture = (grad_seg * gate_two).reshape(-1, D).astype(bf)
    pack = jnp.concatenate([hidden_two, d_mixture], axis=1)
    pack_core, meta_core = send(pack, to_core), send(meta, to_core)
    pack_y, meta_y = send(pack, to_y), send(meta, to_y)
    pack_diag, meta_diag = send(pack_y, to_core), send(meta_y, to_core)
    place_ids = jnp.stack([narrow, z, x]).astype(jnp.int32)
    pack, moments = lax.optimization_barrier((pack, moments))
    moments = lax.all_to_all(moments, AXES, 0, 0, tiled=True)
    part_own, part_core, part_y, part_diag, d_gate_rows, *grads = moe(
        place_ids,
        (pack, pack_core, pack_y, pack_diag),
        (meta, meta_core, meta_y, meta_diag),
        near,
        far,
    )
    over = (part_y.astype(f32) + send(part_diag, to_core).astype(f32)).astype(bf)
    own = part_own.astype(f32) + send(part_core, to_core).astype(f32)
    total = own + send(over, to_y).astype(f32)
    mixture, d_hidden = total[:, :D], total[:, D:]
    d_rows = [d_gate_rows[0, :2]]
    d_rows += [send(d_gate_rows[k, :2], NARROW_MOVES[k]) for k in (1, 2, 3)]
    d_gates = xor_blocks(jnp.stack(d_rows), 0, y, c).reshape(ROUTED, TOK)

    g_send, g_keep, g_second, g_third, g_shared = grads
    g_shared, over = lax.optimization_barrier((g_shared, over))

    def shared_part(k):
        return lax.dynamic_slice_in_dim(g_shared, (narrow ^ k) * D, D, 1)

    shared_grad = jnp.concatenate(
        [shared_part(0)] + [send(shared_part(k), NARROW_MOVES[k]) for k in (1, 2, 3)], axis=1
    )

    def back_x(z_, x_, y_, c_):
        return (z_, 0, y_, c_) if x_ == 1 else None

    def added(kept, other):
        return (kept.astype(f32) + other.astype(f32)).astype(bf)

    held_one = added(g_keep, send(g_send, to_x))
    held_three = added(g_third, send(g_third, back_x))
    held_two = added(
        jnp.where(x == 0, g_second, shared_grad),
        send(jnp.where(x == 0, shared_grad, g_second), to_x),
    )
    received = []
    for held, owner in ((held_one, 0), (held_two, 2), (held_three, 3)):
        for step in (1, 2, 3):

            def move(z_, x_, y_, c_, owner=owner, step=step):
                if (z_ + step) % 4 != owner or (owner == 3 and x_ == 1):
                    return None
                return (owner, x_, y_, c_)

            received.append(send(held, move))

    output = (
        mid_state + (mixture.reshape(segments, SHORT, D) * gate_two).reshape(-1, D)
    ).astype(bf)
    d_gate_two = jnp.sum(grad_seg * mixture.reshape(segments, SHORT, D), axis=1)
    d_logits = gates * (d_gates - jnp.sum(gates * d_gates, axis=0, keepdims=True))
    d_logits = d_logits.astype(bf)
    g_router = jnp.dot(d_logits, hidden_two, preferred_element_type=f32)
    d_hidden = d_hidden + dot(d_logits, router_low, TN)
    d_mid_norm, d_shift_two, d_scale_two = second_back(d_hidden.reshape(segments, SHORT, D))
    d_mid = grad_out + d_mid_norm.reshape(-1, D)
    d_mid_seg = d_mid.reshape(segments, SHORT, D)
    d_gate_one = jnp.sum(d_mid_seg * attn_out.reshape(segments, SHORT, D), axis=1)
    d_attn = (d_mid_seg * gate_one).reshape(-1, D).astype(bf)
    g_out = dot(d_attn, attended, TN)
    d_attended = jnp.dot(d_attn, out_map, preferred_element_type=f32).astype(bf)
    d_heads = attend_back_fast(resolution, projected, log_total, d_attended)
    g_qkv = jnp.stack([dot(d_head, hidden_one, TN) for d_head in d_heads])
    d_hidden_one = sum(
        jnp.dot(d_head, first_maps[j], preferred_element_type=f32)
        for j, d_head in enumerate(d_heads)
    )
    d_rows_one, d_shift_one, d_scale_one = first_back(d_hidden_one.reshape(segments, SHORT, D))
    grad_in = d_mid + d_rows_one.reshape(-1, D)
    d_modulation = [
        d_shift_one[:, 0],
        d_scale_one[:, 0],
        d_gate_one,
        d_shift_two[:, 0],
        d_scale_two[:, 0],
        d_gate_two,
    ]

    dense = jnp.concatenate([g_qkv, g_out[None]]).reshape(2, 2, D, D)
    dense = pick(dense, c, 1) + send(pick(dense, 1 - c, 1).astype(bf), to_core).astype(f32)
    dense = pick(dense, y) + send(pick(dense, 1 - y).astype(bf), to_y).astype(f32)
    dense = dense + send(dense.astype(bf), back_x).astype(f32)
    dense_low = dense.astype(bf)
    for step in (1, 2, 3):

        def to_second(z_, x_, y_, c_, step=step):
            return (1, x_, y_, c_) if (z_ + step) % 4 == 1 and x_ == 0 else None

        dense = dense + send(dense_low, to_second).astype(f32)

    cond_rows = cond_low.astype(f32)
    ada_rows = [jnp.concatenate([d_mod, cond_rows]) for d_mod in d_modulation]
    payload = jnp.zeros((8, 4, 8, D), f32)
    payload = payload.at[3].set(jnp.stack(ada_rows[:4]))
    payload = payload.at[7, :3].set(jnp.stack(ada_rows[4:] + [g_router]))
    bias_part = jnp.concatenate([jnp.sum(d_mod, axis=0) for d_mod in d_modulation])
    bias_part = jnp.pad(bias_part.reshape(8, 4, 1, 72), ((0, 0), (0, 0), (0, 7), (0, 56)))
    small = jnp.concatenate([payload, bias_part], axis=3).reshape(32, 8, 512)
    small = lax.all_to_all(small, AXES, 0, 0, tiled=True)
    g_bias = jnp.sum(small[:, 0, D : D + 72], axis=0)
    grad_full, grad_cut = owned_grad(
        place_ids, (held_one, held_two, held_three), received, dense, small.reshape(256, 512)
    )
    grad_parts = lax.all_to_all(grad_cut, AXES, 0, 0, tiled=True)

    state_bias = MOMENTUM_VECTOR * moment_bias + g_bias
    part_sum = jnp.sum(state_bias * state_bias)
    sum_high = part_sum.astype(bf)
    sum_low = (part_sum - sum_high.astype(f32)).astype(bf)

    extra = jnp.pad(jnp.stack([sum_high, sum_low])[None], ((0, 7), (0, D - 2)))
    ortho_cut = ortho_owned(place_ids, grad_full, moments, extra)
    ortho_parts = lax.all_to_all(ortho_cut, AXES, 0, 0, tiled=True)
    square_total = jnp.sum(ortho_parts[:, 48, :2].astype(f32))

    step_value = step_count[0].astype(f32)
    decay = jnp.minimum(0.9999, (1.0 + step_value) / (10.0 + step_value))
    weights = (turned(w_square), turned(w_out), w_router, turned(w_up), turned(w_down))
    emas = (turned(ema_square), turned(ema_out), ema_router, turned(ema_up), turned(ema_down))
    updated = update(decay[None], grad_parts, ortho_parts, weights, moment_parts, emas)
    results = []
    for which in range(5):
        results += [
            array if which == 2 else turned(array) for array in updated[which::5]
        ]
    root_mean = jnp.sqrt(square_total / (6 * D) + 1e-05)
    master_bias = b_ada - RATE_VECTOR * state_bias / root_mean
    average_bias = decay * ema_bias + (1.0 - decay) * master_bias
    return (output, grad_in, *results, state_bias, master_bias, average_bias)


def solution(mesh):
    placed = (
        P((WIDE, NARROW), None),
        P((WIDE, NARROW), None),
        P((WIDE, NARROW), None),
        P((WIDE, NARROW)),
        P(),
        P((WIDE, NARROW), None),
        P(None, NARROW, WIDE),
        P(NARROW, WIDE),
        P(NARROW, WIDE),
        P(None, NARROW, WIDE),
        P(None, NARROW, WIDE),
        P((WIDE, NARROW)),
        P(None, NARROW, WIDE),
        P(NARROW, WIDE),
        P(NARROW, WIDE),
        P(None, NARROW, WIDE),
        P(None, NARROW, WIDE),
        P((WIDE, NARROW)),
        P(None, NARROW, WIDE),
        P(NARROW, WIDE),
        P(NARROW, WIDE),
        P(None, NARROW, WIDE),
        P(None, NARROW, WIDE),
        P((WIDE, NARROW)),
    )
    device_body = fast_device if dict(mesh.shape) == {WIDE: 8, NARROW: 4} else on_device
    return jax.shard_map(
        device_body,
        mesh=mesh,
        in_specs=placed,
        out_specs=(
            P((WIDE, NARROW), None),
            P((WIDE, NARROW), None),
            P(None, NARROW, WIDE),
            P(None, NARROW, WIDE),
            P(None, NARROW, WIDE),
            P(NARROW, WIDE),
            P(NARROW, WIDE),
            P(NARROW, WIDE),
            P(NARROW, WIDE),
            P(NARROW, WIDE),
            P(NARROW, WIDE),
            P(None, NARROW, WIDE),
            P(None, NARROW, WIDE),
            P(None, NARROW, WIDE),
            P(None, NARROW, WIDE),
            P(None, NARROW, WIDE),
            P(None, NARROW, WIDE),
            P((WIDE, NARROW)),
            P((WIDE, NARROW)),
            P((WIDE, NARROW)),
        ),
        check_vma=False,
    )
```

```python
from functools import partial

import jax
import jax.numpy as jnp
from jax import lax
from jax.experimental import pallas as pl
from jax.experimental.pallas import tpu as pltpu
from jax.sharding import PartitionSpec as P

WIDE, NARROW = "wide", "narrow"
D = 384
HEADS = 6
HEAD = 64
FF = 1536
TOP = 2
ROUTED = 8
SHORT = 256
LONG = 1024
CAP = 384


PRECISE = lax.Precision.HIGHEST
EPSILON = 1e-06
NS_FIRST = 3.4445
NS_SECOND = -4.775
NS_THIRD = 2.0315
MOMENTUM = 0.95
MOMENTUM_VECTOR = 0.5
RATE = 0.25
RATE_VECTOR = 0.05


def as_sent(array):

    def short(part):
        return part.astype(jnp.bfloat16) if part.dtype == jnp.float32 else part

    return jax.tree.map(short, array)


def modulate(seg_rows, shift_by, scale_by):
    center = seg_rows - jnp.mean(seg_rows, axis=-1, keepdims=True)
    normed = center * lax.rsqrt(jnp.mean(center * center, axis=-1, keepdims=True) + EPSILON)
    return normed * (1.0 + scale_by) + shift_by


def gelu_tanh(values):
    return jax.nn.gelu(values, approximate=True)


def gelu_grad(pre_act, upstream):
    _, pull_back = jax.vjp(gelu_tanh, pre_act)
    return pull_back(upstream)[0]


def slot_table(route_rows):
    flat_routes = route_rows.reshape(-1)
    hot_table = (flat_routes[:, None] == jnp.arange(ROUTED, dtype=jnp.int32)[None, :]).astype(
        jnp.int32
    )
    earlier = jnp.cumsum(hot_table, axis=0, dtype=jnp.int32) - hot_table
    place_in = jnp.sum(earlier * hot_table, axis=1, dtype=jnp.int32)
    slot_ids = flat_routes * CAP + place_in
    sources = jnp.arange(slot_ids.shape[0], dtype=jnp.int32) // TOP
    slot_owner = jnp.zeros((ROUTED * CAP,), jnp.int32).at[slot_ids].set(sources)
    return (slot_ids, slot_owner)


def attend(projected, length):
    image_count = projected.shape[1] // length
    split_parts = projected.reshape(3, image_count, length, HEADS, HEAD)
    scores = jnp.einsum(
        "bqhe,bkhe->bhqk", split_parts[0], split_parts[1], preferred_element_type=jnp.float32
    ) * HEAD ** (-0.5)
    highest = jnp.max(scores, axis=-1, keepdims=True)
    expo = jnp.exp(scores - highest)
    totals = jnp.sum(expo, axis=-1, keepdims=True)
    weights_low = (expo / totals).astype(jnp.bfloat16)
    mixed_heads = jnp.einsum(
        "bhqk,bkhe->bqhe", weights_low, split_parts[2], preferred_element_type=jnp.float32
    )
    log_total = (highest + jnp.log(totals))[..., 0]
    return (
        mixed_heads.reshape(-1, D).astype(jnp.bfloat16),
        jnp.transpose(log_total, (0, 2, 1)).reshape(-1, HEADS),
    )


def attend_back(projected, log_total, d_attended, length):
    image_count = projected.shape[1] // length
    split_parts = projected.reshape(3, image_count, length, HEADS, HEAD)
    scale_qk = HEAD ** (-0.5)
    scores = (
        jnp.einsum(
            "bqhe,bkhe->bhqk", split_parts[0], split_parts[1], preferred_element_type=jnp.float32
        )
        * scale_qk
    )
    log_four = jnp.transpose(log_total.reshape(image_count, length, HEADS), (0, 2, 1))[..., None]
    probs = jnp.exp(scores - log_four)
    weights_low = probs.astype(jnp.bfloat16)
    d_heads = d_attended.reshape(image_count, length, HEADS, HEAD)
    d_weights = jnp.einsum(
        "bqhe,bkhe->bhqk", d_heads, split_parts[2], preferred_element_type=jnp.float32
    )
    d_values = jnp.einsum(
        "bhqk,bqhe->bkhe", weights_low, d_heads, preferred_element_type=jnp.float32
    )
    d_scores = (probs * (d_weights - jnp.sum(d_weights * probs, axis=-1, keepdims=True))).astype(
        jnp.bfloat16
    )
    d_queries = (
        jnp.einsum("bhqk,bkhe->bqhe", d_scores, split_parts[1], preferred_element_type=jnp.float32)
        * scale_qk
    )
    d_keys = (
        jnp.einsum("bhqk,bqhe->bkhe", d_scores, split_parts[0], preferred_element_type=jnp.float32)
        * scale_qk
    )
    return jnp.stack([d_queries, d_keys, d_values]).reshape(3, -1, D).astype(jnp.bfloat16)


def on_device(
    tokens,
    conditions,
    routes,
    resolution,
    step_count,
    cotangent,
    w_square,
    w_out,
    w_router,
    w_up,
    w_down,
    b_ada,
    moment_square,
    moment_out,
    moment_router,
    moment_up,
    moment_down,
    moment_bias,
    ema_square,
    ema_out,
    ema_router,
    ema_up,
    ema_down,
    ema_bias,
):
    bf_type = jnp.bfloat16
    fl_type = jnp.float32
    row_pieces = (
        lax.all_gather(w_square.astype(bf_type), NARROW, axis=1, tiled=True),
        lax.all_gather(w_out.astype(bf_type), NARROW, axis=0, tiled=True),
        lax.all_gather(w_router.astype(bf_type), NARROW, axis=0, tiled=True),
        lax.all_gather(w_up.astype(bf_type), NARROW, axis=1, tiled=True),
        lax.all_gather(w_down.astype(bf_type), NARROW, axis=1, tiled=True),
        lax.all_gather(b_ada.astype(bf_type), NARROW, axis=0, tiled=True),
    )
    whole_low = (
        lax.all_gather(row_pieces[0], WIDE, axis=2, tiled=True),
        lax.all_gather(row_pieces[1], WIDE, axis=1, tiled=True),
        lax.all_gather(row_pieces[2], WIDE, axis=1, tiled=True),
        lax.all_gather(row_pieces[3], WIDE, axis=2, tiled=True),
        lax.all_gather(row_pieces[4], WIDE, axis=2, tiled=True),
        lax.all_gather(row_pieces[5], WIDE, axis=0, tiled=True),
    )
    square_low, out_low, router_low, up_low, down_low, bias_low = whole_low
    res_group = resolution[0]
    token_f = tokens.astype(fl_type)
    segments = tokens.shape[0] // SHORT
    seg_ratio = LONG // SHORT
    first_seg = jnp.arange(segments, dtype=jnp.int32) // seg_ratio * seg_ratio
    chosen = jnp.where(res_group == 1, conditions[first_seg], conditions)
    cond_low = jax.nn.silu(chosen.astype(fl_type)).astype(bf_type)
    modulation = jnp.einsum(
        "sd,jde->sje", cond_low, square_low[3:], preferred_element_type=fl_type
    ) + bias_low.astype(fl_type).reshape(6, D)
    seg_rows = token_f.reshape(segments, SHORT, D)
    first_mod, first_back = jax.vjp(modulate, seg_rows, modulation[:, 0:1], modulation[:, 1:2])
    hidden_one = first_mod.reshape(-1, D).astype(bf_type)
    projected = jnp.einsum(
        "td,jde->jte", hidden_one, square_low[:3], preferred_element_type=fl_type
    ).astype(bf_type)
    attended, log_total = lax.cond(
        res_group == 1, partial(attend, length=LONG), partial(attend, length=SHORT), projected
    )
    attn_out = jnp.dot(attended, out_low, preferred_element_type=fl_type)
    mid_state = token_f + (attn_out.reshape(segments, SHORT, D) * modulation[:, 2:3]).reshape(-1, D)
    second_mod, second_back = jax.vjp(
        modulate, mid_state.reshape(segments, SHORT, D), modulation[:, 3:4], modulation[:, 4:5]
    )
    hidden_two = second_mod.reshape(-1, D).astype(bf_type)
    logits = jnp.einsum("td,rd->tr", hidden_two, router_low, preferred_element_type=fl_type)
    gate_probs = jax.nn.softmax(jnp.take_along_axis(logits, routes, axis=1), axis=1)
    slot_ids, slot_owner = slot_table(routes)
    inputs = hidden_two[slot_owner].reshape(ROUTED, CAP, D)
    pre_act = jnp.einsum("ecd,efd->ecf", inputs, up_low[:ROUTED], preferred_element_type=fl_type)
    act_low = gelu_tanh(pre_act).astype(bf_type)
    produced = jnp.einsum(
        "ecf,efd->ecd", act_low, down_low[:ROUTED], preferred_element_type=fl_type
    ).reshape(-1, D)
    chosen_out = produced[slot_ids].reshape(-1, TOP, D)
    routed = jnp.sum(chosen_out * gate_probs[:, :, None], axis=1)
    shared_pre = jnp.einsum(
        "td,sfd->stf", hidden_two, up_low[ROUTED:], preferred_element_type=fl_type
    )
    shared_act = gelu_tanh(shared_pre).astype(bf_type)
    shared_out = jnp.einsum(
        "stf,sfd->std", shared_act, down_low[ROUTED:], preferred_element_type=fl_type
    )
    mixture = routed + jnp.sum(shared_out, axis=0)
    output = (
        mid_state + (mixture.reshape(segments, SHORT, D) * modulation[:, 5:6]).reshape(-1, D)
    ).astype(bf_type)
    again_rows = (
        lax.all_gather(w_square.astype(bf_type), NARROW, axis=1, tiled=True),
        lax.all_gather(w_out.astype(bf_type), NARROW, axis=0, tiled=True),
        lax.all_gather(w_router.astype(bf_type), NARROW, axis=0, tiled=True),
        lax.all_gather(w_up.astype(bf_type), NARROW, axis=1, tiled=True),
        lax.all_gather(w_down.astype(bf_type), NARROW, axis=1, tiled=True),
    )
    again_whole = (
        lax.all_gather(again_rows[0], WIDE, axis=2, tiled=True),
        lax.all_gather(again_rows[1], WIDE, axis=1, tiled=True),
        lax.all_gather(again_rows[2], WIDE, axis=1, tiled=True),
        lax.all_gather(again_rows[3], WIDE, axis=2, tiled=True),
        lax.all_gather(again_rows[4], WIDE, axis=2, tiled=True),
    )
    square_low, out_low, router_low, up_low, down_low = again_whole
    grad_out = cotangent.astype(fl_type)
    grad_seg = grad_out.reshape(segments, SHORT, D)
    d_gate_two = jnp.sum(grad_seg * mixture.reshape(segments, SHORT, D), axis=1)
    d_mixture = (grad_seg * modulation[:, 5:6]).reshape(-1, D)
    d_shared = d_mixture.astype(bf_type)
    d_shared_act = jnp.einsum(
        "td,sfd->stf", d_shared, down_low[ROUTED:], preferred_element_type=fl_type
    )
    d_shared_pre = gelu_grad(shared_pre, d_shared_act).astype(bf_type)
    g_shared_down = jnp.einsum("stf,td->sfd", shared_act, d_shared, preferred_element_type=fl_type)
    g_shared_up = jnp.einsum(
        "stf,td->sfd", d_shared_pre, hidden_two, preferred_element_type=fl_type
    )
    d_hidden = jnp.einsum(
        "stf,sfd->td", d_shared_pre, up_low[ROUTED:], preferred_element_type=fl_type
    )
    d_gates = jnp.sum(d_mixture[:, None, :] * chosen_out, axis=2)
    gate_slot = jnp.zeros((ROUTED * CAP,), fl_type).at[slot_ids].set(gate_probs.reshape(-1))
    d_produced = (
        (gate_slot[:, None] * d_mixture[slot_owner]).astype(bf_type).reshape(ROUTED, CAP, D)
    )
    d_act = jnp.einsum(
        "ecd,efd->ecf", d_produced, down_low[:ROUTED], preferred_element_type=fl_type
    )
    d_pre = gelu_grad(pre_act, d_act).astype(bf_type)
    g_routed_down = jnp.einsum("ecf,ecd->efd", act_low, d_produced, preferred_element_type=fl_type)
    g_routed_up = jnp.einsum("ecf,ecd->efd", d_pre, inputs, preferred_element_type=fl_type)
    d_inputs = jnp.einsum(
        "ecf,efd->ecd", d_pre, up_low[:ROUTED], preferred_element_type=fl_type
    ).reshape(-1, D)
    d_hidden = d_hidden + jnp.sum(d_inputs[slot_ids].reshape(-1, TOP, D), axis=1)
    d_picked = gate_probs * (d_gates - jnp.sum(gate_probs * d_gates, axis=1, keepdims=True))
    route_hot = (routes[:, :, None] == jnp.arange(ROUTED, dtype=jnp.int32)[None, None, :]).astype(
        fl_type
    )
    d_logits = jnp.sum(route_hot * d_picked[:, :, None], axis=1).astype(bf_type)
    g_router = jnp.einsum("tr,td->rd", d_logits, hidden_two, preferred_element_type=fl_type)
    d_hidden = d_hidden + jnp.einsum(
        "tr,rd->td", d_logits, router_low, preferred_element_type=fl_type
    )
    d_mid_norm, d_shift_two, d_scale_two = second_back(d_hidden.reshape(segments, SHORT, D))
    d_mid = grad_out + d_mid_norm.reshape(-1, D)
    d_gate_one = jnp.sum(
        d_mid.reshape(segments, SHORT, D) * attn_out.reshape(segments, SHORT, D), axis=1
    )
    d_attn = (d_mid.reshape(segments, SHORT, D) * modulation[:, 2:3]).reshape(-1, D).astype(bf_type)
    g_out = jnp.einsum("td,te->de", attended, d_attn, preferred_element_type=fl_type)
    d_attended = jnp.einsum("te,de->td", d_attn, out_low, preferred_element_type=fl_type).astype(
        bf_type
    )
    d_projected = lax.cond(
        res_group == 1,
        partial(attend_back, length=LONG),
        partial(attend_back, length=SHORT),
        projected,
        log_total,
        d_attended,
    )
    g_qkv = jnp.einsum("td,jte->jde", hidden_one, d_projected, preferred_element_type=fl_type)
    d_hidden_one = jnp.einsum(
        "jte,jde->td", d_projected, square_low[:3], preferred_element_type=fl_type
    )
    d_rows, d_shift_one, d_scale_one = first_back(d_hidden_one.reshape(segments, SHORT, D))
    grad_in = d_mid + d_rows.reshape(-1, D)
    d_modulation = jnp.stack(
        [
            d_shift_one[:, 0],
            d_scale_one[:, 0],
            d_gate_one,
            d_shift_two[:, 0],
            d_scale_two[:, 0],
            d_gate_two,
        ],
        axis=1,
    )
    g_ada = jnp.einsum("sd,sje->jde", cond_low.astype(fl_type), d_modulation, precision=PRECISE)
    g_bias = jnp.sum(d_modulation, axis=0).reshape(-1)
    g_square = jnp.concatenate([g_qkv, g_ada], axis=0)
    g_up = jnp.concatenate([g_routed_up, g_shared_up], axis=0)
    g_down = jnp.concatenate([g_routed_down, g_shared_down], axis=0)
    by_columns = (
        lax.psum_scatter(g_square, WIDE, scatter_dimension=2, tiled=True),
        lax.psum_scatter(g_out, WIDE, scatter_dimension=1, tiled=True),
        lax.psum_scatter(g_router, WIDE, scatter_dimension=1, tiled=True),
        lax.psum_scatter(g_up, WIDE, scatter_dimension=2, tiled=True),
        lax.psum_scatter(g_down, WIDE, scatter_dimension=2, tiled=True),
        lax.psum_scatter(g_bias, WIDE, scatter_dimension=0, tiled=True),
    )
    summed = (
        lax.psum_scatter(by_columns[0], NARROW, scatter_dimension=1, tiled=True),
        lax.psum_scatter(by_columns[1], NARROW, scatter_dimension=0, tiled=True),
        lax.psum_scatter(by_columns[2], NARROW, scatter_dimension=0, tiled=True),
        lax.psum_scatter(by_columns[3], NARROW, scatter_dimension=1, tiled=True),
        lax.psum_scatter(by_columns[4], NARROW, scatter_dimension=1, tiled=True),
        lax.psum_scatter(by_columns[5], NARROW, scatter_dimension=0, tiled=True),
    )
    state_square = MOMENTUM * moment_square + summed[0]
    state_out = MOMENTUM * moment_out + summed[1]
    state_router = MOMENTUM * moment_router + summed[2]
    state_up = MOMENTUM * moment_up + summed[3]
    state_down = MOMENTUM * moment_down + summed[4]
    local_rows = w_up.shape[1]

    def padded(block):
        return jnp.pad(block, ((0, 0), (0, local_rows - block.shape[1]), (0, 0)))

    stacked = jnp.concatenate(
        [
            padded(state_square),
            padded(state_out[None]),
            padded(state_router[None]),
            state_up,
            state_down,
        ],
        axis=0,
    )
    wide_count = lax.axis_size(WIDE)
    matrices = stacked.shape[0]
    per_owner = -(-matrices // wide_count)
    stacked = jnp.pad(stacked, ((0, per_owner * wide_count - matrices), (0, 0), (0, 0)))
    current = lax.all_to_all(stacked, WIDE, split_axis=0, concat_axis=2, tiled=True)
    for sweep_num in range(5):
        gram_mat = lax.psum(
            jnp.einsum("mrc,mrd->mcd", current, current, precision=PRECISE).astype(jnp.bfloat16),
            NARROW,
        ).astype(jnp.float32)
        if sweep_num == 0:
            factor = 1.0 / (jnp.sqrt(jnp.trace(gram_mat, axis1=1, axis2=2)) + 1e-07)
            current = current * factor[:, None, None]
            gram_mat = gram_mat * (factor * factor)[:, None, None]
        polynomial = NS_SECOND * gram_mat + NS_THIRD * jnp.einsum(
            "mcd,mde->mce", gram_mat, gram_mat, precision=PRECISE
        )
        current = NS_FIRST * current + jnp.einsum(
            "mrc,mcd->mrd", current, polynomial, precision=PRECISE
        )
    spread_back = lax.all_to_all(
        as_sent(current), WIDE, split_axis=2, concat_axis=0, tiled=True
    ).astype(current.dtype)[:matrices]
    expert_total = w_up.shape[0]
    small_factor = RATE * 0.2 * D**0.5
    large_factor = RATE * 0.2 * FF**0.5
    master_square = w_square - small_factor * spread_back[0:9, : w_square.shape[1]]
    master_out = w_out - small_factor * spread_back[9, : w_out.shape[0]]
    master_router = w_router - small_factor * spread_back[10, : w_router.shape[0]]
    master_up = w_up - large_factor * spread_back[11 : 11 + expert_total]
    master_down = w_down - large_factor * spread_back[11 + expert_total : 11 + 2 * expert_total]
    state_bias = MOMENTUM_VECTOR * moment_bias + summed[5]
    square_total = lax.psum(jnp.sum(state_bias * state_bias), (WIDE, NARROW))
    root_mean = jnp.sqrt(square_total / (6 * D) + 1e-05)
    master_bias = b_ada - RATE_VECTOR * state_bias / root_mean
    step_value = step_count[0].astype(fl_type)
    decay = jnp.minimum(0.9999, (1.0 + step_value) / (10.0 + step_value))
    average_square = decay * ema_square + (1.0 - decay) * master_square
    average_out = decay * ema_out + (1.0 - decay) * master_out
    average_router = decay * ema_router + (1.0 - decay) * master_router
    average_up = decay * ema_up + (1.0 - decay) * master_up
    average_down = decay * ema_down + (1.0 - decay) * master_down
    average_bias = decay * ema_bias + (1.0 - decay) * master_bias
    return (
        output,
        grad_in,
        state_square,
        master_square,
        average_square,
        state_out,
        master_out,
        average_out,
        state_router,
        master_router,
        average_router,
        state_up,
        master_up,
        average_up,
        state_down,
        master_down,
        average_down,
        state_bias,
        master_bias,
        average_bias,
    )


bf = jnp.bfloat16
f32 = jnp.float32
TOK = 1024
ROWS = 512
UNITS = 512
NN = (((1,), (0,)), ((), ()))
NT = (((1,), (1,)), ((), ()))
TN = (((0,), (0,)), ((), ()))


def dot(a, b, dims=NN):
    return lax.dot_general(a, b, dims, preferred_element_type=f32)


def gelu_pair(pre):
    sq = pre * pre
    th = jnp.tanh(pre * (0.7978845608028654 + 0.035677408136300125 * sq))
    half = 0.5 * th + 0.5
    act = pre * half
    slope = half + act * (1.0 - half) * (1.5957691216057308 + 0.21406444881780075 * sq)
    return act, slope


def moe_kernel(last, ids, *refs):
    hidden, d_mix, metas = refs[0:2], refs[2:4], refs[4:6]
    gathered = refs[6]
    prior = refs[7:12] if last else ()
    refs = refs[7 + len(prior) :]
    part_out, d_gate_out, refs = refs[0:2], refs[2], refs[3:]
    grads = refs[: 6 if last else 5]
    refs = refs[len(grads) :]
    tok, meta, up, down, up_s, down_s, g_up, g_down, g_up_s, g_down_s = refs[:10]
    acc, part, d_gate, stage, tok_sem, w_sem, out_sem, g_sem = refs[10:]
    n, x = ids[0], ids[2]

    def token_copies(i):
        return [
            pltpu.make_async_copy(hidden[i], tok.at[i, :, pl.ds(0, D)], tok_sem.at[i, 0]),
            pltpu.make_async_copy(d_mix[i], tok.at[i, :, pl.ds(D, D)], tok_sem.at[i, 1]),
            pltpu.make_async_copy(metas[i], meta.at[i], tok_sem.at[i, 2]),
        ]

    for copy in token_copies(0):
        copy.start()
    loads = []
    for w in range(8):
        rows = pl.ds(48 * w, 48)
        for e in range(2):
            for m, whole, shared in ((0, up, up_s), (1, down, down_s)):
                slot = 2 * e + m
                loads.append((gathered.at[w, 4, slot], shared.at[rows, pl.ds(e * D, D)]))
                for k in range(4):
                    target = whole.at[e, rows, pl.ds(k * D, D)]
                    loads.append((gathered.at[w, k, slot], target))
    loads = [pltpu.make_async_copy(source, target, w_sem.at[0]) for source, target in loads]
    for copy in loads:
        copy.start()
    for copy in token_copies(1):
        copy.start()
    carried = [
        pltpu.make_async_copy(source, stage.at[i], g_sem.at[i]) for i, source in enumerate(prior)
    ]
    for copy in carried:
        copy.start()
    if last:
        for copy in carried:
            copy.wait()
        for e in range(2):
            g_up[e] = stage[2 * e].astype(f32)
            g_down[e] = stage[2 * e + 1].astype(f32)
            g_up_s[:, e * D : e * D + D] = stage[4, :, 2 * e * D : 2 * e * D + D].astype(f32)
            g_down_s[:, e * D : e * D + D] = stage[
                4, :, 2 * e * D + D : 2 * e * D + 2 * D
            ].astype(f32)
    else:
        for total in (g_up, g_down, g_up_s, g_down_s):
            total[...] = jnp.zeros_like(total)
    for copy in loads:
        copy.wait()
    for i in range(2):
        for copy in token_copies(i):
            copy.wait()

    def units(xs, ds, up_ref, down_ref, g_up_ref, g_down_ref, count):
        out = jnp.zeros(xs.shape, f32)
        dx = jnp.zeros(xs.shape, f32)
        for first in range(0, count, UNITS):
            lanes = slice(first, min(first + UNITS, count))
            act, slope = gelu_pair(dot(xs, up_ref[:, lanes]))
            act = act.astype(bf)
            d_pre = (slope * dot(ds, down_ref[:, lanes])).astype(bf)
            out = out + dot(act, down_ref[:, lanes], NT)
            dx = dx + dot(d_pre, up_ref[:, lanes], NT)
            g_up_ref[:, lanes] += dot(xs, d_pre, TN)
            g_down_ref[:, lanes] += dot(ds, act, TN)
        return out, dx

    def one_source(s, carry):
        def shared(r, carry):
            rows = pl.ds(pl.multiple_of(r * ROWS, ROWS), ROWS)
            out, dx = units(
                tok[s, rows, :D], tok[s, rows, D:], up_s, down_s, g_up_s, g_down_s, 2 * D
            )
            acc[rows, :D] = out
            acc[rows, D:] = dx
            return carry

        lax.fori_loop(0, TOK // ROWS, shared, 0)

        def routed(e, carry):
            place = meta[s, pl.ds(2 * n + e, 1), :]
            gate = meta[s, pl.ds(8 + 2 * n + e, 1), :]
            slot = lax.broadcasted_iota(jnp.int32, (CAP, TOK), 0).astype(f32)
            hit = slot == place
            hot = hit.astype(f32).astype(bf)
            gates = jnp.sum(jnp.where(hit, gate, 0.0), axis=1, keepdims=True)
            rows = dot(hot, tok[s])
            d_rows = rows[:, D:]
            out, dx = units(
                rows[:, :D].astype(bf),
                (d_rows * gates).astype(bf),
                up.at[e],
                down.at[e],
                g_up.at[e],
                g_down.at[e],
                FF,
            )
            d_slot = jnp.sum(out * d_rows, axis=1, keepdims=True)
            d_gate[s, pl.ds(e, 1), :] = jnp.sum(
                jnp.where(hit, d_slot, 0.0), axis=0, keepdims=True
            )
            both = jnp.concatenate([(out * gates).astype(bf), dx.astype(bf)], axis=1)
            acc[...] += dot(hot, both, TN)
            return carry

        lax.fori_loop(0, 2, routed, 0)
        part[s] = acc[...].astype(bf)
        for i in range(2):

            @pl.when(s == i)
            def _():
                pltpu.make_async_copy(part.at[i], part_out[i], out_sem.at[i]).start()

        return carry

    lax.fori_loop(0, 2, one_source, 0)
    gate_copy = pltpu.make_async_copy(d_gate, d_gate_out, out_sem.at[2])
    gate_copy.start()
    for e in range(2):
        stage[2 * e] = g_up[e].astype(bf)
        stage[2 * e + 1] = g_down[e].astype(bf)
        stage[4, :, 2 * e * D : 2 * e * D + D] = g_up_s[:, e * D : e * D + D].astype(bf)
        stage[4, :, 2 * e * D + D : 2 * e * D + 2 * D] = g_down_s[
            :, e * D : e * D + D
        ].astype(bf)

    def store(slot, target, sem):
        return pltpu.make_async_copy(slot, target, g_sem.at[sem])

    if last:
        g_send, g_keep, g_second, g_left, g_right, g_shared = grads

        @pl.when(x == 0)
        def _():
            store(stage.at[0], g_keep, 0).start()
            store(stage.at[3], g_send, 1).start()

        @pl.when(x != 0)
        def _():
            store(stage.at[3], g_keep, 0).start()
            store(stage.at[0], g_send, 1).start()

        rest = [
            store(stage.at[1], g_second, 2),
            store(stage.at[2, :, pl.ds(0, FF // 2)], g_left, 3),
            store(stage.at[2, :, pl.ds(FF // 2, FF // 2)], g_right, 5),
            store(stage.at[4], g_shared, 4),
        ]
        for copy in rest:
            copy.start()
        rest += [store(stage.at[0], g_keep, 0), store(stage.at[3], g_send, 1)]
    else:
        rest = [store(stage.at[i], grads[i], i) for i in range(5)]
        for copy in rest:
            copy.start()
    for copy in rest:
        copy.wait()
    for i in range(2):
        pltpu.make_async_copy(part.at[i], part_out[i], out_sem.at[i]).wait()
    gate_copy.wait()


def moe(ids, hidden, d_mix, metas, gathered, prior=()):
    last = len(prior) > 0
    anyspec = pl.BlockSpec(memory_space=pl.ANY)
    whole = jax.ShapeDtypeStruct((D, FF), bf)
    half = jax.ShapeDtypeStruct((D, FF // 2), bf)
    grads = [whole, whole, whole, half, half, whole] if last else [whole] * 5
    shapes = [jax.ShapeDtypeStruct((TOK, 2 * D), bf)] * 2
    shapes += [jax.ShapeDtypeStruct((2, 8, TOK), f32)] + grads
    return pl.pallas_call(
        partial(moe_kernel, last),
        out_shape=shapes,
        in_specs=[pl.BlockSpec(memory_space=pltpu.SMEM)] + [anyspec] * (7 + len(prior)),
        out_specs=[anyspec] * len(shapes),
        scratch_shapes=[
            pltpu.VMEM((2, TOK, 2 * D), bf),
            pltpu.VMEM((2, 16, TOK), f32),
            pltpu.VMEM((2, D, FF), bf),
            pltpu.VMEM((2, D, FF), bf),
            pltpu.VMEM((D, 2 * D), bf),
            pltpu.VMEM((D, 2 * D), bf),
            pltpu.VMEM((2, D, FF), f32),
            pltpu.VMEM((2, D, FF), f32),
            pltpu.VMEM((D, 2 * D), f32),
            pltpu.VMEM((D, 2 * D), f32),
            pltpu.VMEM((TOK, 2 * D), f32),
            pltpu.VMEM((2, TOK, 2 * D), bf),
            pltpu.VMEM((2, 8, TOK), f32),
            pltpu.VMEM((5, D, FF), bf),
            pltpu.SemaphoreType.DMA((2, 3)),
            pltpu.SemaphoreType.DMA((1,)),
            pltpu.SemaphoreType.DMA((3,)),
            pltpu.SemaphoreType.DMA((6,)),
        ],
        compiler_params=pltpu.CompilerParams(vmem_limit_bytes=56 * 1024 * 1024),
        name="moe_last" if last else "moe_first",
    )(ids, *hidden, *d_mix, *metas, gathered, *prior)


def head_only(block, head):
    lane = lax.broadcasted_iota(jnp.int32, block.shape, 1)
    return jnp.where((lane >= 64) == (head == 1), block, jnp.zeros_like(block))


def attend_kernel(res, q_ref, k_ref, v_ref, o_ref, lse_ref, vt_ref):
    qb = pl.program_id(1)

    @pl.when(qb == 0)
    def _():
        vt_ref[...] = v_ref[...].T

    def work(rows):
        q = q_ref[...] * 0.125
        outs = []
        for head in range(2):
            scores = dot(k_ref[rows, :], head_only(q, head), NT)
            top = jnp.max(scores, axis=0, keepdims=True)
            expo = jnp.exp(scores - top)
            total = jnp.sum(expo, axis=0, keepdims=True)
            weights = (expo * (1.0 / total)).astype(bf)
            outs.append(dot(vt_ref[head * 64 : head * 64 + 64, rows], weights))
            lse_ref[0, head : head + 1, :] = top + jnp.log(total)
        o_ref[...] = jnp.concatenate(outs, axis=0).T.astype(bf)

    @pl.when(res[0] == 1)
    def _():
        work(pl.ds(0, TOK))

    @pl.when(res[0] != 1)
    def _():
        work(pl.ds(pl.multiple_of(qb * 256, 256), 256))


def attend_fast(resolution, projected):
    return pl.pallas_call(
        attend_kernel,
        grid_spec=pltpu.PrefetchScalarGridSpec(
            num_scalar_prefetch=1,
            grid=(3, 4),
            in_specs=[
                pl.BlockSpec((256, 128), lambda h, i, r: (i, h)),
                pl.BlockSpec((TOK, 128), lambda h, i, r: (0, 3 + h)),
                pl.BlockSpec((TOK, 128), lambda h, i, r: (0, 6 + h)),
            ],
            out_specs=[
                pl.BlockSpec((256, 128), lambda h, i, r: (i, h)),
                pl.BlockSpec((1, 8, 256), lambda h, i, r: (h, 0, i)),
            ],
            scratch_shapes=[pltpu.VMEM((128, TOK), bf)],
        ),
        out_shape=(
            jax.ShapeDtypeStruct((TOK, D), bf),
            jax.ShapeDtypeStruct((3, 8, TOK), f32),
        ),
        compiler_params=pltpu.CompilerParams(vmem_limit_bytes=48 * 1024 * 1024),
        name="attend_fast",
    )(resolution, projected, projected, projected)


def attend_back_kernel(
    res, q_ref, k_ref, v_ref, do_ref, lse_ref, dq_ref, dk_ref, dv_ref, kt_ref, dk_acc, dv_acc
):
    qb = pl.program_id(1)

    @pl.when(qb == 0)
    def _():
        kt_ref[...] = k_ref[...].T

    def work(rows, whole):
        q = q_ref[...] * 0.125
        grads = []
        dk = dv = None
        for head in range(2):
            qh = head_only(q, head)
            doh = head_only(do_ref[...], head)
            scores = dot(k_ref[rows, :], qh, NT)
            probs = jnp.exp(scores - lse_ref[0, head : head + 1, :])
            d_weights = dot(v_ref[rows, :], doh, NT)
            delta = jnp.sum(d_weights * probs, axis=0, keepdims=True)
            d_scores = (probs * (d_weights - delta)).astype(bf)
            dv_one = dot(probs.astype(bf), doh)
            dk_one = dot(d_scores, qh)
            dv = dv_one if dv is None else dv + dv_one
            dk = dk_one if dk is None else dk + dk_one
            grads.append(dot(kt_ref[head * 64 : head * 64 + 64, rows], d_scores))
        dq_ref[...] = (jnp.concatenate(grads, axis=0).T * 0.125).astype(bf)
        if not whole:
            dk_ref[rows, :] = dk.astype(bf)
            dv_ref[rows, :] = dv.astype(bf)
            return

        @pl.when(qb == 0)
        def _():
            dk_acc[...] = dk
            dv_acc[...] = dv

        @pl.when(qb != 0)
        def _():
            dk_acc[...] += dk
            dv_acc[...] += dv

        @pl.when(qb == 3)
        def _():
            dk_ref[...] = dk_acc[...].astype(bf)
            dv_ref[...] = dv_acc[...].astype(bf)

    @pl.when(res[0] == 1)
    def _():
        work(pl.ds(0, TOK), True)

    @pl.when(res[0] != 1)
    def _():
        work(pl.ds(pl.multiple_of(qb * 256, 256), 256), False)


def attend_back_fast(resolution, projected, lse, d_attended):
    return pl.pallas_call(
        attend_back_kernel,
        grid_spec=pltpu.PrefetchScalarGridSpec(
            num_scalar_prefetch=1,
            grid=(3, 4),
            in_specs=[
                pl.BlockSpec((256, 128), lambda h, i, r: (i, h)),
                pl.BlockSpec((TOK, 128), lambda h, i, r: (0, 3 + h)),
                pl.BlockSpec((TOK, 128), lambda h, i, r: (0, 6 + h)),
                pl.BlockSpec((256, 128), lambda h, i, r: (i, h)),
                pl.BlockSpec((1, 8, 256), lambda h, i, r: (h, 0, i)),
            ],
            out_specs=[
                pl.BlockSpec((256, 128), lambda h, i, r: (i, h)),
                pl.BlockSpec((TOK, 128), lambda h, i, r: (0, h)),
                pl.BlockSpec((TOK, 128), lambda h, i, r: (0, h)),
            ],
            scratch_shapes=[
                pltpu.VMEM((128, TOK), bf),
                pltpu.VMEM((TOK, 128), f32),
                pltpu.VMEM((TOK, 128), f32),
            ],
        ),
        out_shape=[jax.ShapeDtypeStruct((TOK, D), bf)] * 3,
        compiler_params=pltpu.CompilerParams(vmem_limit_bytes=48 * 1024 * 1024),
        name="attend_back_fast",
    )(resolution, projected, projected, projected, d_attended, lse)


def halves(value):
    high = value.astype(bf)
    return high, (value - high.astype(f32)).astype(bf)


def dot_three(a, b, dims=NN):
    return dot(a[0], b[0], dims) + dot(a[0], b[1], dims) + dot(a[1], b[0], dims)


def up_owner(e):
    return (24 if e % 2 else 0) + e // 2 if e < 8 else 20 + 2 * (e - 8)


def down_owner(e):
    return (4 if e % 2 else 16) + e // 2 if e < 8 else 21 + 2 * (e - 8)


def square_owner(j):
    return 8 + j if j < 3 else (9 + j if j < 7 else 21 + j)


OUT_OWNER, ROUTER_OWNER = 11, 30


def pack_kernel(square, out, router, up, down, packed):
    for e in range(10):
        packed[up_owner(e)] = up[e]
        packed[down_owner(e)] = down[e]
    rest = jnp.zeros((48, D - 96), f32)
    for j in range(9):
        packed[square_owner(j)] = jnp.concatenate([square[j], rest], axis=1)
    packed[OUT_OWNER] = jnp.concatenate([out[...], rest], axis=1)
    packed[ROUTER_OWNER] = router[...]
    packed[31] = jnp.zeros((48, D), f32)


def pack_owned(square, out, router, up, down):
    vmem = pl.BlockSpec(memory_space=pltpu.VMEM)
    return pl.pallas_call(
        pack_kernel,
        out_shape=jax.ShapeDtypeStruct((32, 48, D), f32),
        in_specs=[vmem] * 5,
        out_specs=vmem,
        name="pack_owned",
    )(square, out, router, up, down)


def owned_grad_kernel(ids, *refs):
    pieces = refs[:8]
    dense, small, extra, full_out, cut_out, buf, sems = refs[8:]
    n, z, x = ids[0], ids[1], ids[2]
    is_small = (z == 1) | ((z == 3) & (x == 1))
    left, right = buf.at[:, :, pl.ds(0, FF // 2)], buf.at[:, :, pl.ds(FF // 2, FF // 2)]
    groups = (
        (0, [(pieces[0], buf.at[0]), (pieces[1], buf.at[1])]),
        (2, [(pieces[2], buf.at[0]), (pieces[3], buf.at[1])]),
        (
            3,
            [
                (pieces[4], left.at[0]),
                (pieces[5], left.at[1]),
                (pieces[6], right.at[0]),
                (pieces[7], right.at[1]),
            ],
        ),
    )
    for owner, moves in groups:

        @pl.when((z == owner) & jnp.logical_not(is_small))
        def _():
            copies = [
                pltpu.make_async_copy(source, target, sems.at[i])
                for i, (source, target) in enumerate(moves)
            ]
            for copy in copies:
                copy.start()
            for copy in copies:
                copy.wait()

    @pl.when(jnp.logical_not(is_small))
    def _():
        for k in range(4):
            lanes = slice(k * D, k * D + D)
            full_out[k] = buf[0, :, lanes].astype(f32) + buf[1, :, lanes].astype(f32)

    @pl.when(is_small)
    def _():
        rows = small[...].reshape(32, 8, 512)

        def place(matrix, width):
            rest = jnp.zeros((D, D - width), f32)
            for m in range(4):
                part = matrix[:, m * width : m * width + width]
                full_out[m ^ n] = jnp.concatenate([part, rest], axis=1)

        @pl.when(z == 1)
        def _():
            @pl.when(x == 0)
            def _():
                place(dense[...], 96)

        @pl.when(jnp.logical_not((z == 1) & (x == 0)))
        def _():
            is_router = (z == 3) & (n == 2)

            @pl.when(is_router)
            def _():
                summed = jnp.sum(rows[:, :, :D], axis=0)
                place(jnp.concatenate([summed, jnp.zeros((120, D), f32)], axis=0).T[:, :8], 2)

            @pl.when(jnp.logical_not(is_router))
            def _():
                first = (lax.broadcasted_iota(jnp.int32, (256, D), 0) % 8) < 4
                both = small[:, :D]
                mods = jnp.where(first, both, 0.0)
                conds = pltpu.roll(both, 252, 0)
                conds = jnp.where(first, conds, 0.0)
                place(dot_three(halves(mods), halves(conds), TN), 96)

    for w in range(8):
        for m in range(4):
            cut_out[4 * w + m, :48] = full_out[m ^ n, 48 * w : 48 * w + 48, :].astype(bf)
            cut_out[4 * w + m, 48:] = extra[...]


def owned_grad(ids, pieces, dense, small, extra):
    anyspec, vmem = pl.BlockSpec(memory_space=pl.ANY), pl.BlockSpec(memory_space=pltpu.VMEM)
    return pl.pallas_call(
        owned_grad_kernel,
        out_shape=(
            jax.ShapeDtypeStruct((4, D, D), f32),
            jax.ShapeDtypeStruct((32, 56, D), bf),
        ),
        in_specs=[pl.BlockSpec(memory_space=pltpu.SMEM)] + [anyspec] * 8 + [vmem] * 3,
        out_specs=[vmem, vmem],
        scratch_shapes=[pltpu.VMEM((2, D, FF), bf), pltpu.SemaphoreType.DMA((4,))],
        compiler_params=pltpu.CompilerParams(vmem_limit_bytes=40 * 1024 * 1024),
        name="owned_grad",
    )(ids, *pieces, dense, small, extra)


def ortho_kernel(ids, grad, moment, cut_out, cur, high, low, cross):
    n = ids[0]
    for k in range(4):
        cur[k] = grad[k]
    for w in range(8):
        rows = slice(48 * w, 48 * w + 48)
        for m in range(4):
            cur[m ^ n, rows, :] += MOMENTUM * moment[4 * w + m]
    total = jnp.zeros((1, D), f32)
    for k in range(4):
        total = total + jnp.sum(cur[k] * cur[k], axis=0, keepdims=True)
    factor = 1.0 / (jnp.sqrt(jnp.sum(total, axis=1, keepdims=True)) + 1e-07)

    def keep(k, value):
        cur[k] = value
        high[:, k * D : k * D + D], low[:, k * D : k * D + D] = halves(value)

    for k in range(4):
        keep(k, cur[k] * factor)

    def sweep(_, carry):
        cross[...] = dot(high[...], low[...], NT)
        gram = dot(high[...], high[...], NT) + (cross[...] + cross[...].T)
        gram_high, gram_low = halves(gram)
        cross[...] = dot(gram_high, gram_low)
        square = dot(gram_high, gram_high) + (cross[...] + cross[...].T)
        poly = halves(NS_SECOND * gram + NS_THIRD * square)
        for k in range(4):
            lanes = slice(k * D, k * D + D)
            step = dot_three(poly, (high[:, lanes], low[:, lanes]))
            keep(k, NS_FIRST * cur[k] + step)
        return carry

    lax.fori_loop(0, 5, sweep, 0)
    for w in range(8):
        for m in range(4):
            cut_out[4 * w + m] = cur[m ^ n, 48 * w : 48 * w + 48, :].astype(bf)


def ortho_owned(ids, grad, moment):
    vmem = pl.BlockSpec(memory_space=pltpu.VMEM)
    return pl.pallas_call(
        ortho_kernel,
        out_shape=jax.ShapeDtypeStruct((32, 48, D), bf),
        in_specs=[pl.BlockSpec(memory_space=pltpu.SMEM), vmem, vmem],
        out_specs=vmem,
        scratch_shapes=[
            pltpu.VMEM((4, D, D), f32),
            pltpu.VMEM((D, FF), bf),
            pltpu.VMEM((D, FF), bf),
            pltpu.VMEM((D, D), f32),
        ],
        compiler_params=pltpu.CompilerParams(vmem_limit_bytes=40 * 1024 * 1024),
        name="ortho_owned",
    )(ids, grad, moment)


def update_kernel(decay_ref, grads, orthos, *refs):
    decay = decay_ref[0]
    weights, moments, emas = refs[0:5], refs[5:10], refs[10:15]
    states, masters, averages = refs[15:20], refs[20:25], refs[25:30]
    small_rate, large_rate = RATE * 0.2 * D**0.5, RATE * 0.2 * FF**0.5

    def step(which, at, grad, ortho, rate):
        states[which][at] = MOMENTUM * moments[which][at] + grad.astype(f32)
        master = weights[which][at] - rate * ortho.astype(f32)
        masters[which][at] = master
        averages[which][at] = decay * emas[which][at] + (1.0 - decay) * master

    for j in range(9):
        own = square_owner(j)
        step(0, j, grads[own, :48, :96], orthos[own, :48, :96], small_rate)
    step(1, slice(None), grads[OUT_OWNER, :48, :96], orthos[OUT_OWNER, :48, :96], small_rate)

    def router_rows(source):
        return source[ROUTER_OWNER, :48, :128].astype(f32).T[:2]

    step(2, slice(None), router_rows(grads), router_rows(orthos), small_rate)
    for e in range(10):
        step(3, e, grads[up_owner(e), :48], orthos[up_owner(e), :48], large_rate)
        step(4, e, grads[down_owner(e), :48], orthos[down_owner(e), :48], large_rate)


def update(decay, grads, orthos, weights, moments, emas):
    vmem = pl.BlockSpec(memory_space=pltpu.VMEM)
    shapes = [jax.ShapeDtypeStruct(weight.shape, f32) for weight in weights]
    return pl.pallas_call(
        update_kernel,
        out_shape=shapes * 3,
        in_specs=[pl.BlockSpec(memory_space=pltpu.SMEM)] + [vmem] * 17,
        out_specs=[vmem] * 15,
        compiler_params=pltpu.CompilerParams(vmem_limit_bytes=48 * 1024 * 1024),
        name="update",
    )(decay, grads, orthos, *weights, *moments, *emas)


AXES = (WIDE, NARROW)


def route_pairs(move):
    pairs = []
    for index in range(32):
        w, n = divmod(index, 4)
        target = move(w // 2, w % 2, n // 2, n % 2)
        if target is not None:
            z, x, y, c = target
            pairs.append((index, (z * 2 + x) * 4 + y * 2 + c))
    return pairs


def send(array, move):
    return lax.ppermute(array, AXES, route_pairs(move))


def to_core(z, x, y, c):
    return (z, x, y, 1 - c)


def to_y(z, x, y, c):
    return (z, x, 1 - y, c)


def to_diag(z, x, y, c):
    return (z, x, 1 - y, 1 - c)


def to_x(z, x, y, c):
    return (z, 1 - x, y, c)


def to_z(step):
    return lambda z, x, y, c: ((z + step) % 4, x, y, c)


NARROW_MOVES = (None, to_core, to_y, to_diag)


def pick(array, index, axis=0):
    return lax.dynamic_index_in_dim(array, index, axis, keepdims=False)


def in_order(mine, other, flag):
    return jnp.where(flag == 0, mine, other), jnp.where(flag == 0, other, mine)


def xor_blocks(array, axis, y, c):
    parts = [lax.index_in_dim(array, i, axis, keepdims=True) for i in range(4)]
    parts = [jnp.where(c == 0, parts[i], parts[i ^ 1]) for i in range(4)]
    parts = [jnp.where(y == 0, parts[i], parts[i ^ 2]) for i in range(4)]
    return jnp.concatenate(parts, axis=axis)


def gather_rows(rows, z, x, c):
    pieces = [send(rows, to_z(step)) for step in (3, 2, 1)] + [rows]
    pieces = [pieces[2], pieces[1], pieces[0]]
    recv = {step: send_piece for step, send_piece in zip((1, 2, 3), pieces)}
    ring = jnp.stack([recv[3], recv[2], recv[1], rows])
    doubled = jnp.concatenate([ring, ring])
    by_z = lax.dynamic_slice_in_dim(doubled, (3 - z) % 4, 4, 0)
    by_zx = jnp.stack(in_order(by_z, send(by_z, to_x), x), axis=1)
    return jnp.stack(in_order(by_zx, send(by_zx, to_core), c), axis=2)


def lanes_to(block, width):
    return jnp.pad(block, [(0, 0)] * (block.ndim - 1) + [(0, width - block.shape[-1])])


def turned(array):
    return jnp.swapaxes(array, -1, -2)


def fast_device(
    tokens,
    conditions,
    routes,
    resolution,
    step_count,
    cotangent,
    w_square,
    w_out,
    w_router,
    w_up,
    w_down,
    b_ada,
    moment_square,
    moment_out,
    moment_router,
    moment_up,
    moment_down,
    moment_bias,
    ema_square,
    ema_out,
    ema_router,
    ema_up,
    ema_down,
    ema_bias,
):
    wide = lax.axis_index(WIDE)
    narrow = lax.axis_index(NARROW)
    z, x = wide // 2, wide % 2
    y, c = narrow // 2, narrow % 2

    square_t = turned(w_square).astype(bf)
    out_t = turned(w_out).astype(bf)[None]
    misc = jnp.concatenate(
        [
            lanes_to(b_ada.astype(bf)[None], 96),
            lanes_to(w_router.astype(bf), 96),
            jnp.zeros((5, 96), bf),
        ]
    )
    flat = jnp.concatenate(
        [
            square_t[:5].reshape(-1, 96),
            misc,
            square_t[5:].reshape(-1, 96),
            out_t.reshape(-1, 96),
        ]
    )
    lanes = jnp.stack([flat] + [send(flat, move) for move in NARROW_MOVES[1:]])
    rows = jnp.concatenate(list(xor_blocks(lanes, 0, y, c)), axis=1)

    def my_half(block):
        return pick(block.reshape(5, 2, 24, D), c, 1).reshape(120, D)

    first_rows = jnp.concatenate([my_half(rows[:240]), rows[240:248]])
    first_all = gather_rows(first_rows, z, x, c)
    second_all = gather_rows(my_half(rows[248:]), z, x, c)

    def assemble(gathered):
        parts = gathered[..., :120, :].reshape(8, 2, 5, 24, D)
        return jnp.transpose(parts, (2, 0, 1, 3, 4)).reshape(5, D, D)

    first_maps = assemble(first_all)
    second_maps = assemble(second_all)
    misc_all = first_all[:, :, 0, 120:, :].reshape(8, 8, 4, 96)
    bias_low = misc_all[:, 0, :, :72].reshape(-1)
    router_low = jnp.transpose(misc_all[:, 1:3, :, :48], (2, 1, 0, 3)).reshape(ROUTED, D)

    up_t = turned(w_up).astype(bf)
    down_t = turned(w_down).astype(bf)
    routed_t = jnp.stack([up_t[:8], down_t[:8]], axis=1).reshape(4, 4, 48, D)
    shared_t = jnp.stack([up_t[8:], down_t[8:]], axis=1).reshape(4, 48, D)
    mine = [pick(routed_t, narrow)]
    mine += [send(pick(routed_t, narrow ^ k), NARROW_MOVES[k]) for k in (1, 2, 3)]
    gathered = lax.all_gather(jnp.stack(mine + [shared_t]), WIDE)

    moment_parts = (
        turned(moment_square),
        turned(moment_out),
        moment_router,
        turned(moment_up),
        turned(moment_down),
    )
    router_block = lanes_to(turned(moment_router), D)
    moments = pack_owned(*moment_parts[:2], router_block, *moment_parts[3:])

    res_group = resolution[0]
    token_f = tokens.astype(f32)
    segments = tokens.shape[0] // SHORT
    seg_ratio = LONG // SHORT
    first_seg = jnp.arange(segments, dtype=jnp.int32) // seg_ratio * seg_ratio
    chosen = jnp.where(res_group == 1, conditions[first_seg], conditions)
    cond_low = jax.nn.silu(chosen.astype(f32)).astype(bf)
    bias_rows = bias_low.astype(f32).reshape(6, D)

    def modulation_of(maps, bias):
        return dot(cond_low, maps.reshape(-1, D), NT).reshape(segments, -1, D) + bias

    first_two = modulation_of(first_maps[3:], bias_rows[:2])
    last_four = modulation_of(second_maps[:4], bias_rows[2:])
    out_map = second_maps[4]
    seg_rows = token_f.reshape(segments, SHORT, D)
    first_mod, first_back = jax.vjp(modulate, seg_rows, first_two[:, 0:1], first_two[:, 1:2])
    hidden_one = first_mod.reshape(-1, D).astype(bf)
    query_maps = first_maps[:3].reshape(3 * D, D)
    projected = dot(hidden_one, query_maps, NT).astype(bf)
    gate_one, gate_two = last_four[:, 0:1], last_four[:, 3:4]
    grad_out = cotangent.astype(f32)
    grad_seg = grad_out.reshape(segments, SHORT, D)
    d_mixture = (grad_seg * gate_two).reshape(-1, D).astype(bf)
    d_mix_core = send(d_mixture, to_core)
    d_mix_y = send(d_mixture, to_y)
    attended, log_total = attend_fast(resolution, projected)
    attended, d_mix_y = lax.optimization_barrier((attended, d_mix_y))
    d_mix_diag = send(d_mix_y, to_core)
    attn_out = dot(attended, out_map, NT)
    mid_state = token_f + (attn_out.reshape(segments, SHORT, D) * gate_one).reshape(-1, D)
    second_mod, second_back = jax.vjp(
        modulate, mid_state.reshape(segments, SHORT, D), last_four[:, 1:2], last_four[:, 2:3]
    )
    hidden_two = second_mod.reshape(-1, D).astype(bf)

    logits = dot(router_low, hidden_two, NT)
    experts = jnp.arange(ROUTED, dtype=jnp.int32)[:, None]
    named = (routes[:, 0][None] == experts) | (routes[:, 1][None] == experts)
    index = jnp.arange(TOK, dtype=jnp.int32)
    earlier = (index[:, None] < index[None, :]).astype(bf)
    place = jnp.dot(named.astype(bf), earlier, preferred_element_type=f32)
    masked = jnp.where(named, logits, -jnp.inf)
    expo = jnp.where(named, jnp.exp(logits - jnp.max(masked, axis=0, keepdims=True)), 0.0)
    gates = expo / jnp.sum(expo, axis=0, keepdims=True)
    meta = jnp.concatenate([jnp.where(named, place, -1.0), gates])

    hidden_core, meta_core = send(hidden_two, to_core), send(meta, to_core)
    hidden_y, meta_y = send(hidden_two, to_y), send(meta, to_y)
    meta_diag = send(meta, to_diag)
    hidden_y, _ = lax.optimization_barrier((hidden_y, meta))
    hidden_diag = send(hidden_y, to_core)
    place_ids = jnp.stack([narrow, z, x]).astype(jnp.int32)
    hidden_diag, moments = lax.optimization_barrier((hidden_diag, moments))
    moments = lax.all_to_all(moments, AXES, 0, 0, tiled=True)
    part_y, part_diag, gate_far, *first_grads = moe(
        place_ids, (hidden_y, hidden_diag), (d_mix_y, d_mix_diag), (meta_y, meta_diag), gathered
    )
    over = (part_y.astype(f32) + send(part_diag, to_core).astype(f32)).astype(bf)
    over, moments, hidden_mine = lax.optimization_barrier((over, moments, hidden_two))
    returned = send(over, to_y)
    part_own, part_core, gate_near, *grads = moe(
        place_ids,
        (hidden_mine, hidden_core),
        (d_mixture, d_mix_core),
        (meta, meta_core),
        gathered,
        first_grads,
    )
    part_own, part_core, gate_near, grads, returned = lax.optimization_barrier(
        (part_own, part_core, gate_near, grads, returned)
    )
    own = part_own.astype(f32) + send(part_core, to_core).astype(f32)
    total = own + returned.astype(f32)
    mixture, d_hidden = total[:, :D], total[:, D:]
    d_rows = [gate_near[0, :2], send(gate_near[1, :2], to_core)]
    d_rows += [send(gate_far[0, :2], to_y), send(gate_far[1, :2], to_diag)]
    d_gates = xor_blocks(jnp.stack(d_rows), 0, y, c).reshape(ROUTED, TOK)

    g_send, g_keep, g_second, g_left, g_right, g_shared = grads

    def shared_part(k):
        return lax.dynamic_slice_in_dim(g_shared, (narrow ^ k) * D, D, 1)

    shared_grad = jnp.concatenate(
        [shared_part(0)] + [send(shared_part(k), NARROW_MOVES[k]) for k in (1, 2, 3)], axis=1
    )

    def back_x(z_, x_, y_, c_):
        return (z_, 0, y_, c_) if x_ == 1 else None

    def along_z(hops, sides=(0, 1)):
        table = dict(hops)

        def move(z_, x_, y_, c_):
            return (table[z_], x_, y_, c_) if z_ in table and x_ in sides else None

        return move

    def added(kept, other):
        return (kept.astype(f32) + other.astype(f32)).astype(bf)

    def to_owner(held, pairs, last_hop, sides=(0, 1)):
        held = added(held, send(held, along_z(pairs, sides)))
        return held, send(held, along_z(last_hop, sides))

    received_one = send(g_send, to_x)
    received_two = send(jnp.where(x == 0, shared_grad, g_second), to_x)
    kept_two = jnp.where(x == 0, g_second, shared_grad)

    output = (
        mid_state + (mixture.reshape(segments, SHORT, D) * gate_two).reshape(-1, D)
    ).astype(bf)
    d_gate_two = jnp.sum(grad_seg * mixture.reshape(segments, SHORT, D), axis=1)
    d_logits = gates * (d_gates - jnp.sum(gates * d_gates, axis=0, keepdims=True))
    d_logits = d_logits.astype(bf)
    g_router = jnp.dot(d_logits, hidden_two, preferred_element_type=f32)
    d_hidden = d_hidden + dot(d_logits, router_low, TN)
    d_mid_norm, d_shift_two, d_scale_two = second_back(d_hidden.reshape(segments, SHORT, D))
    d_mid = grad_out + d_mid_norm.reshape(-1, D)
    d_mid_seg = d_mid.reshape(segments, SHORT, D)
    d_gate_one = jnp.sum(d_mid_seg * attn_out.reshape(segments, SHORT, D), axis=1)
    d_attn = (d_mid_seg * gate_one).reshape(-1, D).astype(bf)
    g_out = dot(d_attn, attended, TN)
    d_attended = jnp.dot(d_attn, out_map, preferred_element_type=f32).astype(bf)
    received_left, received_right = send(g_left, back_x), send(g_right, back_x)
    d_heads = attend_back_fast(resolution, projected, log_total, d_attended)
    d_heads, received_one, received_left, received_right = lax.optimization_barrier(
        (d_heads, received_one, received_left, received_right)
    )
    held_one = added(g_keep, received_one)
    held_left = added(g_left, received_left)
    held_right = added(g_right, received_right)
    g_qkv = jnp.stack([dot(d_head, hidden_one, TN) for d_head in d_heads])
    d_hidden_one = sum(
        jnp.dot(d_head, first_maps[j], preferred_element_type=f32)
        for j, d_head in enumerate(d_heads)
    )
    d_rows_one, d_shift_one, d_scale_one = first_back(d_hidden_one.reshape(segments, SHORT, D))
    grad_in = d_mid + d_rows_one.reshape(-1, D)
    d_modulation = [
        d_shift_one[:, 0],
        d_scale_one[:, 0],
        d_gate_one,
        d_shift_two[:, 0],
        d_scale_two[:, 0],
        d_gate_two,
    ]

    dense = jnp.concatenate([g_qkv, g_out[None]]).reshape(2, 2, D, D)
    dense = pick(dense, c, 1) + send(pick(dense, 1 - c, 1).astype(bf), to_core).astype(f32)
    dense = pick(dense, y) + send(pick(dense, 1 - y).astype(bf), to_y).astype(f32)
    dense, received_two = lax.optimization_barrier((dense, received_two))
    held_two = added(kept_two, received_two)
    dense = dense + send(dense.astype(bf), back_x).astype(f32)
    dense_low = dense.astype(bf)
    for step in (1, 2, 3):

        def to_second(z_, x_, y_, c_, step=step):
            return (1, x_, y_, c_) if (z_ + step) % 4 == 1 and x_ == 0 else None

        dense = dense + send(dense_low, to_second).astype(f32)

    cond_rows = cond_low.astype(f32)
    ada_rows = [jnp.concatenate([d_mod, cond_rows]) for d_mod in d_modulation]
    payload = jnp.zeros((8, 4, 8, D), f32)
    payload = payload.at[3].set(jnp.stack(ada_rows[:4]))
    payload = payload.at[7, :3].set(jnp.stack(ada_rows[4:] + [g_router]))
    bias_part = jnp.concatenate([jnp.sum(d_mod, axis=0) for d_mod in d_modulation])
    bias_part = jnp.pad(bias_part.reshape(8, 4, 1, 72), ((0, 0), (0, 0), (0, 7), (0, 56)))
    small = jnp.concatenate([payload, bias_part], axis=3).reshape(32, 8, 512)
    small = lax.all_to_all(small, AXES, 0, 0, tiled=True)
    g_bias = jnp.sum(small[:, 0, D : D + 72], axis=0)
    pieces = to_owner(held_one, ((3, 2), (1, 0)), ((2, 0),))
    pieces += to_owner(held_two, ((0, 1), (3, 2)), ((1, 2),))
    pieces += to_owner(held_left, ((0, 1), (2, 3)), ((1, 3),), (0,))
    pieces += to_owner(held_right, ((0, 1), (2, 3)), ((1, 3),), (0,))
    state_bias = MOMENTUM_VECTOR * moment_bias + g_bias
    part_sum = jnp.sum(state_bias * state_bias)
    sum_high = part_sum.astype(bf)
    sum_low = (part_sum - sum_high.astype(f32)).astype(bf)

    extra = jnp.pad(jnp.stack([sum_high, sum_low])[None], ((0, 7), (0, D - 2)))
    grad_full, grad_cut = owned_grad(place_ids, pieces, dense, small.reshape(256, 512), extra)
    grad_parts = lax.all_to_all(grad_cut, AXES, 0, 0, tiled=True)

    ortho_cut = ortho_owned(place_ids, grad_full, moments)
    ortho_cut, grad_parts = lax.optimization_barrier((ortho_cut, grad_parts))
    ortho_parts = lax.all_to_all(ortho_cut, AXES, 0, 0, tiled=True)
    square_total = jnp.sum(grad_parts[:, 48, :2].astype(f32))

    step_value = step_count[0].astype(f32)
    decay = jnp.minimum(0.9999, (1.0 + step_value) / (10.0 + step_value))
    masters = (turned(w_square), turned(w_out), w_router, turned(w_up), turned(w_down))
    emas = (turned(ema_square), turned(ema_out), ema_router, turned(ema_up), turned(ema_down))
    updated = update(decay[None], grad_parts, ortho_parts, masters, moment_parts, emas)
    results = []
    for which in range(5):
        results += [
            array if which == 2 else turned(array) for array in updated[which::5]
        ]
    root_mean = jnp.sqrt(square_total / (6 * D) + 1e-05)
    master_bias = b_ada - RATE_VECTOR * state_bias / root_mean
    average_bias = decay * ema_bias + (1.0 - decay) * master_bias
    return (output, grad_in, *results, state_bias, master_bias, average_bias)


def solution(mesh):
    placed = (
        P((WIDE, NARROW), None),
        P((WIDE, NARROW), None),
        P((WIDE, NARROW), None),
        P((WIDE, NARROW)),
        P(),
        P((WIDE, NARROW), None),
        P(None, NARROW, WIDE),
        P(NARROW, WIDE),
        P(NARROW, WIDE),
        P(None, NARROW, WIDE),
        P(None, NARROW, WIDE),
        P((WIDE, NARROW)),
        P(None, NARROW, WIDE),
        P(NARROW, WIDE),
        P(NARROW, WIDE),
        P(None, NARROW, WIDE),
        P(None, NARROW, WIDE),
        P((WIDE, NARROW)),
        P(None, NARROW, WIDE),
        P(NARROW, WIDE),
        P(NARROW, WIDE),
        P(None, NARROW, WIDE),
        P(None, NARROW, WIDE),
        P((WIDE, NARROW)),
    )
    device_body = fast_device if dict(mesh.shape) == {WIDE: 8, NARROW: 4} else on_device
    return jax.shard_map(
        device_body,
        mesh=mesh,
        in_specs=placed,
        out_specs=(
            P((WIDE, NARROW), None),
            P((WIDE, NARROW), None),
            P(None, NARROW, WIDE),
            P(None, NARROW, WIDE),
            P(None, NARROW, WIDE),
            P(NARROW, WIDE),
            P(NARROW, WIDE),
            P(NARROW, WIDE),
            P(NARROW, WIDE),
            P(NARROW, WIDE),
            P(NARROW, WIDE),
            P(None, NARROW, WIDE),
            P(None, NARROW, WIDE),
            P(None, NARROW, WIDE),
            P(None, NARROW, WIDE),
            P(None, NARROW, WIDE),
            P(None, NARROW, WIDE),
            P((WIDE, NARROW)),
            P((WIDE, NARROW)),
            P((WIDE, NARROW)),
        ),
        check_vma=False,
    )
```

```python
from functools import partial

import jax
import jax.numpy as jnp
from jax import lax
from jax.experimental import pallas as pl
from jax.experimental.pallas import tpu as pltpu
from jax.sharding import PartitionSpec as P

WIDE, NARROW = "wide", "narrow"
D = 384
HEADS = 6
HEAD = 64
FF = 1536
TOP = 2
ROUTED = 8
SHORT = 256
LONG = 1024
CAP = 384


PRECISE = lax.Precision.HIGHEST
EPSILON = 1e-06
NS_FIRST = 3.4445
NS_SECOND = -4.775
NS_THIRD = 2.0315
MOMENTUM = 0.95
MOMENTUM_VECTOR = 0.5
RATE = 0.25
RATE_VECTOR = 0.05


def as_sent(array):

    def short(part):
        return part.astype(jnp.bfloat16) if part.dtype == jnp.float32 else part

    return jax.tree.map(short, array)


def modulate(seg_rows, shift_by, scale_by):
    center = seg_rows - jnp.mean(seg_rows, axis=-1, keepdims=True)
    normed = center * lax.rsqrt(jnp.mean(center * center, axis=-1, keepdims=True) + EPSILON)
    return normed * (1.0 + scale_by) + shift_by


def gelu_tanh(values):
    return jax.nn.gelu(values, approximate=True)


def gelu_grad(pre_act, upstream):
    _, pull_back = jax.vjp(gelu_tanh, pre_act)
    return pull_back(upstream)[0]


def slot_table(route_rows):
    flat_routes = route_rows.reshape(-1)
    hot_table = (flat_routes[:, None] == jnp.arange(ROUTED, dtype=jnp.int32)[None, :]).astype(
        jnp.int32
    )
    earlier = jnp.cumsum(hot_table, axis=0, dtype=jnp.int32) - hot_table
    place_in = jnp.sum(earlier * hot_table, axis=1, dtype=jnp.int32)
    slot_ids = flat_routes * CAP + place_in
    sources = jnp.arange(slot_ids.shape[0], dtype=jnp.int32) // TOP
    slot_owner = jnp.zeros((ROUTED * CAP,), jnp.int32).at[slot_ids].set(sources)
    return (slot_ids, slot_owner)


def attend(projected, length):
    image_count = projected.shape[1] // length
    split_parts = projected.reshape(3, image_count, length, HEADS, HEAD)
    scores = jnp.einsum(
        "bqhe,bkhe->bhqk", split_parts[0], split_parts[1], preferred_element_type=jnp.float32
    ) * HEAD ** (-0.5)
    highest = jnp.max(scores, axis=-1, keepdims=True)
    expo = jnp.exp(scores - highest)
    totals = jnp.sum(expo, axis=-1, keepdims=True)
    weights_low = (expo / totals).astype(jnp.bfloat16)
    mixed_heads = jnp.einsum(
        "bhqk,bkhe->bqhe", weights_low, split_parts[2], preferred_element_type=jnp.float32
    )
    log_total = (highest + jnp.log(totals))[..., 0]
    return (
        mixed_heads.reshape(-1, D).astype(jnp.bfloat16),
        jnp.transpose(log_total, (0, 2, 1)).reshape(-1, HEADS),
    )


def attend_back(projected, log_total, d_attended, length):
    image_count = projected.shape[1] // length
    split_parts = projected.reshape(3, image_count, length, HEADS, HEAD)
    scale_qk = HEAD ** (-0.5)
    scores = (
        jnp.einsum(
            "bqhe,bkhe->bhqk", split_parts[0], split_parts[1], preferred_element_type=jnp.float32
        )
        * scale_qk
    )
    log_four = jnp.transpose(log_total.reshape(image_count, length, HEADS), (0, 2, 1))[..., None]
    probs = jnp.exp(scores - log_four)
    weights_low = probs.astype(jnp.bfloat16)
    d_heads = d_attended.reshape(image_count, length, HEADS, HEAD)
    d_weights = jnp.einsum(
        "bqhe,bkhe->bhqk", d_heads, split_parts[2], preferred_element_type=jnp.float32
    )
    d_values = jnp.einsum(
        "bhqk,bqhe->bkhe", weights_low, d_heads, preferred_element_type=jnp.float32
    )
    d_scores = (probs * (d_weights - jnp.sum(d_weights * probs, axis=-1, keepdims=True))).astype(
        jnp.bfloat16
    )
    d_queries = (
        jnp.einsum("bhqk,bkhe->bqhe", d_scores, split_parts[1], preferred_element_type=jnp.float32)
        * scale_qk
    )
    d_keys = (
        jnp.einsum("bhqk,bqhe->bkhe", d_scores, split_parts[0], preferred_element_type=jnp.float32)
        * scale_qk
    )
    return jnp.stack([d_queries, d_keys, d_values]).reshape(3, -1, D).astype(jnp.bfloat16)


def on_device(
    tokens,
    conditions,
    routes,
    resolution,
    step_count,
    cotangent,
    w_square,
    w_out,
    w_router,
    w_up,
    w_down,
    b_ada,
    moment_square,
    moment_out,
    moment_router,
    moment_up,
    moment_down,
    moment_bias,
    ema_square,
    ema_out,
    ema_router,
    ema_up,
    ema_down,
    ema_bias,
):
    bf_type = jnp.bfloat16
    fl_type = jnp.float32
    row_pieces = (
        lax.all_gather(w_square.astype(bf_type), NARROW, axis=1, tiled=True),
        lax.all_gather(w_out.astype(bf_type), NARROW, axis=0, tiled=True),
        lax.all_gather(w_router.astype(bf_type), NARROW, axis=0, tiled=True),
        lax.all_gather(w_up.astype(bf_type), NARROW, axis=1, tiled=True),
        lax.all_gather(w_down.astype(bf_type), NARROW, axis=1, tiled=True),
        lax.all_gather(b_ada.astype(bf_type), NARROW, axis=0, tiled=True),
    )
    whole_low = (
        lax.all_gather(row_pieces[0], WIDE, axis=2, tiled=True),
        lax.all_gather(row_pieces[1], WIDE, axis=1, tiled=True),
        lax.all_gather(row_pieces[2], WIDE, axis=1, tiled=True),
        lax.all_gather(row_pieces[3], WIDE, axis=2, tiled=True),
        lax.all_gather(row_pieces[4], WIDE, axis=2, tiled=True),
        lax.all_gather(row_pieces[5], WIDE, axis=0, tiled=True),
    )
    square_low, out_low, router_low, up_low, down_low, bias_low = whole_low
    res_group = resolution[0]
    token_f = tokens.astype(fl_type)
    segments = tokens.shape[0] // SHORT
    seg_ratio = LONG // SHORT
    first_seg = jnp.arange(segments, dtype=jnp.int32) // seg_ratio * seg_ratio
    chosen = jnp.where(res_group == 1, conditions[first_seg], conditions)
    cond_low = jax.nn.silu(chosen.astype(fl_type)).astype(bf_type)
    modulation = jnp.einsum(
        "sd,jde->sje", cond_low, square_low[3:], preferred_element_type=fl_type
    ) + bias_low.astype(fl_type).reshape(6, D)
    seg_rows = token_f.reshape(segments, SHORT, D)
    first_mod, first_back = jax.vjp(modulate, seg_rows, modulation[:, 0:1], modulation[:, 1:2])
    hidden_one = first_mod.reshape(-1, D).astype(bf_type)
    projected = jnp.einsum(
        "td,jde->jte", hidden_one, square_low[:3], preferred_element_type=fl_type
    ).astype(bf_type)
    attended, log_total = lax.cond(
        res_group == 1, partial(attend, length=LONG), partial(attend, length=SHORT), projected
    )
    attn_out = jnp.dot(attended, out_low, preferred_element_type=fl_type)
    mid_state = token_f + (attn_out.reshape(segments, SHORT, D) * modulation[:, 2:3]).reshape(-1, D)
    second_mod, second_back = jax.vjp(
        modulate, mid_state.reshape(segments, SHORT, D), modulation[:, 3:4], modulation[:, 4:5]
    )
    hidden_two = second_mod.reshape(-1, D).astype(bf_type)
    logits = jnp.einsum("td,rd->tr", hidden_two, router_low, preferred_element_type=fl_type)
    gate_probs = jax.nn.softmax(jnp.take_along_axis(logits, routes, axis=1), axis=1)
    slot_ids, slot_owner = slot_table(routes)
    inputs = hidden_two[slot_owner].reshape(ROUTED, CAP, D)
    pre_act = jnp.einsum("ecd,efd->ecf", inputs, up_low[:ROUTED], preferred_element_type=fl_type)
    act_low = gelu_tanh(pre_act).astype(bf_type)
    produced = jnp.einsum(
        "ecf,efd->ecd", act_low, down_low[:ROUTED], preferred_element_type=fl_type
    ).reshape(-1, D)
    chosen_out = produced[slot_ids].reshape(-1, TOP, D)
    routed = jnp.sum(chosen_out * gate_probs[:, :, None], axis=1)
    shared_pre = jnp.einsum(
        "td,sfd->stf", hidden_two, up_low[ROUTED:], preferred_element_type=fl_type
    )
    shared_act = gelu_tanh(shared_pre).astype(bf_type)
    shared_out = jnp.einsum(
        "stf,sfd->std", shared_act, down_low[ROUTED:], preferred_element_type=fl_type
    )
    mixture = routed + jnp.sum(shared_out, axis=0)
    output = (
        mid_state + (mixture.reshape(segments, SHORT, D) * modulation[:, 5:6]).reshape(-1, D)
    ).astype(bf_type)
    again_rows = (
        lax.all_gather(w_square.astype(bf_type), NARROW, axis=1, tiled=True),
        lax.all_gather(w_out.astype(bf_type), NARROW, axis=0, tiled=True),
        lax.all_gather(w_router.astype(bf_type), NARROW, axis=0, tiled=True),
        lax.all_gather(w_up.astype(bf_type), NARROW, axis=1, tiled=True),
        lax.all_gather(w_down.astype(bf_type), NARROW, axis=1, tiled=True),
    )
    again_whole = (
        lax.all_gather(again_rows[0], WIDE, axis=2, tiled=True),
        lax.all_gather(again_rows[1], WIDE, axis=1, tiled=True),
        lax.all_gather(again_rows[2], WIDE, axis=1, tiled=True),
        lax.all_gather(again_rows[3], WIDE, axis=2, tiled=True),
        lax.all_gather(again_rows[4], WIDE, axis=2, tiled=True),
    )
    square_low, out_low, router_low, up_low, down_low = again_whole
    grad_out = cotangent.astype(fl_type)
    grad_seg = grad_out.reshape(segments, SHORT, D)
    d_gate_two = jnp.sum(grad_seg * mixture.reshape(segments, SHORT, D), axis=1)
    d_mixture = (grad_seg * modulation[:, 5:6]).reshape(-1, D)
    d_shared = d_mixture.astype(bf_type)
    d_shared_act = jnp.einsum(
        "td,sfd->stf", d_shared, down_low[ROUTED:], preferred_element_type=fl_type
    )
    d_shared_pre = gelu_grad(shared_pre, d_shared_act).astype(bf_type)
    g_shared_down = jnp.einsum("stf,td->sfd", shared_act, d_shared, preferred_element_type=fl_type)
    g_shared_up = jnp.einsum(
        "stf,td->sfd", d_shared_pre, hidden_two, preferred_element_type=fl_type
    )
    d_hidden = jnp.einsum(
        "stf,sfd->td", d_shared_pre, up_low[ROUTED:], preferred_element_type=fl_type
    )
    d_gates = jnp.sum(d_mixture[:, None, :] * chosen_out, axis=2)
    gate_slot = jnp.zeros((ROUTED * CAP,), fl_type).at[slot_ids].set(gate_probs.reshape(-1))
    d_produced = (
        (gate_slot[:, None] * d_mixture[slot_owner]).astype(bf_type).reshape(ROUTED, CAP, D)
    )
    d_act = jnp.einsum(
        "ecd,efd->ecf", d_produced, down_low[:ROUTED], preferred_element_type=fl_type
    )
    d_pre = gelu_grad(pre_act, d_act).astype(bf_type)
    g_routed_down = jnp.einsum("ecf,ecd->efd", act_low, d_produced, preferred_element_type=fl_type)
    g_routed_up = jnp.einsum("ecf,ecd->efd", d_pre, inputs, preferred_element_type=fl_type)
    d_inputs = jnp.einsum(
        "ecf,efd->ecd", d_pre, up_low[:ROUTED], preferred_element_type=fl_type
    ).reshape(-1, D)
    d_hidden = d_hidden + jnp.sum(d_inputs[slot_ids].reshape(-1, TOP, D), axis=1)
    d_picked = gate_probs * (d_gates - jnp.sum(gate_probs * d_gates, axis=1, keepdims=True))
    route_hot = (routes[:, :, None] == jnp.arange(ROUTED, dtype=jnp.int32)[None, None, :]).astype(
        fl_type
    )
    d_logits = jnp.sum(route_hot * d_picked[:, :, None], axis=1).astype(bf_type)
    g_router = jnp.einsum("tr,td->rd", d_logits, hidden_two, preferred_element_type=fl_type)
    d_hidden = d_hidden + jnp.einsum(
        "tr,rd->td", d_logits, router_low, preferred_element_type=fl_type
    )
    d_mid_norm, d_shift_two, d_scale_two = second_back(d_hidden.reshape(segments, SHORT, D))
    d_mid = grad_out + d_mid_norm.reshape(-1, D)
    d_gate_one = jnp.sum(
        d_mid.reshape(segments, SHORT, D) * attn_out.reshape(segments, SHORT, D), axis=1
    )
    d_attn = (d_mid.reshape(segments, SHORT, D) * modulation[:, 2:3]).reshape(-1, D).astype(bf_type)
    g_out = jnp.einsum("td,te->de", attended, d_attn, preferred_element_type=fl_type)
    d_attended = jnp.einsum("te,de->td", d_attn, out_low, preferred_element_type=fl_type).astype(
        bf_type
    )
    d_projected = lax.cond(
        res_group == 1,
        partial(attend_back, length=LONG),
        partial(attend_back, length=SHORT),
        projected,
        log_total,
        d_attended,
    )
    g_qkv = jnp.einsum("td,jte->jde", hidden_one, d_projected, preferred_element_type=fl_type)
    d_hidden_one = jnp.einsum(
        "jte,jde->td", d_projected, square_low[:3], preferred_element_type=fl_type
    )
    d_rows, d_shift_one, d_scale_one = first_back(d_hidden_one.reshape(segments, SHORT, D))
    grad_in = d_mid + d_rows.reshape(-1, D)
    d_modulation = jnp.stack(
        [
            d_shift_one[:, 0],
            d_scale_one[:, 0],
            d_gate_one,
            d_shift_two[:, 0],
            d_scale_two[:, 0],
            d_gate_two,
        ],
        axis=1,
    )
    g_ada = jnp.einsum("sd,sje->jde", cond_low.astype(fl_type), d_modulation, precision=PRECISE)
    g_bias = jnp.sum(d_modulation, axis=0).reshape(-1)
    g_square = jnp.concatenate([g_qkv, g_ada], axis=0)
    g_up = jnp.concatenate([g_routed_up, g_shared_up], axis=0)
    g_down = jnp.concatenate([g_routed_down, g_shared_down], axis=0)
    by_columns = (
        lax.psum_scatter(g_square, WIDE, scatter_dimension=2, tiled=True),
        lax.psum_scatter(g_out, WIDE, scatter_dimension=1, tiled=True),
        lax.psum_scatter(g_router, WIDE, scatter_dimension=1, tiled=True),
        lax.psum_scatter(g_up, WIDE, scatter_dimension=2, tiled=True),
        lax.psum_scatter(g_down, WIDE, scatter_dimension=2, tiled=True),
        lax.psum_scatter(g_bias, WIDE, scatter_dimension=0, tiled=True),
    )
    summed = (
        lax.psum_scatter(by_columns[0], NARROW, scatter_dimension=1, tiled=True),
        lax.psum_scatter(by_columns[1], NARROW, scatter_dimension=0, tiled=True),
        lax.psum_scatter(by_columns[2], NARROW, scatter_dimension=0, tiled=True),
        lax.psum_scatter(by_columns[3], NARROW, scatter_dimension=1, tiled=True),
        lax.psum_scatter(by_columns[4], NARROW, scatter_dimension=1, tiled=True),
        lax.psum_scatter(by_columns[5], NARROW, scatter_dimension=0, tiled=True),
    )
    state_square = MOMENTUM * moment_square + summed[0]
    state_out = MOMENTUM * moment_out + summed[1]
    state_router = MOMENTUM * moment_router + summed[2]
    state_up = MOMENTUM * moment_up + summed[3]
    state_down = MOMENTUM * moment_down + summed[4]
    local_rows = w_up.shape[1]

    def padded(block):
        return jnp.pad(block, ((0, 0), (0, local_rows - block.shape[1]), (0, 0)))

    stacked = jnp.concatenate(
        [
            padded(state_square),
            padded(state_out[None]),
            padded(state_router[None]),
            state_up,
            state_down,
        ],
        axis=0,
    )
    wide_count = lax.axis_size(WIDE)
    matrices = stacked.shape[0]
    per_owner = -(-matrices // wide_count)
    stacked = jnp.pad(stacked, ((0, per_owner * wide_count - matrices), (0, 0), (0, 0)))
    current = lax.all_to_all(stacked, WIDE, split_axis=0, concat_axis=2, tiled=True)
    for sweep_num in range(5):
        gram_mat = lax.psum(
            jnp.einsum("mrc,mrd->mcd", current, current, precision=PRECISE).astype(jnp.bfloat16),
            NARROW,
        ).astype(jnp.float32)
        if sweep_num == 0:
            factor = 1.0 / (jnp.sqrt(jnp.trace(gram_mat, axis1=1, axis2=2)) + 1e-07)
            current = current * factor[:, None, None]
            gram_mat = gram_mat * (factor * factor)[:, None, None]
        polynomial = NS_SECOND * gram_mat + NS_THIRD * jnp.einsum(
            "mcd,mde->mce", gram_mat, gram_mat, precision=PRECISE
        )
        current = NS_FIRST * current + jnp.einsum(
            "mrc,mcd->mrd", current, polynomial, precision=PRECISE
        )
    spread_back = lax.all_to_all(
        as_sent(current), WIDE, split_axis=2, concat_axis=0, tiled=True
    ).astype(current.dtype)[:matrices]
    expert_total = w_up.shape[0]
    small_factor = RATE * 0.2 * D**0.5
    large_factor = RATE * 0.2 * FF**0.5
    master_square = w_square - small_factor * spread_back[0:9, : w_square.shape[1]]
    master_out = w_out - small_factor * spread_back[9, : w_out.shape[0]]
    master_router = w_router - small_factor * spread_back[10, : w_router.shape[0]]
    master_up = w_up - large_factor * spread_back[11 : 11 + expert_total]
    master_down = w_down - large_factor * spread_back[11 + expert_total : 11 + 2 * expert_total]
    state_bias = MOMENTUM_VECTOR * moment_bias + summed[5]
    square_total = lax.psum(jnp.sum(state_bias * state_bias), (WIDE, NARROW))
    root_mean = jnp.sqrt(square_total / (6 * D) + 1e-05)
    master_bias = b_ada - RATE_VECTOR * state_bias / root_mean
    step_value = step_count[0].astype(fl_type)
    decay = jnp.minimum(0.9999, (1.0 + step_value) / (10.0 + step_value))
    average_square = decay * ema_square + (1.0 - decay) * master_square
    average_out = decay * ema_out + (1.0 - decay) * master_out
    average_router = decay * ema_router + (1.0 - decay) * master_router
    average_up = decay * ema_up + (1.0 - decay) * master_up
    average_down = decay * ema_down + (1.0 - decay) * master_down
    average_bias = decay * ema_bias + (1.0 - decay) * master_bias
    return (
        output,
        grad_in,
        state_square,
        master_square,
        average_square,
        state_out,
        master_out,
        average_out,
        state_router,
        master_router,
        average_router,
        state_up,
        master_up,
        average_up,
        state_down,
        master_down,
        average_down,
        state_bias,
        master_bias,
        average_bias,
    )


bf = jnp.bfloat16
f32 = jnp.float32
TOK = 1024
ROWS = 512
UNITS = 512
NN = (((1,), (0,)), ((), ()))
NT = (((1,), (1,)), ((), ()))
TN = (((0,), (0,)), ((), ()))


def dot(a, b, dims=NN):
    return lax.dot_general(a, b, dims, preferred_element_type=f32)


def gelu_pair(pre):
    sq = pre * pre
    th = jnp.tanh(pre * (0.7978845608028654 + 0.035677408136300125 * sq))
    half = 0.5 * th + 0.5
    act = pre * half
    slope = half + act * (1.0 - half) * (1.5957691216057308 + 0.21406444881780075 * sq)
    return act, slope


def units(xs, ds, up_ref, down_ref, g_up_ref, g_down_ref, count):
    out = jnp.zeros(xs.shape, f32)
    dx = jnp.zeros(xs.shape, f32)
    for first in range(0, count, UNITS):
        lanes = slice(first, min(first + UNITS, count))
        act, slope = gelu_pair(dot(xs, up_ref[:, lanes]))
        act = act.astype(bf)
        d_pre = (slope * dot(ds, down_ref[:, lanes])).astype(bf)
        out = out + dot(act, down_ref[:, lanes], NT)
        dx = dx + dot(d_pre, up_ref[:, lanes], NT)
        g_up_ref[:, lanes] += dot(xs, d_pre, TN)
        g_down_ref[:, lanes] += dot(ds, act, TN)
    return out, dx


def start_all(copies):
    copies = [pltpu.make_async_copy(*copy) for copy in copies]
    for copy in copies:
        copy.start()
    return copies


def wait_all(copies):
    for copy in copies:
        copy.wait()


def routed_kernel(ids, *refs):
    hidden, d_mix, metas, priors = refs[0:4], refs[4:8], refs[8:12], refs[12:16]
    gathered, mix_out, dx_out, d_gate_out = refs[16], refs[17:21], refs[21:25], refs[25]
    g_send, g_keep, g_second, g_third = refs[26:30]
    tok, meta, up, down, g_up, g_down, acc, part, d_gate, stage = refs[30:40]
    tok_sem, w_sem, out_sem, g_sem = refs[40:]
    n, x = ids[0], ids[2]
    loads = []
    for w in range(8):
        for e in range(2):
            for k in range(4):
                where = (e, pl.ds(48 * w, 48), pl.ds(k * D, D))
                loads.append((gathered.at[w, k, 2 * e], up.at[where], w_sem.at[0]))
                loads.append((gathered.at[w, k, 2 * e + 1], down.at[where], w_sem.at[0]))
    token_loads = []
    for i in range(4):
        token_loads.append((hidden[i], tok.at[i, :, pl.ds(0, D)], tok_sem.at[i, 0]))
        token_loads.append((d_mix[i], tok.at[i, :, pl.ds(D, D)], tok_sem.at[i, 1]))
        token_loads.append((metas[i], meta.at[i], tok_sem.at[i, 2]))
        token_loads.append((priors[i], part.at[i], tok_sem.at[i, 3]))
    loads = start_all(loads)
    tokens = start_all(token_loads)
    g_up[...] = jnp.zeros_like(g_up)
    g_down[...] = jnp.zeros_like(g_down)
    wait_all(loads)
    wait_all(tokens)

    def one_source(s, carry):
        acc[...] = part[s].astype(f32)

        def routed(e, carry):
            place = meta[s, pl.ds(2 * n + e, 1), :]
            gate = meta[s, pl.ds(8 + 2 * n + e, 1), :]
            slot = lax.broadcasted_iota(jnp.int32, (CAP, TOK), 0).astype(f32)
            hit = slot == place
            hot = hit.astype(f32).astype(bf)
            gates = jnp.sum(jnp.where(hit, gate, 0.0), axis=1, keepdims=True)
            rows = dot(hot, tok[s])
            d_rows = rows[:, D:]
            xs, ds = rows[:, :D].astype(bf), (d_rows * gates).astype(bf)
            out, dx = units(xs, ds, up.at[e], down.at[e], g_up.at[e], g_down.at[e], FF)
            d_slot = jnp.sum(out * d_rows, axis=1, keepdims=True)
            d_gate[s, pl.ds(e, 1), :] = jnp.sum(
                jnp.where(hit, d_slot, 0.0), axis=0, keepdims=True
            )
            both = jnp.concatenate([(out * gates).astype(bf), dx.astype(bf)], axis=1)
            acc[...] += dot(hot, both, TN)
            return carry

        lax.fori_loop(0, 2, routed, 0)
        part[s] = acc[...].astype(bf)
        return carry

    lax.fori_loop(0, 4, one_source, 0)
    outs = start_all(
        [(part.at[i, :, pl.ds(0, D)], mix_out[i], out_sem.at[i]) for i in range(4)]
        + [(part.at[i, :, pl.ds(D, D)], dx_out[i], out_sem.at[5 + i]) for i in range(4)]
        + [(d_gate, d_gate_out, out_sem.at[4])]
    )
    for e in range(2):
        stage[2 * e] = g_up[e].astype(bf)
        stage[2 * e + 1] = g_down[e].astype(bf)

    @pl.when(x == 0)
    def _():
        wait_all(
            start_all([(stage.at[0], g_keep, g_sem.at[0]), (stage.at[3], g_send, g_sem.at[1])])
        )

    @pl.when(x != 0)
    def _():
        wait_all(
            start_all([(stage.at[3], g_keep, g_sem.at[0]), (stage.at[0], g_send, g_sem.at[1])])
        )

    outs += start_all(
        [(stage.at[1], g_second, g_sem.at[2]), (stage.at[2], g_third, g_sem.at[3])]
    )
    wait_all(outs)


def shared_kernel(*refs):
    hidden, d_mix, gathered, part_out, g_out = refs[0:4], refs[4:8], refs[8], refs[9:13], refs[13]
    tok, up, down, g_up, g_down, part, stage, tok_sem, w_sem, out_sem = refs[14:]
    loads = []
    for w in range(8):
        for s in range(2):
            where = (pl.ds(48 * w, 48), pl.ds(s * D, D))
            loads.append((gathered.at[w, 4, 2 * s], up.at[where], w_sem.at[0]))
            loads.append((gathered.at[w, 4, 2 * s + 1], down.at[where], w_sem.at[0]))
    loads = start_all(loads)
    token_loads = []
    for i in range(4):
        token_loads.append((hidden[i], tok.at[i, :, pl.ds(0, D)], tok_sem.at[i, 0]))
        token_loads.append((d_mix[i], tok.at[i, :, pl.ds(D, D)], tok_sem.at[i, 1]))
    tokens = start_all(token_loads)
    g_up[...] = jnp.zeros_like(g_up)
    g_down[...] = jnp.zeros_like(g_down)
    wait_all(loads)
    outs = []
    for i in range(4):
        wait_all(tokens[2 * i : 2 * i + 2])

        def some_rows(r, carry, i=i):
            rows = pl.ds(pl.multiple_of(r * ROWS, ROWS), ROWS)
            out, dx = units(tok[i, rows, :D], tok[i, rows, D:], up, down, g_up, g_down, 2 * D)
            part[i, rows, :D] = out.astype(bf)
            part[i, rows, D:] = dx.astype(bf)
            return carry

        lax.fori_loop(0, TOK // ROWS, some_rows, 0)
        outs += start_all([(part.at[i], part_out[i], out_sem.at[i])])
    for s in range(2):
        stage[:, 2 * s * D : 2 * s * D + D] = g_up[:, s * D : s * D + D].astype(bf)
        stage[:, 2 * s * D + D : 2 * s * D + 2 * D] = g_down[:, s * D : s * D + D].astype(bf)
    wait_all(outs + start_all([(stage, g_out, w_sem.at[1])]))


def routed_experts(ids, hidden, d_mix, metas, priors, gathered):
    anyspec = pl.BlockSpec(memory_space=pl.ANY)
    hbm = pl.BlockSpec(memory_space=pltpu.HBM)
    whole = jax.ShapeDtypeStruct((D, FF), bf)
    shapes = [jax.ShapeDtypeStruct((TOK, D), bf)] * 8
    shapes += [jax.ShapeDtypeStruct((4, 8, TOK), f32)] + [whole] * 4
    return pl.pallas_call(
        routed_kernel,
        out_shape=shapes,
        in_specs=[pl.BlockSpec(memory_space=pltpu.SMEM)] + [anyspec] * 17,
        out_specs=[hbm] * len(shapes),
        scratch_shapes=[
            pltpu.VMEM((4, TOK, 2 * D), bf),
            pltpu.VMEM((4, 16, TOK), f32),
            pltpu.VMEM((2, D, FF), bf),
            pltpu.VMEM((2, D, FF), bf),
            pltpu.VMEM((2, D, FF), f32),
            pltpu.VMEM((2, D, FF), f32),
            pltpu.VMEM((TOK, 2 * D), f32),
            pltpu.VMEM((4, TOK, 2 * D), bf),
            pltpu.VMEM((4, 8, TOK), f32),
            pltpu.VMEM((4, D, FF), bf),
            pltpu.SemaphoreType.DMA((4, 4)),
            pltpu.SemaphoreType.DMA((1,)),
            pltpu.SemaphoreType.DMA((9,)),
            pltpu.SemaphoreType.DMA((4,)),
        ],
        compiler_params=pltpu.CompilerParams(vmem_limit_bytes=58 * 1024 * 1024),
        name="routed_experts",
    )(ids, *hidden, *d_mix, *metas, *priors, gathered)


def shared_units(hidden, d_mix, gathered):
    anyspec = pl.BlockSpec(memory_space=pl.ANY)
    hbm = pl.BlockSpec(memory_space=pltpu.HBM)
    shapes = [jax.ShapeDtypeStruct((TOK, 2 * D), bf)] * 4 + [jax.ShapeDtypeStruct((D, FF), bf)]
    return pl.pallas_call(
        shared_kernel,
        out_shape=shapes,
        in_specs=[anyspec] * 9,
        out_specs=[hbm] * 5,
        scratch_shapes=[
            pltpu.VMEM((4, TOK, 2 * D), bf),
            pltpu.VMEM((D, 2 * D), bf),
            pltpu.VMEM((D, 2 * D), bf),
            pltpu.VMEM((D, 2 * D), f32),
            pltpu.VMEM((D, 2 * D), f32),
            pltpu.VMEM((4, TOK, 2 * D), bf),
            pltpu.VMEM((D, FF), bf),
            pltpu.SemaphoreType.DMA((4, 2)),
            pltpu.SemaphoreType.DMA((2,)),
            pltpu.SemaphoreType.DMA((4,)),
        ],
        compiler_params=pltpu.CompilerParams(vmem_limit_bytes=58 * 1024 * 1024),
        name="shared_units",
    )(*hidden, *d_mix, gathered)


def head_only(block, head):
    lane = lax.broadcasted_iota(jnp.int32, block.shape, 1)
    return jnp.where((lane >= 64) == (head == 1), block, jnp.zeros_like(block))


def attend_kernel(res, q_ref, k_ref, v_ref, o_ref, lse_ref, vt_ref):
    qb = pl.program_id(1)

    @pl.when(qb == 0)
    def _():
        vt_ref[...] = v_ref[...].T

    def work(rows):
        q = q_ref[...] * 0.125
        outs = []
        for head in range(2):
            scores = dot(k_ref[rows, :], head_only(q, head), NT)
            top = jnp.max(scores, axis=0, keepdims=True)
            expo = jnp.exp(scores - top)
            total = jnp.sum(expo, axis=0, keepdims=True)
            weights = (expo * (1.0 / total)).astype(bf)
            outs.append(dot(vt_ref[head * 64 : head * 64 + 64, rows], weights))
            lse_ref[0, head : head + 1, :] = top + jnp.log(total)
        o_ref[...] = jnp.concatenate(outs, axis=0).T.astype(bf)

    @pl.when(res[0] == 1)
    def _():
        work(pl.ds(0, TOK))

    @pl.when(res[0] != 1)
    def _():
        work(pl.ds(pl.multiple_of(qb * 256, 256), 256))


def attend_fast(resolution, projected):
    return pl.pallas_call(
        attend_kernel,
        grid_spec=pltpu.PrefetchScalarGridSpec(
            num_scalar_prefetch=1,
            grid=(3, 4),
            in_specs=[
                pl.BlockSpec((256, 128), lambda h, i, r: (i, h)),
                pl.BlockSpec((TOK, 128), lambda h, i, r: (0, 3 + h)),
                pl.BlockSpec((TOK, 128), lambda h, i, r: (0, 6 + h)),
            ],
            out_specs=[
                pl.BlockSpec((256, 128), lambda h, i, r: (i, h)),
                pl.BlockSpec((1, 8, 256), lambda h, i, r: (h, 0, i)),
            ],
            scratch_shapes=[pltpu.VMEM((128, TOK), bf)],
        ),
        out_shape=(
            jax.ShapeDtypeStruct((TOK, D), bf),
            jax.ShapeDtypeStruct((3, 8, TOK), f32),
        ),
        compiler_params=pltpu.CompilerParams(vmem_limit_bytes=48 * 1024 * 1024),
        name="attend_fast",
    )(resolution, projected, projected, projected)


def attend_back_kernel(
    res, q_ref, k_ref, v_ref, do_ref, lse_ref, dq_ref, dk_ref, dv_ref, kt_ref, dk_acc, dv_acc
):
    qb = pl.program_id(1)

    @pl.when(qb == 0)
    def _():
        kt_ref[...] = k_ref[...].T

    def work(rows, whole):
        q = q_ref[...] * 0.125
        grads = []
        dk = dv = None
        for head in range(2):
            qh = head_only(q, head)
            doh = head_only(do_ref[...], head)
            scores = dot(k_ref[rows, :], qh, NT)
            probs = jnp.exp(scores - lse_ref[0, head : head + 1, :])
            d_weights = dot(v_ref[rows, :], doh, NT)
            delta = jnp.sum(d_weights * probs, axis=0, keepdims=True)
            d_scores = (probs * (d_weights - delta)).astype(bf)
            dv_one = dot(probs.astype(bf), doh)
            dk_one = dot(d_scores, qh)
            dv = dv_one if dv is None else dv + dv_one
            dk = dk_one if dk is None else dk + dk_one
            grads.append(dot(kt_ref[head * 64 : head * 64 + 64, rows], d_scores))
        dq_ref[...] = (jnp.concatenate(grads, axis=0).T * 0.125).astype(bf)
        if not whole:
            dk_ref[rows, :] = dk.astype(bf)
            dv_ref[rows, :] = dv.astype(bf)
            return

        @pl.when(qb == 0)
        def _():
            dk_acc[...] = dk
            dv_acc[...] = dv

        @pl.when(qb != 0)
        def _():
            dk_acc[...] += dk
            dv_acc[...] += dv

        @pl.when(qb == 3)
        def _():
            dk_ref[...] = dk_acc[...].astype(bf)
            dv_ref[...] = dv_acc[...].astype(bf)

    @pl.when(res[0] == 1)
    def _():
        work(pl.ds(0, TOK), True)

    @pl.when(res[0] != 1)
    def _():
        work(pl.ds(pl.multiple_of(qb * 256, 256), 256), False)


def attend_back_fast(resolution, projected, lse, d_attended):
    return pl.pallas_call(
        attend_back_kernel,
        grid_spec=pltpu.PrefetchScalarGridSpec(
            num_scalar_prefetch=1,
            grid=(3, 4),
            in_specs=[
                pl.BlockSpec((256, 128), lambda h, i, r: (i, h)),
                pl.BlockSpec((TOK, 128), lambda h, i, r: (0, 3 + h)),
                pl.BlockSpec((TOK, 128), lambda h, i, r: (0, 6 + h)),
                pl.BlockSpec((256, 128), lambda h, i, r: (i, h)),
                pl.BlockSpec((1, 8, 256), lambda h, i, r: (h, 0, i)),
            ],
            out_specs=[
                pl.BlockSpec((256, 128), lambda h, i, r: (i, h)),
                pl.BlockSpec((TOK, 128), lambda h, i, r: (0, h)),
                pl.BlockSpec((TOK, 128), lambda h, i, r: (0, h)),
            ],
            scratch_shapes=[
                pltpu.VMEM((128, TOK), bf),
                pltpu.VMEM((TOK, 128), f32),
                pltpu.VMEM((TOK, 128), f32),
            ],
        ),
        out_shape=[jax.ShapeDtypeStruct((TOK, D), bf)] * 3,
        compiler_params=pltpu.CompilerParams(vmem_limit_bytes=48 * 1024 * 1024),
        name="attend_back_fast",
    )(resolution, projected, projected, projected, d_attended, lse)


def halves(value):
    high = value.astype(bf)
    return high, (value - high.astype(f32)).astype(bf)


def dot_three(a, b, dims=NN):
    return dot(a[0], b[0], dims) + dot(a[0], b[1], dims) + dot(a[1], b[0], dims)


def up_owner(e):
    return (24 if e % 2 else 0) + e // 2 if e < 8 else 20 + 2 * (e - 8)


def down_owner(e):
    return (4 if e % 2 else 16) + e // 2 if e < 8 else 21 + 2 * (e - 8)


def square_owner(j):
    return 8 + j if j < 3 else (9 + j if j < 7 else 21 + j)


OUT_OWNER, ROUTER_OWNER = 11, 30


def pack_kernel(square, out, router, up, down, packed):
    for e in range(10):
        packed[up_owner(e)] = up[e]
        packed[down_owner(e)] = down[e]
    rest = jnp.zeros((48, D - 96), f32)
    for j in range(9):
        packed[square_owner(j)] = jnp.concatenate([square[j], rest], axis=1)
    packed[OUT_OWNER] = jnp.concatenate([out[...], rest], axis=1)
    packed[ROUTER_OWNER] = router[...]
    packed[31] = jnp.zeros((48, D), f32)


def pack_owned(square, out, router, up, down):
    vmem = pl.BlockSpec(memory_space=pltpu.VMEM)
    return pl.pallas_call(
        pack_kernel,
        out_shape=jax.ShapeDtypeStruct((32, 48, D), f32),
        in_specs=[vmem] * 5,
        out_specs=vmem,
        name="pack_owned",
    )(square, out, router, up, down)


def owned_grad_kernel(ids, *refs):
    pieces = refs[:6]
    dense, small, extra, full_out, cut_out, buf, sems = refs[6:]
    n, z, x = ids[0], ids[1], ids[2]
    is_small = (z == 1) | ((z == 3) & (x == 1))
    for group, owner in enumerate((0, 2, 3)):

        @pl.when((z == owner) & jnp.logical_not(is_small))
        def _():
            copies = [
                pltpu.make_async_copy(pieces[2 * group + i], buf.at[i], sems.at[i])
                for i in range(2)
            ]
            for copy in copies:
                copy.start()
            for copy in copies:
                copy.wait()

    @pl.when(jnp.logical_not(is_small))
    def _():
        for k in range(4):
            lanes = slice(k * D, k * D + D)
            full_out[k] = buf[0, :, lanes].astype(f32) + buf[1, :, lanes].astype(f32)

    @pl.when(is_small)
    def _():
        rows = small[...].reshape(32, 8, 512)

        def place(matrix, width):
            rest = jnp.zeros((D, D - width), f32)
            for m in range(4):
                part = matrix[:, m * width : m * width + width]
                full_out[m ^ n] = jnp.concatenate([part, rest], axis=1)

        @pl.when(z == 1)
        def _():
            @pl.when(x == 0)
            def _():
                place(dense[...], 96)

        @pl.when(jnp.logical_not((z == 1) & (x == 0)))
        def _():
            is_router = (z == 3) & (n == 2)

            @pl.when(is_router)
            def _():
                summed = jnp.sum(rows[:, :, :D], axis=0)
                place(jnp.concatenate([summed, jnp.zeros((120, D), f32)], axis=0).T[:, :8], 2)

            @pl.when(jnp.logical_not(is_router))
            def _():
                first = (lax.broadcasted_iota(jnp.int32, (256, D), 0) % 8) < 4
                both = small[:, :D]
                mods = jnp.where(first, both, 0.0)
                conds = pltpu.roll(both, 252, 0)
                conds = jnp.where(first, conds, 0.0)
                place(dot_three(halves(mods), halves(conds), TN), 96)

    for w in range(8):
        for m in range(4):
            cut_out[4 * w + m, :48] = full_out[m ^ n, 48 * w : 48 * w + 48, :].astype(bf)
            cut_out[4 * w + m, 48:] = extra[...]


def owned_grad(ids, pieces, dense, small, extra):
    anyspec, vmem = pl.BlockSpec(memory_space=pltpu.HBM), pl.BlockSpec(memory_space=pltpu.VMEM)
    return pl.pallas_call(
        owned_grad_kernel,
        out_shape=(
            jax.ShapeDtypeStruct((4, D, D), f32),
            jax.ShapeDtypeStruct((32, 56, D), bf),
        ),
        in_specs=[pl.BlockSpec(memory_space=pltpu.SMEM)] + [anyspec] * 6 + [vmem] * 3,
        out_specs=[vmem, vmem],
        scratch_shapes=[pltpu.VMEM((2, D, FF), bf), pltpu.SemaphoreType.DMA((2,))],
        compiler_params=pltpu.CompilerParams(vmem_limit_bytes=40 * 1024 * 1024),
        name="owned_grad",
    )(ids, *pieces, dense, small, extra)


def ortho_kernel(ids, grad, moment, cut_out, cur, high, low, cross):
    n = ids[0]
    for k in range(4):
        cur[k] = grad[k]
    for w in range(8):
        rows = slice(48 * w, 48 * w + 48)
        for m in range(4):
            cur[m ^ n, rows, :] += MOMENTUM * moment[4 * w + m]
    total = jnp.zeros((1, D), f32)
    for k in range(4):
        total = total + jnp.sum(cur[k] * cur[k], axis=0, keepdims=True)
    factor = 1.0 / (jnp.sqrt(jnp.sum(total, axis=1, keepdims=True)) + 1e-07)

    def keep(k, value):
        cur[k] = value
        high[:, k * D : k * D + D], low[:, k * D : k * D + D] = halves(value)

    for k in range(4):
        keep(k, cur[k] * factor)

    def sweep(_, carry):
        cross[...] = dot(high[...], low[...], NT)
        gram = dot(high[...], high[...], NT) + (cross[...] + cross[...].T)
        gram_high, gram_low = halves(gram)
        cross[...] = dot(gram_high, gram_low)
        square = dot(gram_high, gram_high) + (cross[...] + cross[...].T)
        poly = halves(NS_SECOND * gram + NS_THIRD * square)
        for k in range(4):
            lanes = slice(k * D, k * D + D)
            step = dot_three(poly, (high[:, lanes], low[:, lanes]))
            keep(k, NS_FIRST * cur[k] + step)
        return carry

    lax.fori_loop(0, 5, sweep, 0)
    for w in range(8):
        for m in range(4):
            cut_out[4 * w + m] = cur[m ^ n, 48 * w : 48 * w + 48, :].astype(bf)


def ortho_owned(ids, grad, moment):
    vmem = pl.BlockSpec(memory_space=pltpu.VMEM)
    return pl.pallas_call(
        ortho_kernel,
        out_shape=jax.ShapeDtypeStruct((32, 48, D), bf),
        in_specs=[pl.BlockSpec(memory_space=pltpu.SMEM), vmem, vmem],
        out_specs=vmem,
        scratch_shapes=[
            pltpu.VMEM((4, D, D), f32),
            pltpu.VMEM((D, FF), bf),
            pltpu.VMEM((D, FF), bf),
            pltpu.VMEM((D, D), f32),
        ],
        compiler_params=pltpu.CompilerParams(vmem_limit_bytes=40 * 1024 * 1024),
        name="ortho_owned",
    )(ids, grad, moment)


def update_kernel(decay_ref, grads, orthos, *refs):
    decay = decay_ref[0]
    weights, moments, emas = refs[0:5], refs[5:10], refs[10:15]
    states, masters, averages = refs[15:20], refs[20:25], refs[25:30]
    small_rate, large_rate = RATE * 0.2 * D**0.5, RATE * 0.2 * FF**0.5

    def step(which, at, grad, ortho, rate):
        states[which][at] = MOMENTUM * moments[which][at] + grad.astype(f32)
        master = weights[which][at] - rate * ortho.astype(f32)
        masters[which][at] = master
        averages[which][at] = decay * emas[which][at] + (1.0 - decay) * master

    for j in range(9):
        own = square_owner(j)
        step(0, j, grads[own, :48, :96], orthos[own, :48, :96], small_rate)
    step(1, slice(None), grads[OUT_OWNER, :48, :96], orthos[OUT_OWNER, :48, :96], small_rate)

    def router_rows(source):
        return source[ROUTER_OWNER, :48, :128].astype(f32).T[:2]

    step(2, slice(None), router_rows(grads), router_rows(orthos), small_rate)
    for e in range(10):
        step(3, e, grads[up_owner(e), :48], orthos[up_owner(e), :48], large_rate)
        step(4, e, grads[down_owner(e), :48], orthos[down_owner(e), :48], large_rate)


def update(decay, grads, orthos, weights, moments, emas):
    vmem = pl.BlockSpec(memory_space=pltpu.VMEM)
    shapes = [jax.ShapeDtypeStruct(weight.shape, f32) for weight in weights]
    return pl.pallas_call(
        update_kernel,
        out_shape=shapes * 3,
        in_specs=[pl.BlockSpec(memory_space=pltpu.SMEM)] + [vmem] * 17,
        out_specs=[vmem] * 15,
        compiler_params=pltpu.CompilerParams(vmem_limit_bytes=48 * 1024 * 1024),
        name="update",
    )(decay, grads, orthos, *weights, *moments, *emas)


def first_back_kernel(
    ids, dq, dk, dv, hidden, tokens, d_mid, maps, scales, g_out, mods, cond, g_router, *refs
):
    grad_in, keep, out_send, payload, g_acc, sums = refs
    i = pl.program_id(0)
    heads = (dq, dk, dv)
    d_hidden = jnp.zeros((SHORT, D), f32)
    for j in range(3):
        d_hidden = d_hidden + dot(heads[j][...], maps[j * D : j * D + D, :])

    @pl.when(i == 0)
    def _():
        for j in range(3):
            g_acc[j] = dot(heads[j][...], hidden[...], TN)

    @pl.when(i != 0)
    def _():
        for j in range(3):
            g_acc[j] += dot(heads[j][...], hidden[...], TN)

    rows = tokens[...].astype(f32)
    center = rows - jnp.mean(rows, axis=1, keepdims=True)
    inverse = lax.rsqrt(jnp.mean(center * center, axis=1, keepdims=True) + EPSILON)
    normed = center * inverse
    d_normed = d_hidden * (1.0 + scales[pl.ds(i, 1), :])
    inner = d_normed - jnp.mean(d_normed, axis=1, keepdims=True)
    inner = inner - normed * jnp.mean(d_normed * normed, axis=1, keepdims=True)
    grad_in[...] = d_mid[...] + inverse * inner
    sums[0, pl.ds(i, 1), :] = jnp.sum(d_hidden, axis=0, keepdims=True)
    sums[1, pl.ds(i, 1), :] = jnp.sum(d_hidden * normed, axis=0, keepdims=True)

    @pl.when(i == 3)
    def _():
        c = lax.rem(ids[0], 2)
        for m in range(4):

            def total(m=m):
                return g_acc[m] if m < 3 else g_out[...]

            @pl.when(c == m % 2)
            def _():
                keep[m // 2] = total()

            @pl.when(c != m % 2)
            def _():
                out_send[m // 2] = total().astype(bf)

        rows = [sums[0, :4, :], sums[1, :4, :]] + [mods[j] for j in range(4)]
        payload[...] = jnp.zeros_like(payload)
        for j, slot in enumerate((12, 13, 14, 15, 28, 29)):
            payload[slot, :4, :D] = rows[j]
            payload[slot, 4:, :D] = cond[...]
        payload[30, :, :D] = g_router[...]
        bias = jnp.concatenate([jnp.sum(row, axis=0, keepdims=True) for row in rows], axis=1)
        for slot in range(32):
            payload[slot, 0:1, D : D + 72] = bias[:, slot * 72 : slot * 72 + 72]


def first_back_fast(ids, d_heads, hidden, tokens, d_mid, maps, scales, g_out, mods, cond, g_router):
    block = pl.BlockSpec((SHORT, D), lambda i: (i, 0))

    def whole(*shape):
        return pl.BlockSpec(shape, lambda i: (0,) * len(shape))

    return pl.pallas_call(
        first_back_kernel,
        grid=(4,),
        out_shape=(
            jax.ShapeDtypeStruct((TOK, D), f32),
            jax.ShapeDtypeStruct((2, D, D), f32),
            jax.ShapeDtypeStruct((2, D, D), bf),
            jax.ShapeDtypeStruct((32, 8, 512), f32),
        ),
        in_specs=[pl.BlockSpec(memory_space=pltpu.SMEM)]
        + [block] * 6
        + [
            whole(3 * D, D),
            whole(4, D),
            whole(D, D),
            whole(4, 4, D),
            whole(4, D),
            whole(8, D),
        ],
        out_specs=[block, whole(2, D, D), whole(2, D, D), whole(32, 8, 512)],
        scratch_shapes=[pltpu.VMEM((3, D, D), f32), pltpu.VMEM((2, 8, D), f32)],
        compiler_params=pltpu.CompilerParams(vmem_limit_bytes=40 * 1024 * 1024),
        name="first_back",
    )(ids, *d_heads, hidden, tokens, d_mid, maps, scales, g_out, mods, cond, g_router)


AXES = (WIDE, NARROW)


def route_pairs(move):
    pairs = []
    for index in range(32):
        w, n = divmod(index, 4)
        target = move(w // 2, w % 2, n // 2, n % 2)
        if target is not None:
            z, x, y, c = target
            pairs.append((index, (z * 2 + x) * 4 + y * 2 + c))
    return pairs


def send(array, move):
    return lax.ppermute(array, AXES, route_pairs(move))


def to_core(z, x, y, c):
    return (z, x, y, 1 - c)


def to_y(z, x, y, c):
    return (z, x, 1 - y, c)


def to_diag(z, x, y, c):
    return (z, x, 1 - y, 1 - c)


def to_x(z, x, y, c):
    return (z, 1 - x, y, c)


def to_z(step):
    return lambda z, x, y, c: ((z + step) % 4, x, y, c)


NARROW_MOVES = (None, to_core, to_y, to_diag)


def pick(array, index, axis=0):
    return lax.dynamic_index_in_dim(array, index, axis, keepdims=False)


def in_order(mine, other, flag):
    return jnp.where(flag == 0, mine, other), jnp.where(flag == 0, other, mine)


def xor_blocks(array, axis, y, c):
    parts = [lax.index_in_dim(array, i, axis, keepdims=True) for i in range(4)]
    parts = [jnp.where(c == 0, parts[i], parts[i ^ 1]) for i in range(4)]
    parts = [jnp.where(y == 0, parts[i], parts[i ^ 2]) for i in range(4)]
    return jnp.concatenate(parts, axis=axis)


def gather_rows(rows, z, x, c):
    pieces = [send(rows, to_z(step)) for step in (3, 2, 1)] + [rows]
    pieces = [pieces[2], pieces[1], pieces[0]]
    recv = {step: send_piece for step, send_piece in zip((1, 2, 3), pieces)}
    ring = jnp.stack([recv[3], recv[2], recv[1], rows])
    doubled = jnp.concatenate([ring, ring])
    by_z = lax.dynamic_slice_in_dim(doubled, (3 - z) % 4, 4, 0)
    by_zx = jnp.stack(in_order(by_z, send(by_z, to_x), x), axis=1)
    return jnp.stack(in_order(by_zx, send(by_zx, to_core), c), axis=2)


def lanes_to(block, width):
    return jnp.pad(block, [(0, 0)] * (block.ndim - 1) + [(0, width - block.shape[-1])])


def turned(array):
    return jnp.swapaxes(array, -1, -2)


def fast_device(
    tokens,
    conditions,
    routes,
    resolution,
    step_count,
    cotangent,
    w_square,
    w_out,
    w_router,
    w_up,
    w_down,
    b_ada,
    moment_square,
    moment_out,
    moment_router,
    moment_up,
    moment_down,
    moment_bias,
    ema_square,
    ema_out,
    ema_router,
    ema_up,
    ema_down,
    ema_bias,
):
    wide = lax.axis_index(WIDE)
    narrow = lax.axis_index(NARROW)
    z, x = wide // 2, wide % 2
    y, c = narrow // 2, narrow % 2

    square_t = turned(w_square).astype(bf)
    out_t = turned(w_out).astype(bf)[None]
    misc = jnp.concatenate(
        [
            lanes_to(b_ada.astype(bf)[None], 96),
            lanes_to(w_router.astype(bf), 96),
            jnp.zeros((5, 96), bf),
        ]
    )
    flat = jnp.concatenate(
        [
            square_t[:5].reshape(-1, 96),
            misc,
            square_t[5:].reshape(-1, 96),
            out_t.reshape(-1, 96),
        ]
    )
    lanes = jnp.stack([flat] + [send(flat, move) for move in NARROW_MOVES[1:]])
    rows = jnp.concatenate(list(xor_blocks(lanes, 0, y, c)), axis=1)

    moment_parts = (
        turned(moment_square),
        turned(moment_out),
        moment_router,
        turned(moment_up),
        turned(moment_down),
    )
    router_block = lanes_to(turned(moment_router), D)
    moments = pack_owned(*moment_parts[:2], router_block, *moment_parts[3:])

    def my_half(block):
        return pick(block.reshape(5, 2, 24, D), c, 1).reshape(120, D)

    first_rows = jnp.concatenate([my_half(rows[:240]), rows[240:248]])
    first_all = gather_rows(first_rows, z, x, c)
    first_all, moments = lax.optimization_barrier((first_all, moments))
    second_all = gather_rows(my_half(rows[248:]), z, x, c)

    def assemble(gathered):
        parts = gathered[..., :120, :].reshape(8, 2, 5, 24, D)
        return jnp.transpose(parts, (2, 0, 1, 3, 4)).reshape(5, D, D)

    first_maps = assemble(first_all)
    second_maps = assemble(second_all)
    misc_all = first_all[:, :, 0, 120:, :].reshape(8, 8, 4, 96)
    bias_low = misc_all[:, 0, :, :72].reshape(-1)
    router_low = jnp.transpose(misc_all[:, 1:3, :, :48], (2, 1, 0, 3)).reshape(ROUTED, D)

    up_t = turned(w_up).astype(bf)
    down_t = turned(w_down).astype(bf)
    routed_t = jnp.stack([up_t[:8], down_t[:8]], axis=1).reshape(4, 4, 48, D)
    shared_t = jnp.stack([up_t[8:], down_t[8:]], axis=1).reshape(4, 48, D)
    mine = [pick(routed_t, narrow)]
    mine += [send(pick(routed_t, narrow ^ k), NARROW_MOVES[k]) for k in (1, 2, 3)]
    gathered = lax.all_gather(jnp.stack(mine + [shared_t]), WIDE)

    res_group = resolution[0]
    token_f = tokens.astype(f32)
    segments = tokens.shape[0] // SHORT
    seg_ratio = LONG // SHORT
    first_seg = jnp.arange(segments, dtype=jnp.int32) // seg_ratio * seg_ratio
    chosen = jnp.where(res_group == 1, conditions[first_seg], conditions)
    cond_low = jax.nn.silu(chosen.astype(f32)).astype(bf)
    bias_rows = bias_low.astype(f32).reshape(6, D)

    def modulation_of(maps, bias):
        return dot(cond_low, maps.reshape(-1, D), NT).reshape(segments, -1, D) + bias

    first_two = modulation_of(first_maps[3:], bias_rows[:2])
    last_four = modulation_of(second_maps[:4], bias_rows[2:])
    out_map = second_maps[4]
    seg_rows = token_f.reshape(segments, SHORT, D)
    first_mod = modulate(seg_rows, first_two[:, 0:1], first_two[:, 1:2])
    hidden_one = first_mod.reshape(-1, D).astype(bf)
    query_maps = first_maps[:3].reshape(3 * D, D)
    projected = dot(hidden_one, query_maps, NT).astype(bf)
    gate_one, gate_two = last_four[:, 0:1], last_four[:, 3:4]
    grad_out = cotangent.astype(f32)
    grad_seg = grad_out.reshape(segments, SHORT, D)
    d_mixture = (grad_seg * gate_two).reshape(-1, D).astype(bf)
    d_mix_core = send(d_mixture, to_core)
    d_mix_y = send(d_mixture, to_y)
    attended, log_total = attend_fast(resolution, projected)
    attended, d_mix_y = lax.optimization_barrier((attended, d_mix_y))
    d_mix_diag = send(d_mix_y, to_core)
    attn_out = dot(attended, out_map, NT)
    mid_state = token_f + (attn_out.reshape(segments, SHORT, D) * gate_one).reshape(-1, D)
    second_mod, second_back = jax.vjp(
        modulate, mid_state.reshape(segments, SHORT, D), last_four[:, 1:2], last_four[:, 2:3]
    )
    hidden_two = second_mod.reshape(-1, D).astype(bf)

    logits = dot(router_low, hidden_two, NT)
    experts = jnp.arange(ROUTED, dtype=jnp.int32)[:, None]
    named = (routes[:, 0][None] == experts) | (routes[:, 1][None] == experts)
    index = jnp.arange(TOK, dtype=jnp.int32)
    earlier = (index[:, None] < index[None, :]).astype(bf)
    place = jnp.dot(named.astype(bf), earlier, preferred_element_type=f32)
    masked = jnp.where(named, logits, -jnp.inf)
    expo = jnp.where(named, jnp.exp(logits - jnp.max(masked, axis=0, keepdims=True)), 0.0)
    gates = expo / jnp.sum(expo, axis=0, keepdims=True)
    meta = jnp.concatenate([jnp.where(named, place, -1.0), gates])

    hidden_core, meta_core = send(hidden_two, to_core), send(meta, to_core)
    hidden_y, meta_y = send(hidden_two, to_y), send(meta, to_y)
    meta_diag = send(meta, to_diag)
    hidden_y, _ = lax.optimization_barrier((hidden_y, meta))
    hidden_diag = send(hidden_y, to_core)
    place_ids = jnp.stack([narrow, z, x]).astype(jnp.int32)
    hiddens = (hidden_two, hidden_core, hidden_y, hidden_diag)
    d_mixes = (d_mixture, d_mix_core, d_mix_y, d_mix_diag)
    metas = (meta, meta_core, meta_y, meta_diag)
    hiddens, d_mixes, metas, moments = lax.optimization_barrier((hiddens, d_mixes, metas, moments))
    moments = lax.all_to_all(moments, AXES, 0, 0, tiled=True)
    *priors, g_shared = shared_units(hiddens, d_mixes, gathered)

    def back_x(z_, x_, y_, c_):
        return (z_, 0, y_, c_) if x_ == 1 else None

    def forth_x(z_, x_, y_, c_):
        return (z_, 1, y_, c_) if x_ == 0 else None

    def along_z(hops, sides=(0, 1)):
        table = dict(hops)

        def move(z_, x_, y_, c_):
            return (table[z_], x_, y_, c_) if z_ in table and x_ in sides else None

        return move

    def added(kept, other):
        return (kept.astype(f32) + other.astype(f32)).astype(bf)

    def shared_part(k):
        return lax.dynamic_slice_in_dim(g_shared, (narrow ^ k) * D, D, 1)

    def over_core(parts):
        over = (parts[2].astype(f32) + send(parts[3], to_core).astype(f32)).astype(bf)
        return parts[0].astype(f32) + send(parts[1], to_core).astype(f32), over

    gate = lax.optimization_barrier
    shared_parts = [shared_part(0)]
    shared_parts += [send(shared_part(k), NARROW_MOVES[k]) for k in (1, 2, 3)]
    *routed_outs, d_gate_rows, g_send, g_keep, g_second, g_third = routed_experts(
        place_ids, hiddens, d_mixes, metas, priors, gathered
    )
    routed_outs, shared_parts, moments, d_gate_rows, g_send = gate(
        (routed_outs, shared_parts, moments, d_gate_rows, g_send)
    )
    pairs_one, pairs_two, pairs_three = ((3, 2), (1, 0)), ((0, 1), (3, 2)), ((0, 1), (2, 3))
    received_one = send(g_send, to_x)
    step_three = send(g_third, along_z(pairs_three))
    d_rows = [d_gate_rows[0, :2]]
    d_rows += [send(d_gate_rows[k, :2], NARROW_MOVES[k]) for k in (1, 2, 3)]
    own_hidden, over_hidden = over_core(routed_outs[4:])
    own_hidden, over_hidden, mix_outs, shared_parts, g_keep, g_second, d_rows = gate(
        (own_hidden, over_hidden, routed_outs[:4], shared_parts, g_keep, g_second, d_rows)
    )
    far_hidden = send(over_hidden, to_y)
    shared_grad = jnp.concatenate(shared_parts, axis=1)
    received_second = send(g_second, back_x)
    received_shared = send(shared_grad, forth_x)
    own_mix, over_mix = over_core(mix_outs)
    d_gates = xor_blocks(jnp.stack(d_rows), 0, y, c).reshape(ROUTED, TOK)
    far_hidden, own_mix, over_mix, received_one, step_three, shared_grad, d_gates = gate(
        (far_hidden, own_mix, over_mix, received_one, step_three, shared_grad, d_gates)
    )
    held_one = added(g_keep, received_one)
    held_three = added(g_third, step_three)
    d_hidden = own_hidden + far_hidden.astype(f32)

    d_logits = gates * (d_gates - jnp.sum(gates * d_gates, axis=0, keepdims=True))
    d_logits = d_logits.astype(bf)
    g_router = jnp.dot(d_logits, hidden_two, preferred_element_type=f32)
    d_hidden = d_hidden + dot(d_logits, router_low, TN)
    d_mid_norm, d_shift_two, d_scale_two = second_back(d_hidden.reshape(segments, SHORT, D))
    d_mid = grad_out + d_mid_norm.reshape(-1, D)
    d_mid_seg = d_mid.reshape(segments, SHORT, D)
    d_gate_one = jnp.sum(d_mid_seg * attn_out.reshape(segments, SHORT, D), axis=1)
    d_attn = (d_mid_seg * gate_one).reshape(-1, D).astype(bf)
    g_out = dot(d_attn, attended, TN)
    d_attended = jnp.dot(d_attn, out_map, preferred_element_type=f32).astype(bf)
    d_attended, held_one, held_three, over_mix = gate(
        (d_attended, held_one, held_three, over_mix)
    )
    step_one = send(held_one, along_z(pairs_one))
    last_three = send(held_three, along_z(((1, 3),)))
    far_mix = send(over_mix, to_y)
    d_heads = attend_back_fast(resolution, projected, log_total, d_attended)
    d_heads, step_one, last_three, received_second, received_shared, far_mix = gate(
        (d_heads, step_one, last_three, received_second, received_shared, far_mix)
    )
    held_two = added(
        jnp.where(x == 0, g_second, shared_grad), jnp.where(x == 0, received_second, received_shared)
    )
    held_one = added(held_one, step_one)
    held_three = added(held_three, last_three)
    d_heads, held_one, held_two, held_three = gate((d_heads, held_one, held_two, held_three))

    def cross_x(z_, x_, y_, c_):
        return (z_, 0, y_, c_) if x_ == 1 and z_ == 3 else None

    step_two = send(held_two, along_z(pairs_two))
    last_one = send(held_one, along_z(((2, 0),)))
    cross_three = send(held_three, cross_x)
    mixture = own_mix + far_mix.astype(f32)
    output = (
        mid_state + (mixture.reshape(segments, SHORT, D) * gate_two).reshape(-1, D)
    ).astype(bf)
    d_gate_two = jnp.sum(grad_seg * mixture.reshape(segments, SHORT, D), axis=1)
    mods = jnp.stack([d_gate_one, d_shift_two[:, 0], d_scale_two[:, 0], d_gate_two])
    grad_in, dense_keep, dense_send, small = first_back_fast(
        place_ids,
        d_heads,
        hidden_one,
        tokens,
        d_mid,
        query_maps,
        first_two[:, 1],
        g_out,
        mods,
        cond_low.astype(f32),
        g_router,
    )

    dense_recv = send(dense_send, to_core)
    small, dense_recv = gate((small, dense_recv))
    dense = dense_keep + dense_recv.astype(f32)
    dense_far = send(pick(dense, 1 - y).astype(bf), to_y)
    small = lax.all_to_all(small, AXES, 0, 0, tiled=True)
    g_bias = jnp.sum(small[:, 0, D : D + 72], axis=0)
    dense_far, step_two = gate((dense_far, step_two))
    held_two = added(held_two, step_two)
    last_two = send(held_two, along_z(((1, 2),)))
    dense = pick(dense, y) + dense_far.astype(f32)
    dense_side = send(dense.astype(bf), back_x)
    pieces = (held_one, last_one, held_two, last_two, held_three, cross_three)
    dense = dense + dense_side.astype(f32)
    dense_low = dense.astype(bf)
    for step in (1, 2, 3):

        def to_second(z_, x_, y_, c_, step=step):
            return (1, x_, y_, c_) if (z_ + step) % 4 == 1 and x_ == 0 else None

        dense = dense + send(dense_low, to_second).astype(f32)

    state_bias = MOMENTUM_VECTOR * moment_bias + g_bias
    part_sum = jnp.sum(state_bias * state_bias)
    sum_high = part_sum.astype(bf)
    sum_low = (part_sum - sum_high.astype(f32)).astype(bf)

    extra = jnp.pad(jnp.stack([sum_high, sum_low])[None], ((0, 7), (0, D - 2)))
    grad_full, grad_cut = owned_grad(place_ids, pieces, dense, small.reshape(256, 512), extra)
    grad_parts = lax.all_to_all(grad_cut, AXES, 0, 0, tiled=True)

    ortho_cut = ortho_owned(place_ids, grad_full, moments)
    ortho_cut, grad_parts = lax.optimization_barrier((ortho_cut, grad_parts))
    ortho_parts = lax.all_to_all(ortho_cut, AXES, 0, 0, tiled=True)
    square_total = jnp.sum(grad_parts[:, 48, :2].astype(f32))

    step_value = step_count[0].astype(f32)
    decay = jnp.minimum(0.9999, (1.0 + step_value) / (10.0 + step_value))
    masters = (turned(w_square), turned(w_out), w_router, turned(w_up), turned(w_down))
    emas = (turned(ema_square), turned(ema_out), ema_router, turned(ema_up), turned(ema_down))
    updated = update(decay[None], grad_parts, ortho_parts, masters, moment_parts, emas)
    results = []
    for which in range(5):
        results += [
            array if which == 2 else turned(array) for array in updated[which::5]
        ]
    root_mean = jnp.sqrt(square_total / (6 * D) + 1e-05)
    master_bias = b_ada - RATE_VECTOR * state_bias / root_mean
    average_bias = decay * ema_bias + (1.0 - decay) * master_bias
    return (output, grad_in, *results, state_bias, master_bias, average_bias)


def solution(mesh):
    placed = (
        P((WIDE, NARROW), None),
        P((WIDE, NARROW), None),
        P((WIDE, NARROW), None),
        P((WIDE, NARROW)),
        P(),
        P((WIDE, NARROW), None),
        P(None, NARROW, WIDE),
        P(NARROW, WIDE),
        P(NARROW, WIDE),
        P(None, NARROW, WIDE),
        P(None, NARROW, WIDE),
        P((WIDE, NARROW)),
        P(None, NARROW, WIDE),
        P(NARROW, WIDE),
        P(NARROW, WIDE),
        P(None, NARROW, WIDE),
        P(None, NARROW, WIDE),
        P((WIDE, NARROW)),
        P(None, NARROW, WIDE),
        P(NARROW, WIDE),
        P(NARROW, WIDE),
        P(None, NARROW, WIDE),
        P(None, NARROW, WIDE),
        P((WIDE, NARROW)),
    )
    device_body = fast_device if dict(mesh.shape) == {WIDE: 8, NARROW: 4} else on_device
    return jax.shard_map(
        device_body,
        mesh=mesh,
        in_specs=placed,
        out_specs=(
            P((WIDE, NARROW), None),
            P((WIDE, NARROW), None),
            P(None, NARROW, WIDE),
            P(None, NARROW, WIDE),
            P(None, NARROW, WIDE),
            P(NARROW, WIDE),
            P(NARROW, WIDE),
            P(NARROW, WIDE),
            P(NARROW, WIDE),
            P(NARROW, WIDE),
            P(NARROW, WIDE),
            P(None, NARROW, WIDE),
            P(None, NARROW, WIDE),
            P(None, NARROW, WIDE),
            P(None, NARROW, WIDE),
            P(None, NARROW, WIDE),
            P(None, NARROW, WIDE),
            P((WIDE, NARROW)),
            P((WIDE, NARROW)),
            P((WIDE, NARROW)),
        ),
        check_vma=False,
    )
```

```python
from functools import partial

import jax
import jax.numpy as jnp
from jax import lax
from jax.experimental import pallas as pl
from jax.experimental.pallas import tpu as pltpu
from jax.sharding import PartitionSpec as P

WIDE, NARROW = "wide", "narrow"
D = 384
HEADS = 6
HEAD = 64
FF = 1536
TOP = 2
ROUTED = 8
SHORT = 256
LONG = 1024
CAP = 384


PRECISE = lax.Precision.HIGHEST
EPSILON = 1e-06
NS_FIRST = 3.4445
NS_SECOND = -4.775
NS_THIRD = 2.0315
MOMENTUM = 0.95
MOMENTUM_VECTOR = 0.5
RATE = 0.25
RATE_VECTOR = 0.05


def as_sent(array):

    def short(part):
        return part.astype(jnp.bfloat16) if part.dtype == jnp.float32 else part

    return jax.tree.map(short, array)


def modulate(seg_rows, shift_by, scale_by):
    center = seg_rows - jnp.mean(seg_rows, axis=-1, keepdims=True)
    normed = center * lax.rsqrt(jnp.mean(center * center, axis=-1, keepdims=True) + EPSILON)
    return normed * (1.0 + scale_by) + shift_by


def gelu_tanh(values):
    return jax.nn.gelu(values, approximate=True)


def gelu_grad(pre_act, upstream):
    _, pull_back = jax.vjp(gelu_tanh, pre_act)
    return pull_back(upstream)[0]


def slot_table(route_rows):
    flat_routes = route_rows.reshape(-1)
    hot_table = (flat_routes[:, None] == jnp.arange(ROUTED, dtype=jnp.int32)[None, :]).astype(
        jnp.int32
    )
    earlier = jnp.cumsum(hot_table, axis=0, dtype=jnp.int32) - hot_table
    place_in = jnp.sum(earlier * hot_table, axis=1, dtype=jnp.int32)
    slot_ids = flat_routes * CAP + place_in
    sources = jnp.arange(slot_ids.shape[0], dtype=jnp.int32) // TOP
    slot_owner = jnp.zeros((ROUTED * CAP,), jnp.int32).at[slot_ids].set(sources)
    return (slot_ids, slot_owner)


def attend(projected, length):
    image_count = projected.shape[1] // length
    split_parts = projected.reshape(3, image_count, length, HEADS, HEAD)
    scores = jnp.einsum(
        "bqhe,bkhe->bhqk", split_parts[0], split_parts[1], preferred_element_type=jnp.float32
    ) * HEAD ** (-0.5)
    highest = jnp.max(scores, axis=-1, keepdims=True)
    expo = jnp.exp(scores - highest)
    totals = jnp.sum(expo, axis=-1, keepdims=True)
    weights_low = (expo / totals).astype(jnp.bfloat16)
    mixed_heads = jnp.einsum(
        "bhqk,bkhe->bqhe", weights_low, split_parts[2], preferred_element_type=jnp.float32
    )
    log_total = (highest + jnp.log(totals))[..., 0]
    return (
        mixed_heads.reshape(-1, D).astype(jnp.bfloat16),
        jnp.transpose(log_total, (0, 2, 1)).reshape(-1, HEADS),
    )


def attend_back(projected, log_total, d_attended, length):
    image_count = projected.shape[1] // length
    split_parts = projected.reshape(3, image_count, length, HEADS, HEAD)
    scale_qk = HEAD ** (-0.5)
    scores = (
        jnp.einsum(
            "bqhe,bkhe->bhqk", split_parts[0], split_parts[1], preferred_element_type=jnp.float32
        )
        * scale_qk
    )
    log_four = jnp.transpose(log_total.reshape(image_count, length, HEADS), (0, 2, 1))[..., None]
    probs = jnp.exp(scores - log_four)
    weights_low = probs.astype(jnp.bfloat16)
    d_heads = d_attended.reshape(image_count, length, HEADS, HEAD)
    d_weights = jnp.einsum(
        "bqhe,bkhe->bhqk", d_heads, split_parts[2], preferred_element_type=jnp.float32
    )
    d_values = jnp.einsum(
        "bhqk,bqhe->bkhe", weights_low, d_heads, preferred_element_type=jnp.float32
    )
    d_scores = (probs * (d_weights - jnp.sum(d_weights * probs, axis=-1, keepdims=True))).astype(
        jnp.bfloat16
    )
    d_queries = (
        jnp.einsum("bhqk,bkhe->bqhe", d_scores, split_parts[1], preferred_element_type=jnp.float32)
        * scale_qk
    )
    d_keys = (
        jnp.einsum("bhqk,bqhe->bkhe", d_scores, split_parts[0], preferred_element_type=jnp.float32)
        * scale_qk
    )
    return jnp.stack([d_queries, d_keys, d_values]).reshape(3, -1, D).astype(jnp.bfloat16)


def on_device(
    tokens,
    conditions,
    routes,
    resolution,
    step_count,
    cotangent,
    w_square,
    w_out,
    w_router,
    w_up,
    w_down,
    b_ada,
    moment_square,
    moment_out,
    moment_router,
    moment_up,
    moment_down,
    moment_bias,
    ema_square,
    ema_out,
    ema_router,
    ema_up,
    ema_down,
    ema_bias,
):
    bf_type = jnp.bfloat16
    fl_type = jnp.float32
    row_pieces = (
        lax.all_gather(w_square.astype(bf_type), NARROW, axis=1, tiled=True),
        lax.all_gather(w_out.astype(bf_type), NARROW, axis=0, tiled=True),
        lax.all_gather(w_router.astype(bf_type), NARROW, axis=0, tiled=True),
        lax.all_gather(w_up.astype(bf_type), NARROW, axis=1, tiled=True),
        lax.all_gather(w_down.astype(bf_type), NARROW, axis=1, tiled=True),
        lax.all_gather(b_ada.astype(bf_type), NARROW, axis=0, tiled=True),
    )
    whole_low = (
        lax.all_gather(row_pieces[0], WIDE, axis=2, tiled=True),
        lax.all_gather(row_pieces[1], WIDE, axis=1, tiled=True),
        lax.all_gather(row_pieces[2], WIDE, axis=1, tiled=True),
        lax.all_gather(row_pieces[3], WIDE, axis=2, tiled=True),
        lax.all_gather(row_pieces[4], WIDE, axis=2, tiled=True),
        lax.all_gather(row_pieces[5], WIDE, axis=0, tiled=True),
    )
    square_low, out_low, router_low, up_low, down_low, bias_low = whole_low
    res_group = resolution[0]
    token_f = tokens.astype(fl_type)
    segments = tokens.shape[0] // SHORT
    seg_ratio = LONG // SHORT
    first_seg = jnp.arange(segments, dtype=jnp.int32) // seg_ratio * seg_ratio
    chosen = jnp.where(res_group == 1, conditions[first_seg], conditions)
    cond_low = jax.nn.silu(chosen.astype(fl_type)).astype(bf_type)
    modulation = jnp.einsum(
        "sd,jde->sje", cond_low, square_low[3:], preferred_element_type=fl_type
    ) + bias_low.astype(fl_type).reshape(6, D)
    seg_rows = token_f.reshape(segments, SHORT, D)
    first_mod, first_back = jax.vjp(modulate, seg_rows, modulation[:, 0:1], modulation[:, 1:2])
    hidden_one = first_mod.reshape(-1, D).astype(bf_type)
    projected = jnp.einsum(
        "td,jde->jte", hidden_one, square_low[:3], preferred_element_type=fl_type
    ).astype(bf_type)
    attended, log_total = lax.cond(
        res_group == 1, partial(attend, length=LONG), partial(attend, length=SHORT), projected
    )
    attn_out = jnp.dot(attended, out_low, preferred_element_type=fl_type)
    mid_state = token_f + (attn_out.reshape(segments, SHORT, D) * modulation[:, 2:3]).reshape(-1, D)
    second_mod, second_back = jax.vjp(
        modulate, mid_state.reshape(segments, SHORT, D), modulation[:, 3:4], modulation[:, 4:5]
    )
    hidden_two = second_mod.reshape(-1, D).astype(bf_type)
    logits = jnp.einsum("td,rd->tr", hidden_two, router_low, preferred_element_type=fl_type)
    gate_probs = jax.nn.softmax(jnp.take_along_axis(logits, routes, axis=1), axis=1)
    slot_ids, slot_owner = slot_table(routes)
    inputs = hidden_two[slot_owner].reshape(ROUTED, CAP, D)
    pre_act = jnp.einsum("ecd,efd->ecf", inputs, up_low[:ROUTED], preferred_element_type=fl_type)
    act_low = gelu_tanh(pre_act).astype(bf_type)
    produced = jnp.einsum(
        "ecf,efd->ecd", act_low, down_low[:ROUTED], preferred_element_type=fl_type
    ).reshape(-1, D)
    chosen_out = produced[slot_ids].reshape(-1, TOP, D)
    routed = jnp.sum(chosen_out * gate_probs[:, :, None], axis=1)
    shared_pre = jnp.einsum(
        "td,sfd->stf", hidden_two, up_low[ROUTED:], preferred_element_type=fl_type
    )
    shared_act = gelu_tanh(shared_pre).astype(bf_type)
    shared_out = jnp.einsum(
        "stf,sfd->std", shared_act, down_low[ROUTED:], preferred_element_type=fl_type
    )
    mixture = routed + jnp.sum(shared_out, axis=0)
    output = (
        mid_state + (mixture.reshape(segments, SHORT, D) * modulation[:, 5:6]).reshape(-1, D)
    ).astype(bf_type)
    again_rows = (
        lax.all_gather(w_square.astype(bf_type), NARROW, axis=1, tiled=True),
        lax.all_gather(w_out.astype(bf_type), NARROW, axis=0, tiled=True),
        lax.all_gather(w_router.astype(bf_type), NARROW, axis=0, tiled=True),
        lax.all_gather(w_up.astype(bf_type), NARROW, axis=1, tiled=True),
        lax.all_gather(w_down.astype(bf_type), NARROW, axis=1, tiled=True),
    )
    again_whole = (
        lax.all_gather(again_rows[0], WIDE, axis=2, tiled=True),
        lax.all_gather(again_rows[1], WIDE, axis=1, tiled=True),
        lax.all_gather(again_rows[2], WIDE, axis=1, tiled=True),
        lax.all_gather(again_rows[3], WIDE, axis=2, tiled=True),
        lax.all_gather(again_rows[4], WIDE, axis=2, tiled=True),
    )
    square_low, out_low, router_low, up_low, down_low = again_whole
    grad_out = cotangent.astype(fl_type)
    grad_seg = grad_out.reshape(segments, SHORT, D)
    d_gate_two = jnp.sum(grad_seg * mixture.reshape(segments, SHORT, D), axis=1)
    d_mixture = (grad_seg * modulation[:, 5:6]).reshape(-1, D)
    d_shared = d_mixture.astype(bf_type)
    d_shared_act = jnp.einsum(
        "td,sfd->stf", d_shared, down_low[ROUTED:], preferred_element_type=fl_type
    )
    d_shared_pre = gelu_grad(shared_pre, d_shared_act).astype(bf_type)
    g_shared_down = jnp.einsum("stf,td->sfd", shared_act, d_shared, preferred_element_type=fl_type)
    g_shared_up = jnp.einsum(
        "stf,td->sfd", d_shared_pre, hidden_two, preferred_element_type=fl_type
    )
    d_hidden = jnp.einsum(
        "stf,sfd->td", d_shared_pre, up_low[ROUTED:], preferred_element_type=fl_type
    )
    d_gates = jnp.sum(d_mixture[:, None, :] * chosen_out, axis=2)
    gate_slot = jnp.zeros((ROUTED * CAP,), fl_type).at[slot_ids].set(gate_probs.reshape(-1))
    d_produced = (
        (gate_slot[:, None] * d_mixture[slot_owner]).astype(bf_type).reshape(ROUTED, CAP, D)
    )
    d_act = jnp.einsum(
        "ecd,efd->ecf", d_produced, down_low[:ROUTED], preferred_element_type=fl_type
    )
    d_pre = gelu_grad(pre_act, d_act).astype(bf_type)
    g_routed_down = jnp.einsum("ecf,ecd->efd", act_low, d_produced, preferred_element_type=fl_type)
    g_routed_up = jnp.einsum("ecf,ecd->efd", d_pre, inputs, preferred_element_type=fl_type)
    d_inputs = jnp.einsum(
        "ecf,efd->ecd", d_pre, up_low[:ROUTED], preferred_element_type=fl_type
    ).reshape(-1, D)
    d_hidden = d_hidden + jnp.sum(d_inputs[slot_ids].reshape(-1, TOP, D), axis=1)
    d_picked = gate_probs * (d_gates - jnp.sum(gate_probs * d_gates, axis=1, keepdims=True))
    route_hot = (routes[:, :, None] == jnp.arange(ROUTED, dtype=jnp.int32)[None, None, :]).astype(
        fl_type
    )
    d_logits = jnp.sum(route_hot * d_picked[:, :, None], axis=1).astype(bf_type)
    g_router = jnp.einsum("tr,td->rd", d_logits, hidden_two, preferred_element_type=fl_type)
    d_hidden = d_hidden + jnp.einsum(
        "tr,rd->td", d_logits, router_low, preferred_element_type=fl_type
    )
    d_mid_norm, d_shift_two, d_scale_two = second_back(d_hidden.reshape(segments, SHORT, D))
    d_mid = grad_out + d_mid_norm.reshape(-1, D)
    d_gate_one = jnp.sum(
        d_mid.reshape(segments, SHORT, D) * attn_out.reshape(segments, SHORT, D), axis=1
    )
    d_attn = (d_mid.reshape(segments, SHORT, D) * modulation[:, 2:3]).reshape(-1, D).astype(bf_type)
    g_out = jnp.einsum("td,te->de", attended, d_attn, preferred_element_type=fl_type)
    d_attended = jnp.einsum("te,de->td", d_attn, out_low, preferred_element_type=fl_type).astype(
        bf_type
    )
    d_projected = lax.cond(
        res_group == 1,
        partial(attend_back, length=LONG),
        partial(attend_back, length=SHORT),
        projected,
        log_total,
        d_attended,
    )
    g_qkv = jnp.einsum("td,jte->jde", hidden_one, d_projected, preferred_element_type=fl_type)
    d_hidden_one = jnp.einsum(
        "jte,jde->td", d_projected, square_low[:3], preferred_element_type=fl_type
    )
    d_rows, d_shift_one, d_scale_one = first_back(d_hidden_one.reshape(segments, SHORT, D))
    grad_in = d_mid + d_rows.reshape(-1, D)
    d_modulation = jnp.stack(
        [
            d_shift_one[:, 0],
            d_scale_one[:, 0],
            d_gate_one,
            d_shift_two[:, 0],
            d_scale_two[:, 0],
            d_gate_two,
        ],
        axis=1,
    )
    g_ada = jnp.einsum("sd,sje->jde", cond_low.astype(fl_type), d_modulation, precision=PRECISE)
    g_bias = jnp.sum(d_modulation, axis=0).reshape(-1)
    g_square = jnp.concatenate([g_qkv, g_ada], axis=0)
    g_up = jnp.concatenate([g_routed_up, g_shared_up], axis=0)
    g_down = jnp.concatenate([g_routed_down, g_shared_down], axis=0)
    by_columns = (
        lax.psum_scatter(g_square, WIDE, scatter_dimension=2, tiled=True),
        lax.psum_scatter(g_out, WIDE, scatter_dimension=1, tiled=True),
        lax.psum_scatter(g_router, WIDE, scatter_dimension=1, tiled=True),
        lax.psum_scatter(g_up, WIDE, scatter_dimension=2, tiled=True),
        lax.psum_scatter(g_down, WIDE, scatter_dimension=2, tiled=True),
        lax.psum_scatter(g_bias, WIDE, scatter_dimension=0, tiled=True),
    )
    summed = (
        lax.psum_scatter(by_columns[0], NARROW, scatter_dimension=1, tiled=True),
        lax.psum_scatter(by_columns[1], NARROW, scatter_dimension=0, tiled=True),
        lax.psum_scatter(by_columns[2], NARROW, scatter_dimension=0, tiled=True),
        lax.psum_scatter(by_columns[3], NARROW, scatter_dimension=1, tiled=True),
        lax.psum_scatter(by_columns[4], NARROW, scatter_dimension=1, tiled=True),
        lax.psum_scatter(by_columns[5], NARROW, scatter_dimension=0, tiled=True),
    )
    state_square = MOMENTUM * moment_square + summed[0]
    state_out = MOMENTUM * moment_out + summed[1]
    state_router = MOMENTUM * moment_router + summed[2]
    state_up = MOMENTUM * moment_up + summed[3]
    state_down = MOMENTUM * moment_down + summed[4]
    local_rows = w_up.shape[1]

    def padded(block):
        return jnp.pad(block, ((0, 0), (0, local_rows - block.shape[1]), (0, 0)))

    stacked = jnp.concatenate(
        [
            padded(state_square),
            padded(state_out[None]),
            padded(state_router[None]),
            state_up,
            state_down,
        ],
        axis=0,
    )
    wide_count = lax.axis_size(WIDE)
    matrices = stacked.shape[0]
    per_owner = -(-matrices // wide_count)
    stacked = jnp.pad(stacked, ((0, per_owner * wide_count - matrices), (0, 0), (0, 0)))
    current = lax.all_to_all(stacked, WIDE, split_axis=0, concat_axis=2, tiled=True)
    for sweep_num in range(5):
        gram_mat = lax.psum(
            jnp.einsum("mrc,mrd->mcd", current, current, precision=PRECISE).astype(jnp.bfloat16),
            NARROW,
        ).astype(jnp.float32)
        if sweep_num == 0:
            factor = 1.0 / (jnp.sqrt(jnp.trace(gram_mat, axis1=1, axis2=2)) + 1e-07)
            current = current * factor[:, None, None]
            gram_mat = gram_mat * (factor * factor)[:, None, None]
        polynomial = NS_SECOND * gram_mat + NS_THIRD * jnp.einsum(
            "mcd,mde->mce", gram_mat, gram_mat, precision=PRECISE
        )
        current = NS_FIRST * current + jnp.einsum(
            "mrc,mcd->mrd", current, polynomial, precision=PRECISE
        )
    spread_back = lax.all_to_all(
        as_sent(current), WIDE, split_axis=2, concat_axis=0, tiled=True
    ).astype(current.dtype)[:matrices]
    expert_total = w_up.shape[0]
    small_factor = RATE * 0.2 * D**0.5
    large_factor = RATE * 0.2 * FF**0.5
    master_square = w_square - small_factor * spread_back[0:9, : w_square.shape[1]]
    master_out = w_out - small_factor * spread_back[9, : w_out.shape[0]]
    master_router = w_router - small_factor * spread_back[10, : w_router.shape[0]]
    master_up = w_up - large_factor * spread_back[11 : 11 + expert_total]
    master_down = w_down - large_factor * spread_back[11 + expert_total : 11 + 2 * expert_total]
    state_bias = MOMENTUM_VECTOR * moment_bias + summed[5]
    square_total = lax.psum(jnp.sum(state_bias * state_bias), (WIDE, NARROW))
    root_mean = jnp.sqrt(square_total / (6 * D) + 1e-05)
    master_bias = b_ada - RATE_VECTOR * state_bias / root_mean
    step_value = step_count[0].astype(fl_type)
    decay = jnp.minimum(0.9999, (1.0 + step_value) / (10.0 + step_value))
    average_square = decay * ema_square + (1.0 - decay) * master_square
    average_out = decay * ema_out + (1.0 - decay) * master_out
    average_router = decay * ema_router + (1.0 - decay) * master_router
    average_up = decay * ema_up + (1.0 - decay) * master_up
    average_down = decay * ema_down + (1.0 - decay) * master_down
    average_bias = decay * ema_bias + (1.0 - decay) * master_bias
    return (
        output,
        grad_in,
        state_square,
        master_square,
        average_square,
        state_out,
        master_out,
        average_out,
        state_router,
        master_router,
        average_router,
        state_up,
        master_up,
        average_up,
        state_down,
        master_down,
        average_down,
        state_bias,
        master_bias,
        average_bias,
    )


bf = jnp.bfloat16
f32 = jnp.float32
TOK = 1024
UNITS = 768
NN = (((1,), (0,)), ((), ()))
NT = (((1,), (1,)), ((), ()))
TN = (((0,), (0,)), ((), ()))


def dot(a, b, dims=NN):
    return lax.dot_general(a, b, dims, preferred_element_type=f32)


def gelu_pair(pre):
    sq = pre * pre
    th = jnp.tanh(pre * (0.7978845608028654 + 0.035677408136300125 * sq))
    half = 0.5 * th + 0.5
    act = pre * half
    slope = half + act * (1.0 - half) * (1.5957691216057308 + 0.21406444881780075 * sq)
    return act, slope


def units(xs, ds, up_ref, down_ref, g_up_ref, g_down_ref, count):
    out = jnp.zeros(xs.shape, f32)
    dx = jnp.zeros(xs.shape, f32)
    for first in range(0, count, UNITS):
        lanes = slice(first, min(first + UNITS, count))
        act, slope = gelu_pair(dot(xs, up_ref[:, lanes]))
        act = act.astype(bf)
        d_pre = (slope * dot(ds, down_ref[:, lanes])).astype(bf)
        out = out + dot(act, down_ref[:, lanes], NT)
        dx = dx + dot(d_pre, up_ref[:, lanes], NT)
        g_up_ref[:, lanes] += dot(xs, d_pre, TN)
        g_down_ref[:, lanes] += dot(ds, act, TN)
    return out, dx


def start_all(copies):
    copies = [pltpu.make_async_copy(*copy) for copy in copies]
    for copy in copies:
        copy.start()
    return copies


def wait_all(copies):
    for copy in copies:
        copy.wait()


def routed_kernel(ids, *refs):
    hidden, d_mix, metas, priors = refs[0:4], refs[4:8], refs[8:12], refs[12:16]
    gathered, mix_out, dx_out, d_gate_out = refs[16], refs[17:21], refs[21:25], refs[25]
    g_send, g_keep, g_second, g_third = refs[26:30]
    tok, meta, up, down, g_up, g_down, acc, part, d_gate, stage = refs[30:40]
    tok_sem, w_sem, out_sem, g_sem = refs[40:]
    n, x = ids[0], ids[2]
    loads = []
    for w in range(8):
        for e in range(2):
            for k in range(4):
                where = (e, pl.ds(48 * w, 48), pl.ds(k * D, D))
                loads.append((gathered.at[w, k, 2 * e], up.at[where], w_sem.at[0]))
                loads.append((gathered.at[w, k, 2 * e + 1], down.at[where], w_sem.at[0]))
    token_loads = []
    for i in range(4):
        token_loads.append((hidden[i], tok.at[i, :, pl.ds(0, D)], tok_sem.at[i, 0]))
        token_loads.append((d_mix[i], tok.at[i, :, pl.ds(D, D)], tok_sem.at[i, 1]))
        token_loads.append((metas[i], meta.at[i], tok_sem.at[i, 2]))
        token_loads.append((priors[i], part.at[i], tok_sem.at[i, 3]))
    loads = start_all(loads)
    start_all(token_loads)
    g_up[...] = jnp.zeros_like(g_up)
    g_down[...] = jnp.zeros_like(g_down)
    wait_all(loads)

    def results(i):
        return [
            pltpu.make_async_copy(part.at[i, :, pl.ds(0, D)], mix_out[i], out_sem.at[i]),
            pltpu.make_async_copy(part.at[i, :, pl.ds(D, D)], dx_out[i], out_sem.at[5 + i]),
        ]

    def one_source(s, carry):
        pltpu.make_async_copy(hidden[0], tok.at[s, :, pl.ds(0, D)], tok_sem.at[s, 0]).wait()
        pltpu.make_async_copy(d_mix[0], tok.at[s, :, pl.ds(D, D)], tok_sem.at[s, 1]).wait()
        pltpu.make_async_copy(metas[0], meta.at[s], tok_sem.at[s, 2]).wait()
        pltpu.make_async_copy(priors[0], part.at[s], tok_sem.at[s, 3]).wait()
        acc[...] = part[s].astype(f32)

        def routed(e, carry):
            place = meta[s, pl.ds(2 * n + e, 1), :]
            gate = meta[s, pl.ds(8 + 2 * n + e, 1), :]
            slot = lax.broadcasted_iota(jnp.int32, (CAP, TOK), 0).astype(f32)
            hit = slot == place
            hot = hit.astype(f32).astype(bf)
            gates = jnp.sum(jnp.where(hit, gate, 0.0), axis=1, keepdims=True)
            rows = dot(hot, tok[s])
            d_rows = rows[:, D:]
            xs, ds = rows[:, :D].astype(bf), (d_rows * gates).astype(bf)
            out, dx = units(xs, ds, up.at[e], down.at[e], g_up.at[e], g_down.at[e], FF)
            d_slot = jnp.sum(out * d_rows, axis=1, keepdims=True)
            d_gate[s, pl.ds(e, 1), :] = jnp.sum(
                jnp.where(hit, d_slot, 0.0), axis=0, keepdims=True
            )
            both = jnp.concatenate([(out * gates).astype(bf), dx.astype(bf)], axis=1)
            acc[...] += dot(hot, both, TN)
            return carry

        lax.fori_loop(0, 2, routed, 0)
        part[s] = acc[...].astype(bf)
        for i in range(4):

            @pl.when(s == i)
            def _():
                for copy in results(i):
                    copy.start()

        return carry

    lax.fori_loop(0, 4, one_source, 0)
    outs = start_all([(d_gate, d_gate_out, out_sem.at[4])])
    for i in range(4):
        outs += results(i)
    for e in range(2):
        stage[2 * e] = g_up[e].astype(bf)
        stage[2 * e + 1] = g_down[e].astype(bf)

    @pl.when(x == 0)
    def _():
        wait_all(
            start_all([(stage.at[0], g_keep, g_sem.at[0]), (stage.at[3], g_send, g_sem.at[1])])
        )

    @pl.when(x != 0)
    def _():
        wait_all(
            start_all([(stage.at[3], g_keep, g_sem.at[0]), (stage.at[0], g_send, g_sem.at[1])])
        )

    outs += start_all(
        [(stage.at[1], g_second, g_sem.at[2]), (stage.at[2], g_third, g_sem.at[3])]
    )
    wait_all(outs)


def shared_kernel(*refs):
    hidden, d_mix, gathered, part_out, g_out = refs[0:4], refs[4:8], refs[8], refs[9:13], refs[13]
    tok, up, down, g_up, g_down, part, stage, tok_sem, w_sem, out_sem = refs[14:]
    loads = []
    for w in range(8):
        for s in range(2):
            where = (pl.ds(48 * w, 48), pl.ds(s * D, D))
            loads.append((gathered.at[w, 4, 2 * s], up.at[where], w_sem.at[0]))
            loads.append((gathered.at[w, 4, 2 * s + 1], down.at[where], w_sem.at[0]))
    loads = start_all(loads)
    token_loads = []
    for i in range(4):
        token_loads.append((hidden[i], tok.at[i, :, pl.ds(0, D)], tok_sem.at[i, 0]))
        token_loads.append((d_mix[i], tok.at[i, :, pl.ds(D, D)], tok_sem.at[i, 1]))
    start_all(token_loads)
    g_up[...] = jnp.zeros_like(g_up)
    g_down[...] = jnp.zeros_like(g_down)
    wait_all(loads)
    def one_source(i, carry):
        pltpu.make_async_copy(hidden[0], tok.at[i, :, pl.ds(0, D)], tok_sem.at[i, 0]).wait()
        pltpu.make_async_copy(d_mix[0], tok.at[i, :, pl.ds(D, D)], tok_sem.at[i, 1]).wait()
        out, dx = units(tok[i, :, :D], tok[i, :, D:], up, down, g_up, g_down, 2 * D)
        part[i, :, :D] = out.astype(bf)
        part[i, :, D:] = dx.astype(bf)
        for k in range(4):

            @pl.when(i == k)
            def _():
                pltpu.make_async_copy(part.at[k], part_out[k], out_sem.at[k]).start()

        return carry

    lax.fori_loop(0, 4, one_source, 0)
    outs = [pltpu.make_async_copy(part.at[k], part_out[k], out_sem.at[k]) for k in range(4)]
    for s in range(2):
        stage[:, 2 * s * D : 2 * s * D + D] = g_up[:, s * D : s * D + D].astype(bf)
        stage[:, 2 * s * D + D : 2 * s * D + 2 * D] = g_down[:, s * D : s * D + D].astype(bf)
    wait_all(outs + start_all([(stage, g_out, w_sem.at[1])]))


def routed_experts(ids, hidden, d_mix, metas, priors, gathered):
    anyspec = pl.BlockSpec(memory_space=pl.ANY)
    hbm = pl.BlockSpec(memory_space=pltpu.HBM)
    whole = jax.ShapeDtypeStruct((D, FF), bf)
    shapes = [jax.ShapeDtypeStruct((TOK, D), bf)] * 8
    shapes += [jax.ShapeDtypeStruct((4, 8, TOK), f32)] + [whole] * 4
    return pl.pallas_call(
        routed_kernel,
        out_shape=shapes,
        in_specs=[pl.BlockSpec(memory_space=pltpu.SMEM)] + [anyspec] * 17,
        out_specs=[hbm] * len(shapes),
        scratch_shapes=[
            pltpu.VMEM((4, TOK, 2 * D), bf),
            pltpu.VMEM((4, 16, TOK), f32),
            pltpu.VMEM((2, D, FF), bf),
            pltpu.VMEM((2, D, FF), bf),
            pltpu.VMEM((2, D, FF), f32),
            pltpu.VMEM((2, D, FF), f32),
            pltpu.VMEM((TOK, 2 * D), f32),
            pltpu.VMEM((4, TOK, 2 * D), bf),
            pltpu.VMEM((4, 8, TOK), f32),
            pltpu.VMEM((4, D, FF), bf),
            pltpu.SemaphoreType.DMA((4, 4)),
            pltpu.SemaphoreType.DMA((1,)),
            pltpu.SemaphoreType.DMA((9,)),
            pltpu.SemaphoreType.DMA((4,)),
        ],
        compiler_params=pltpu.CompilerParams(vmem_limit_bytes=58 * 1024 * 1024),
        name="routed_experts",
    )(ids, *hidden, *d_mix, *metas, *priors, gathered)


def shared_units(hidden, d_mix, gathered):
    anyspec = pl.BlockSpec(memory_space=pl.ANY)
    hbm = pl.BlockSpec(memory_space=pltpu.HBM)
    shapes = [jax.ShapeDtypeStruct((TOK, 2 * D), bf)] * 4 + [jax.ShapeDtypeStruct((D, FF), bf)]
    return pl.pallas_call(
        shared_kernel,
        out_shape=shapes,
        in_specs=[anyspec] * 9,
        out_specs=[hbm] * 5,
        scratch_shapes=[
            pltpu.VMEM((4, TOK, 2 * D), bf),
            pltpu.VMEM((D, 2 * D), bf),
            pltpu.VMEM((D, 2 * D), bf),
            pltpu.VMEM((D, 2 * D), f32),
            pltpu.VMEM((D, 2 * D), f32),
            pltpu.VMEM((4, TOK, 2 * D), bf),
            pltpu.VMEM((D, FF), bf),
            pltpu.SemaphoreType.DMA((4, 2)),
            pltpu.SemaphoreType.DMA((2,)),
            pltpu.SemaphoreType.DMA((4,)),
        ],
        compiler_params=pltpu.CompilerParams(vmem_limit_bytes=58 * 1024 * 1024),
        name="shared_units",
    )(*hidden, *d_mix, gathered)


def head_only(block, head):
    lane = lax.broadcasted_iota(jnp.int32, block.shape, 1)
    return jnp.where((lane >= 64) == (head == 1), block, jnp.zeros_like(block))


def attend_kernel(res, q_ref, k_ref, v_ref, o_ref, lse_ref, vt_ref):
    qb = pl.program_id(1)

    @pl.when(qb == 0)
    def _():
        vt_ref[...] = v_ref[...].T

    def work(rows):
        q = q_ref[...] * 0.125
        outs = []
        for head in range(2):
            scores = dot(k_ref[rows, :], head_only(q, head), NT)
            top = jnp.max(scores, axis=0, keepdims=True)
            expo = jnp.exp(scores - top)
            total = jnp.sum(expo, axis=0, keepdims=True)
            weights = (expo * (1.0 / total)).astype(bf)
            outs.append(dot(vt_ref[head * 64 : head * 64 + 64, rows], weights))
            lse_ref[0, head : head + 1, :] = top + jnp.log(total)
        o_ref[...] = jnp.concatenate(outs, axis=0).T.astype(bf)

    @pl.when(res[0] == 1)
    def _():
        work(pl.ds(0, TOK))

    @pl.when(res[0] != 1)
    def _():
        work(pl.ds(pl.multiple_of(qb * 256, 256), 256))


def attend_fast(resolution, projected):
    return pl.pallas_call(
        attend_kernel,
        grid_spec=pltpu.PrefetchScalarGridSpec(
            num_scalar_prefetch=1,
            grid=(3, 4),
            in_specs=[
                pl.BlockSpec((256, 128), lambda h, i, r: (i, h)),
                pl.BlockSpec((TOK, 128), lambda h, i, r: (0, 3 + h)),
                pl.BlockSpec((TOK, 128), lambda h, i, r: (0, 6 + h)),
            ],
            out_specs=[
                pl.BlockSpec((256, 128), lambda h, i, r: (i, h)),
                pl.BlockSpec((1, 8, 256), lambda h, i, r: (h, 0, i)),
            ],
            scratch_shapes=[pltpu.VMEM((128, TOK), bf)],
        ),
        out_shape=(
            jax.ShapeDtypeStruct((TOK, D), bf),
            jax.ShapeDtypeStruct((3, 8, TOK), f32),
        ),
        compiler_params=pltpu.CompilerParams(vmem_limit_bytes=48 * 1024 * 1024),
        name="attend_fast",
    )(resolution, projected, projected, projected)


def attend_back_kernel(
    res, q_ref, k_ref, v_ref, do_ref, lse_ref, dq_ref, dk_ref, dv_ref, kt_ref, dk_acc, dv_acc
):
    qb = pl.program_id(1)

    @pl.when(qb == 0)
    def _():
        kt_ref[...] = k_ref[...].T

    def work(rows, whole):
        q = q_ref[...] * 0.125
        grads = []
        dk = dv = None
        for head in range(2):
            qh = head_only(q, head)
            doh = head_only(do_ref[...], head)
            scores = dot(k_ref[rows, :], qh, NT)
            probs = jnp.exp(scores - lse_ref[0, head : head + 1, :])
            d_weights = dot(v_ref[rows, :], doh, NT)
            delta = jnp.sum(d_weights * probs, axis=0, keepdims=True)
            d_scores = (probs * (d_weights - delta)).astype(bf)
            dv_one = dot(probs.astype(bf), doh)
            dk_one = dot(d_scores, qh)
            dv = dv_one if dv is None else dv + dv_one
            dk = dk_one if dk is None else dk + dk_one
            grads.append(dot(kt_ref[head * 64 : head * 64 + 64, rows], d_scores))
        dq_ref[...] = (jnp.concatenate(grads, axis=0).T * 0.125).astype(bf)
        if not whole:
            dk_ref[rows, :] = dk.astype(bf)
            dv_ref[rows, :] = dv.astype(bf)
            return

        @pl.when(qb == 0)
        def _():
            dk_acc[...] = dk
            dv_acc[...] = dv

        @pl.when(qb != 0)
        def _():
            dk_acc[...] += dk
            dv_acc[...] += dv

        @pl.when(qb == 3)
        def _():
            dk_ref[...] = dk_acc[...].astype(bf)
            dv_ref[...] = dv_acc[...].astype(bf)

    @pl.when(res[0] == 1)
    def _():
        work(pl.ds(0, TOK), True)

    @pl.when(res[0] != 1)
    def _():
        work(pl.ds(pl.multiple_of(qb * 256, 256), 256), False)


def attend_back_fast(resolution, projected, lse, d_attended):
    return pl.pallas_call(
        attend_back_kernel,
        grid_spec=pltpu.PrefetchScalarGridSpec(
            num_scalar_prefetch=1,
            grid=(3, 4),
            in_specs=[
                pl.BlockSpec((256, 128), lambda h, i, r: (i, h)),
                pl.BlockSpec((TOK, 128), lambda h, i, r: (0, 3 + h)),
                pl.BlockSpec((TOK, 128), lambda h, i, r: (0, 6 + h)),
                pl.BlockSpec((256, 128), lambda h, i, r: (i, h)),
                pl.BlockSpec((1, 8, 256), lambda h, i, r: (h, 0, i)),
            ],
            out_specs=[
                pl.BlockSpec((256, 128), lambda h, i, r: (i, h)),
                pl.BlockSpec((TOK, 128), lambda h, i, r: (0, h)),
                pl.BlockSpec((TOK, 128), lambda h, i, r: (0, h)),
            ],
            scratch_shapes=[
                pltpu.VMEM((128, TOK), bf),
                pltpu.VMEM((TOK, 128), f32),
                pltpu.VMEM((TOK, 128), f32),
            ],
        ),
        out_shape=[jax.ShapeDtypeStruct((TOK, D), bf)] * 3,
        compiler_params=pltpu.CompilerParams(vmem_limit_bytes=48 * 1024 * 1024),
        name="attend_back_fast",
    )(resolution, projected, projected, projected, d_attended, lse)


def halves(value):
    high = value.astype(bf)
    return high, (value - high.astype(f32)).astype(bf)


def dot_three(a, b, dims=NN):
    return dot(a[0], b[0], dims) + dot(a[0], b[1], dims) + dot(a[1], b[0], dims)


def up_owner(e):
    return (24 if e % 2 else 0) + e // 2 if e < 8 else 20 + 2 * (e - 8)


def down_owner(e):
    return (4 if e % 2 else 16) + e // 2 if e < 8 else 21 + 2 * (e - 8)


def square_owner(j):
    return 8 + j if j < 3 else (9 + j if j < 7 else 21 + j)


OUT_OWNER, ROUTER_OWNER = 11, 30


def pack_kernel(square, out, router, up, down, packed):
    for e in range(10):
        packed[up_owner(e)] = up[e]
        packed[down_owner(e)] = down[e]
    rest = jnp.zeros((48, D - 96), f32)
    for j in range(9):
        packed[square_owner(j)] = jnp.concatenate([square[j], rest], axis=1)
    packed[OUT_OWNER] = jnp.concatenate([out[...], rest], axis=1)
    packed[ROUTER_OWNER] = router[...]
    packed[31] = jnp.zeros((48, D), f32)


def pack_owned(square, out, router, up, down):
    vmem = pl.BlockSpec(memory_space=pltpu.VMEM)
    return pl.pallas_call(
        pack_kernel,
        out_shape=jax.ShapeDtypeStruct((32, 48, D), f32),
        in_specs=[vmem] * 5,
        out_specs=vmem,
        name="pack_owned",
    )(square, out, router, up, down)


def owned_grad_kernel(ids, *refs):
    pieces = refs[:6]
    dense, small, extra, full_out, cut_out, buf, sems = refs[6:]
    n, z, x = ids[0], ids[1], ids[2]
    is_small = (z == 1) | ((z == 3) & (x == 1))
    for group, owner in enumerate((0, 2, 3)):

        @pl.when((z == owner) & jnp.logical_not(is_small))
        def _():
            copies = [
                pltpu.make_async_copy(pieces[2 * group + i], buf.at[i], sems.at[i])
                for i in range(2)
            ]
            for copy in copies:
                copy.start()
            for copy in copies:
                copy.wait()

    @pl.when(jnp.logical_not(is_small))
    def _():
        for k in range(4):
            lanes = slice(k * D, k * D + D)
            full_out[k] = buf[0, :, lanes].astype(f32) + buf[1, :, lanes].astype(f32)

    @pl.when(is_small)
    def _():
        rows = small[...].reshape(32, 8, 512)

        def place(matrix, width):
            rest = jnp.zeros((D, D - width), f32)
            for m in range(4):
                part = matrix[:, m * width : m * width + width]
                full_out[m ^ n] = jnp.concatenate([part, rest], axis=1)

        @pl.when(z == 1)
        def _():
            @pl.when(x == 0)
            def _():
                place(dense[...], 96)

        @pl.when(jnp.logical_not((z == 1) & (x == 0)))
        def _():
            is_router = (z == 3) & (n == 2)

            @pl.when(is_router)
            def _():
                summed = jnp.sum(rows[:, :, :D], axis=0)
                place(jnp.concatenate([summed, jnp.zeros((120, D), f32)], axis=0).T[:, :8], 2)

            @pl.when(jnp.logical_not(is_router))
            def _():
                first = (lax.broadcasted_iota(jnp.int32, (256, D), 0) % 8) < 4
                both = small[:, :D]
                mods = jnp.where(first, both, 0.0)
                conds = pltpu.roll(both, 252, 0)
                conds = jnp.where(first, conds, 0.0)
                place(dot_three(halves(mods), halves(conds), TN), 96)

    for w in range(8):
        for m in range(4):
            cut_out[4 * w + m, :48] = full_out[m ^ n, 48 * w : 48 * w + 48, :].astype(bf)
            cut_out[4 * w + m, 48:] = extra[...]


def owned_grad(ids, pieces, dense, small, extra):
    anyspec, vmem = pl.BlockSpec(memory_space=pltpu.HBM), pl.BlockSpec(memory_space=pltpu.VMEM)
    return pl.pallas_call(
        owned_grad_kernel,
        out_shape=(
            jax.ShapeDtypeStruct((4, D, D), f32),
            jax.ShapeDtypeStruct((32, 56, D), bf),
        ),
        in_specs=[pl.BlockSpec(memory_space=pltpu.SMEM)] + [anyspec] * 6 + [vmem] * 3,
        out_specs=[vmem, vmem],
        scratch_shapes=[pltpu.VMEM((2, D, FF), bf), pltpu.SemaphoreType.DMA((2,))],
        compiler_params=pltpu.CompilerParams(vmem_limit_bytes=40 * 1024 * 1024),
        name="owned_grad",
    )(ids, *pieces, dense, small, extra)


def ortho_kernel(ids, grad, moment, cut_out, cur, high, low, cross):
    n = ids[0]
    for k in range(4):
        cur[k] = grad[k]
    for w in range(8):
        rows = slice(48 * w, 48 * w + 48)
        for m in range(4):
            cur[m ^ n, rows, :] += MOMENTUM * moment[4 * w + m]
    total = jnp.zeros((1, D), f32)
    for k in range(4):
        total = total + jnp.sum(cur[k] * cur[k], axis=0, keepdims=True)
    factor = 1.0 / (jnp.sqrt(jnp.sum(total, axis=1, keepdims=True)) + 1e-07)

    def keep(k, value):
        cur[k] = value
        high[:, k * D : k * D + D], low[:, k * D : k * D + D] = halves(value)

    for k in range(4):
        keep(k, cur[k] * factor)

    def sweep(_, carry):
        cross[...] = dot(high[...], low[...], NT)
        gram = dot(high[...], high[...], NT) + (cross[...] + cross[...].T)
        gram_high, gram_low = halves(gram)
        cross[...] = dot(gram_high, gram_low)
        square = dot(gram_high, gram_high) + (cross[...] + cross[...].T)
        poly = halves(NS_SECOND * gram + NS_THIRD * square)
        for k in range(4):
            lanes = slice(k * D, k * D + D)
            step = dot_three(poly, (high[:, lanes], low[:, lanes]))
            keep(k, NS_FIRST * cur[k] + step)
        return carry

    lax.fori_loop(0, 5, sweep, 0)
    for w in range(8):
        for m in range(4):
            cut_out[4 * w + m] = cur[m ^ n, 48 * w : 48 * w + 48, :].astype(bf)


def ortho_owned(ids, grad, moment):
    vmem = pl.BlockSpec(memory_space=pltpu.VMEM)
    return pl.pallas_call(
        ortho_kernel,
        out_shape=jax.ShapeDtypeStruct((32, 48, D), bf),
        in_specs=[pl.BlockSpec(memory_space=pltpu.SMEM), vmem, vmem],
        out_specs=vmem,
        scratch_shapes=[
            pltpu.VMEM((4, D, D), f32),
            pltpu.VMEM((D, FF), bf),
            pltpu.VMEM((D, FF), bf),
            pltpu.VMEM((D, D), f32),
        ],
        compiler_params=pltpu.CompilerParams(vmem_limit_bytes=40 * 1024 * 1024),
        name="ortho_owned",
    )(ids, grad, moment)


def update_kernel(decay_ref, grads, orthos, *refs):
    decay = decay_ref[0]
    weights, moments, emas = refs[0:5], refs[5:10], refs[10:15]
    states, masters, averages = refs[15:20], refs[20:25], refs[25:30]
    small_rate, large_rate = RATE * 0.2 * D**0.5, RATE * 0.2 * FF**0.5

    def step(which, at, grad, ortho, rate):
        states[which][at] = MOMENTUM * moments[which][at] + grad.astype(f32)
        master = weights[which][at] - rate * ortho.astype(f32)
        masters[which][at] = master
        averages[which][at] = decay * emas[which][at] + (1.0 - decay) * master

    for j in range(9):
        own = square_owner(j)
        step(0, j, grads[own, :48, :96], orthos[own, :48, :96], small_rate)
    step(1, slice(None), grads[OUT_OWNER, :48, :96], orthos[OUT_OWNER, :48, :96], small_rate)

    def router_rows(source):
        return source[ROUTER_OWNER, :48, :128].astype(f32).T[:2]

    step(2, slice(None), router_rows(grads), router_rows(orthos), small_rate)
    for e in range(10):
        step(3, e, grads[up_owner(e), :48], orthos[up_owner(e), :48], large_rate)
        step(4, e, grads[down_owner(e), :48], orthos[down_owner(e), :48], large_rate)


def update(decay, grads, orthos, weights, moments, emas):
    vmem = pl.BlockSpec(memory_space=pltpu.VMEM)
    shapes = [jax.ShapeDtypeStruct(weight.shape, f32) for weight in weights]
    return pl.pallas_call(
        update_kernel,
        out_shape=shapes * 3,
        in_specs=[pl.BlockSpec(memory_space=pltpu.SMEM)] + [vmem] * 17,
        out_specs=[vmem] * 15,
        compiler_params=pltpu.CompilerParams(vmem_limit_bytes=48 * 1024 * 1024),
        name="update",
    )(decay, grads, orthos, *weights, *moments, *emas)


def first_back_kernel(
    ids, dq, dk, dv, hidden, tokens, d_mid, maps, scales, g_out, mods, cond, g_router, *refs
):
    grad_in, keep, out_send, payload, g_acc, sums = refs
    i = pl.program_id(0)
    heads = (dq, dk, dv)
    d_hidden = jnp.zeros((SHORT, D), f32)
    for j in range(3):
        d_hidden = d_hidden + dot(heads[j][...], maps[j * D : j * D + D, :])

    @pl.when(i == 0)
    def _():
        for j in range(3):
            g_acc[j] = dot(heads[j][...], hidden[...], TN)

    @pl.when(i != 0)
    def _():
        for j in range(3):
            g_acc[j] += dot(heads[j][...], hidden[...], TN)

    rows = tokens[...].astype(f32)
    center = rows - jnp.mean(rows, axis=1, keepdims=True)
    inverse = lax.rsqrt(jnp.mean(center * center, axis=1, keepdims=True) + EPSILON)
    normed = center * inverse
    d_normed = d_hidden * (1.0 + scales[pl.ds(i, 1), :])
    inner = d_normed - jnp.mean(d_normed, axis=1, keepdims=True)
    inner = inner - normed * jnp.mean(d_normed * normed, axis=1, keepdims=True)
    grad_in[...] = d_mid[...] + inverse * inner
    sums[0, pl.ds(i, 1), :] = jnp.sum(d_hidden, axis=0, keepdims=True)
    sums[1, pl.ds(i, 1), :] = jnp.sum(d_hidden * normed, axis=0, keepdims=True)

    @pl.when(i == 3)
    def _():
        c = lax.rem(ids[0], 2)
        for m in range(4):

            def total(m=m):
                return g_acc[m] if m < 3 else g_out[...]

            @pl.when(c == m % 2)
            def _():
                keep[m // 2] = total()

            @pl.when(c != m % 2)
            def _():
                out_send[m // 2] = total().astype(bf)

        rows = [sums[0, :4, :], sums[1, :4, :]] + [mods[j] for j in range(4)]
        payload[...] = jnp.zeros_like(payload)
        for j, slot in enumerate((12, 13, 14, 15, 28, 29)):
            payload[slot, :4, :D] = rows[j]
            payload[slot, 4:, :D] = cond[...]
        payload[30, :, :D] = g_router[...]
        bias = jnp.concatenate([jnp.sum(row, axis=0, keepdims=True) for row in rows], axis=1)
        for slot in range(32):
            payload[slot, 0:1, D : D + 72] = bias[:, slot * 72 : slot * 72 + 72]


def first_back_fast(ids, d_heads, hidden, tokens, d_mid, maps, scales, g_out, mods, cond, g_router):
    block = pl.BlockSpec((SHORT, D), lambda i: (i, 0))

    def whole(*shape):
        return pl.BlockSpec(shape, lambda i: (0,) * len(shape))

    return pl.pallas_call(
        first_back_kernel,
        grid=(4,),
        out_shape=(
            jax.ShapeDtypeStruct((TOK, D), f32),
            jax.ShapeDtypeStruct((2, D, D), f32),
            jax.ShapeDtypeStruct((2, D, D), bf),
            jax.ShapeDtypeStruct((32, 8, 512), f32),
        ),
        in_specs=[pl.BlockSpec(memory_space=pltpu.SMEM)]
        + [block] * 6
        + [
            whole(3 * D, D),
            whole(4, D),
            whole(D, D),
            whole(4, 4, D),
            whole(4, D),
            whole(8, D),
        ],
        out_specs=[block, whole(2, D, D), whole(2, D, D), whole(32, 8, 512)],
        scratch_shapes=[pltpu.VMEM((3, D, D), f32), pltpu.VMEM((2, 8, D), f32)],
        compiler_params=pltpu.CompilerParams(vmem_limit_bytes=40 * 1024 * 1024),
        name="first_back",
    )(ids, *d_heads, hidden, tokens, d_mid, maps, scales, g_out, mods, cond, g_router)


AXES = (WIDE, NARROW)


def route_pairs(move):
    pairs = []
    for index in range(32):
        w, n = divmod(index, 4)
        target = move(w // 2, w % 2, n // 2, n % 2)
        if target is not None:
            z, x, y, c = target
            pairs.append((index, (z * 2 + x) * 4 + y * 2 + c))
    return pairs


def send(array, move):
    return lax.ppermute(array, AXES, route_pairs(move))


def to_core(z, x, y, c):
    return (z, x, y, 1 - c)


def to_y(z, x, y, c):
    return (z, x, 1 - y, c)


def to_diag(z, x, y, c):
    return (z, x, 1 - y, 1 - c)


def to_x(z, x, y, c):
    return (z, 1 - x, y, c)


def to_z(step):
    return lambda z, x, y, c: ((z + step) % 4, x, y, c)


NARROW_MOVES = (None, to_core, to_y, to_diag)


def pick(array, index, axis=0):
    return lax.dynamic_index_in_dim(array, index, axis, keepdims=False)


def in_order(mine, other, flag):
    return jnp.where(flag == 0, mine, other), jnp.where(flag == 0, other, mine)


def xor_blocks(array, axis, y, c):
    parts = [lax.index_in_dim(array, i, axis, keepdims=True) for i in range(4)]
    parts = [jnp.where(c == 0, parts[i], parts[i ^ 1]) for i in range(4)]
    parts = [jnp.where(y == 0, parts[i], parts[i ^ 2]) for i in range(4)]
    return jnp.concatenate(parts, axis=axis)


def gather_z(rows, z):
    ring = jnp.stack([send(rows, to_z(step)) for step in (3, 2, 1)] + [rows])
    return lax.dynamic_slice_in_dim(jnp.concatenate([ring, ring]), (3 - z) % 4, 4, 0)


def gather_core(by_z, received, x, c):
    by_zx = jnp.stack(in_order(by_z, received, x), axis=1)
    return jnp.stack(in_order(by_zx, send(by_zx, to_core), c), axis=2)


def lanes_to(block, width):
    return jnp.pad(block, [(0, 0)] * (block.ndim - 1) + [(0, width - block.shape[-1])])


def turned(array):
    return jnp.swapaxes(array, -1, -2)


def fast_device(
    tokens,
    conditions,
    routes,
    resolution,
    step_count,
    cotangent,
    w_square,
    w_out,
    w_router,
    w_up,
    w_down,
    b_ada,
    moment_square,
    moment_out,
    moment_router,
    moment_up,
    moment_down,
    moment_bias,
    ema_square,
    ema_out,
    ema_router,
    ema_up,
    ema_down,
    ema_bias,
):
    wide = lax.axis_index(WIDE)
    narrow = lax.axis_index(NARROW)
    z, x = wide // 2, wide % 2
    y, c = narrow // 2, narrow % 2

    up_t = turned(w_up).astype(bf)
    down_t = turned(w_down).astype(bf)
    routed_t = jnp.stack([up_t[:8], down_t[:8]], axis=1).reshape(4, 4, 48, D)
    shared_t = jnp.stack([up_t[8:], down_t[8:]], axis=1).reshape(4, 48, D)
    square_t = turned(w_square).astype(bf)
    out_t = turned(w_out).astype(bf)[None]
    misc = jnp.concatenate(
        [
            lanes_to(b_ada.astype(bf)[None], 96),
            lanes_to(w_router.astype(bf), 96),
            jnp.zeros((5, 96), bf),
        ]
    )
    flat = jnp.concatenate(
        [
            square_t[:5].reshape(-1, 96),
            misc,
            square_t[5:].reshape(-1, 96),
            out_t.reshape(-1, 96),
        ]
    )
    lanes = jnp.stack([flat] + [send(flat, move) for move in NARROW_MOVES[1:]])
    rows = jnp.concatenate(list(xor_blocks(lanes, 0, y, c)), axis=1)

    moment_parts = (
        turned(moment_square),
        turned(moment_out),
        moment_router,
        turned(moment_up),
        turned(moment_down),
    )
    router_block = lanes_to(turned(moment_router), D)
    moments = pack_owned(*moment_parts[:2], router_block, *moment_parts[3:])

    def my_half(block):
        return pick(block.reshape(5, 2, 24, D), c, 1).reshape(120, D)

    mine = [pick(routed_t, narrow)]
    mine += [send(pick(routed_t, narrow ^ k), NARROW_MOVES[k]) for k in (1, 2, 3)]
    first_rows = jnp.concatenate([my_half(rows[:240]), rows[240:248]])
    first_z = gather_z(first_rows, z)
    first_z, blocks = lax.optimization_barrier((first_z, jnp.stack(mine + [shared_t])))
    gathered = lax.all_gather(blocks, WIDE)
    first_x = send(first_z, to_x)
    first_x, second_rows, moments = lax.optimization_barrier((first_x, rows[248:], moments))
    second_z = gather_z(my_half(second_rows), z)
    first_all = gather_core(first_z, first_x, x, c)
    second_all = gather_core(second_z, send(second_z, to_x), x, c)

    def assemble(gathered):
        parts = gathered[..., :120, :].reshape(8, 2, 5, 24, D)
        return jnp.transpose(parts, (2, 0, 1, 3, 4)).reshape(5, D, D)

    first_maps = assemble(first_all)
    second_maps = assemble(second_all)
    misc_all = first_all[:, :, 0, 120:, :].reshape(8, 8, 4, 96)
    bias_low = misc_all[:, 0, :, :72].reshape(-1)
    router_low = jnp.transpose(misc_all[:, 1:3, :, :48], (2, 1, 0, 3)).reshape(ROUTED, D)

    res_group = resolution[0]
    token_f = tokens.astype(f32)
    segments = tokens.shape[0] // SHORT
    seg_ratio = LONG // SHORT
    first_seg = jnp.arange(segments, dtype=jnp.int32) // seg_ratio * seg_ratio
    chosen = jnp.where(res_group == 1, conditions[first_seg], conditions)
    cond_low = jax.nn.silu(chosen.astype(f32)).astype(bf)
    bias_rows = bias_low.astype(f32).reshape(6, D)

    def modulation_of(maps, bias):
        return dot(cond_low, maps.reshape(-1, D), NT).reshape(segments, -1, D) + bias

    first_two = modulation_of(first_maps[3:], bias_rows[:2])
    last_four = modulation_of(second_maps[:4], bias_rows[2:])
    out_map = second_maps[4]
    seg_rows = token_f.reshape(segments, SHORT, D)
    first_mod = modulate(seg_rows, first_two[:, 0:1], first_two[:, 1:2])
    hidden_one = first_mod.reshape(-1, D).astype(bf)
    query_maps = first_maps[:3].reshape(3 * D, D)
    projected = dot(hidden_one, query_maps, NT).astype(bf)
    gate_one, gate_two = last_four[:, 0:1], last_four[:, 3:4]
    grad_out = cotangent.astype(f32)
    grad_seg = grad_out.reshape(segments, SHORT, D)
    d_mixture = (grad_seg * gate_two).reshape(-1, D).astype(bf)
    d_mix_core = send(d_mixture, to_core)
    d_mix_y = send(d_mixture, to_y)
    attended, log_total = attend_fast(resolution, projected)
    attended, d_mix_y = lax.optimization_barrier((attended, d_mix_y))
    d_mix_diag = send(d_mix_y, to_core)
    attn_out = dot(attended, out_map, NT)
    mid_state = token_f + (attn_out.reshape(segments, SHORT, D) * gate_one).reshape(-1, D)
    second_mod, second_back = jax.vjp(
        modulate, mid_state.reshape(segments, SHORT, D), last_four[:, 1:2], last_four[:, 2:3]
    )
    hidden_two = second_mod.reshape(-1, D).astype(bf)

    logits = dot(router_low, hidden_two, NT)
    experts = jnp.arange(ROUTED, dtype=jnp.int32)[:, None]
    named = (routes[:, 0][None] == experts) | (routes[:, 1][None] == experts)
    index = jnp.arange(TOK, dtype=jnp.int32)
    earlier = (index[:, None] < index[None, :]).astype(bf)
    place = jnp.dot(named.astype(bf), earlier, preferred_element_type=f32)
    masked = jnp.where(named, logits, -jnp.inf)
    expo = jnp.where(named, jnp.exp(logits - jnp.max(masked, axis=0, keepdims=True)), 0.0)
    gates = expo / jnp.sum(expo, axis=0, keepdims=True)
    meta = jnp.concatenate([jnp.where(named, place, -1.0), gates])

    hidden_core, meta_core = send(hidden_two, to_core), send(meta, to_core)
    hidden_y, meta_y = send(hidden_two, to_y), send(meta, to_y)
    meta_diag = send(meta, to_diag)
    hidden_y, meta_y, meta_core, meta_diag = lax.optimization_barrier(
        (hidden_y, meta_y, meta_core, meta_diag)
    )
    hidden_diag = send(hidden_y, to_core)
    place_ids = jnp.stack([narrow, z, x]).astype(jnp.int32)
    hiddens = (hidden_two, hidden_core, hidden_y, hidden_diag)
    d_mixes = (d_mixture, d_mix_core, d_mix_y, d_mix_diag)
    metas = (meta, meta_core, meta_y, meta_diag)
    hiddens, d_mixes, metas, gathered, moments = lax.optimization_barrier(
        (hiddens, d_mixes, metas, gathered, moments)
    )
    moments = lax.all_to_all(moments, AXES, 0, 0, tiled=True)
    *priors, g_shared = shared_units(hiddens, d_mixes, gathered)

    def back_x(z_, x_, y_, c_):
        return (z_, 0, y_, c_) if x_ == 1 else None

    def forth_x(z_, x_, y_, c_):
        return (z_, 1, y_, c_) if x_ == 0 else None

    def along_z(hops, sides=(0, 1)):
        table = dict(hops)

        def move(z_, x_, y_, c_):
            return (table[z_], x_, y_, c_) if z_ in table and x_ in sides else None

        return move

    def added(kept, other):
        return (kept.astype(f32) + other.astype(f32)).astype(bf)

    def shared_part(k):
        return lax.dynamic_slice_in_dim(g_shared, (narrow ^ k) * D, D, 1)

    def over_core(parts):
        over = (parts[2].astype(f32) + send(parts[3], to_core).astype(f32)).astype(bf)
        return parts[0].astype(f32) + send(parts[1], to_core).astype(f32), over

    gate = lax.optimization_barrier
    shared_parts = [shared_part(0)]
    shared_parts += [send(shared_part(k), NARROW_MOVES[k]) for k in (1, 2, 3)]
    *routed_outs, d_gate_rows, g_send, g_keep, g_second, g_third = routed_experts(
        place_ids, hiddens, d_mixes, metas, priors, gathered
    )
    routed_outs, shared_parts, moments, d_gate_rows, g_send = gate(
        (routed_outs, shared_parts, moments, d_gate_rows, g_send)
    )
    pairs_one, pairs_two, pairs_three = ((3, 2), (1, 0)), ((0, 1), (3, 2)), ((0, 1), (2, 3))
    received_one = send(g_send, to_x)
    step_three = send(g_third, along_z(pairs_three))
    d_rows = [d_gate_rows[0, :2]]
    d_rows += [send(d_gate_rows[k, :2], NARROW_MOVES[k]) for k in (1, 2, 3)]
    own_hidden, over_hidden = over_core(routed_outs[4:])
    own_hidden, over_hidden, mix_outs, shared_parts, g_keep, g_second, d_rows = gate(
        (own_hidden, over_hidden, routed_outs[:4], shared_parts, g_keep, g_second, d_rows)
    )
    far_hidden = send(over_hidden, to_y)
    shared_grad = jnp.concatenate(shared_parts, axis=1)
    received_second = send(g_second, back_x)
    received_shared = send(shared_grad, forth_x)
    own_mix, over_mix = over_core(mix_outs)
    d_gates = xor_blocks(jnp.stack(d_rows), 0, y, c).reshape(ROUTED, TOK)
    far_hidden, own_mix, over_mix, received_one, step_three, shared_grad, d_gates = gate(
        (far_hidden, own_mix, over_mix, received_one, step_three, shared_grad, d_gates)
    )
    held_one = added(g_keep, received_one)
    held_three = added(g_third, step_three)
    d_hidden = own_hidden + far_hidden.astype(f32)

    d_logits = gates * (d_gates - jnp.sum(gates * d_gates, axis=0, keepdims=True))
    d_logits = d_logits.astype(bf)
    g_router = jnp.dot(d_logits, hidden_two, preferred_element_type=f32)
    d_hidden = d_hidden + dot(d_logits, router_low, TN)
    d_mid_norm, d_shift_two, d_scale_two = second_back(d_hidden.reshape(segments, SHORT, D))
    d_mid = grad_out + d_mid_norm.reshape(-1, D)
    d_mid_seg = d_mid.reshape(segments, SHORT, D)
    d_gate_one = jnp.sum(d_mid_seg * attn_out.reshape(segments, SHORT, D), axis=1)
    d_attn = (d_mid_seg * gate_one).reshape(-1, D).astype(bf)
    g_out = dot(d_attn, attended, TN)
    d_attended = jnp.dot(d_attn, out_map, preferred_element_type=f32).astype(bf)
    d_attended, held_one, held_three, over_mix = gate(
        (d_attended, held_one, held_three, over_mix)
    )
    step_one = send(held_one, along_z(pairs_one))
    last_three = send(held_three, along_z(((1, 3),)))
    far_mix = send(over_mix, to_y)
    d_heads = attend_back_fast(resolution, projected, log_total, d_attended)
    d_heads, step_one, last_three, received_second, received_shared, far_mix = gate(
        (d_heads, step_one, last_three, received_second, received_shared, far_mix)
    )
    held_two = added(
        jnp.where(x == 0, g_second, shared_grad), jnp.where(x == 0, received_second, received_shared)
    )
    held_one = added(held_one, step_one)
    held_three = added(held_three, last_three)
    d_heads, held_one, held_two, held_three = gate((d_heads, held_one, held_two, held_three))

    def cross_x(z_, x_, y_, c_):
        return (z_, 0, y_, c_) if x_ == 1 and z_ == 3 else None

    step_two = send(held_two, along_z(pairs_two))
    last_one = send(held_one, along_z(((2, 0),)))
    cross_three = send(held_three, cross_x)
    mixture = own_mix + far_mix.astype(f32)
    output = (
        mid_state + (mixture.reshape(segments, SHORT, D) * gate_two).reshape(-1, D)
    ).astype(bf)
    d_gate_two = jnp.sum(grad_seg * mixture.reshape(segments, SHORT, D), axis=1)
    mods = jnp.stack([d_gate_one, d_shift_two[:, 0], d_scale_two[:, 0], d_gate_two])
    grad_in, dense_keep, dense_send, small = first_back_fast(
        place_ids,
        d_heads,
        hidden_one,
        tokens,
        d_mid,
        query_maps,
        first_two[:, 1],
        g_out,
        mods,
        cond_low.astype(f32),
        g_router,
    )

    dense_recv = send(dense_send, to_core)
    small, dense_recv = gate((small, dense_recv))
    dense = dense_keep + dense_recv.astype(f32)
    dense_far = send(pick(dense, 1 - y).astype(bf), to_y)
    small = lax.all_to_all(small, AXES, 0, 0, tiled=True)
    g_bias = jnp.sum(small[:, 0, D : D + 72], axis=0)
    dense_far, step_two = gate((dense_far, step_two))
    held_two = added(held_two, step_two)
    last_two = send(held_two, along_z(((1, 2),)))
    dense = pick(dense, y) + dense_far.astype(f32)
    dense_side = send(dense.astype(bf), back_x)
    pieces = (held_one, last_one, held_two, last_two, held_three, cross_three)
    dense = dense + dense_side.astype(f32)
    dense_low = dense.astype(bf)
    for step in (1, 2, 3):

        def to_second(z_, x_, y_, c_, step=step):
            return (1, x_, y_, c_) if (z_ + step) % 4 == 1 and x_ == 0 else None

        dense = dense + send(dense_low, to_second).astype(f32)

    state_bias = MOMENTUM_VECTOR * moment_bias + g_bias
    part_sum = jnp.sum(state_bias * state_bias)
    sum_high = part_sum.astype(bf)
    sum_low = (part_sum - sum_high.astype(f32)).astype(bf)

    extra = jnp.pad(jnp.stack([sum_high, sum_low])[None], ((0, 7), (0, D - 2)))
    grad_full, grad_cut = owned_grad(place_ids, pieces, dense, small.reshape(256, 512), extra)
    grad_parts = lax.all_to_all(grad_cut, AXES, 0, 0, tiled=True)

    ortho_cut = ortho_owned(place_ids, grad_full, moments)
    ortho_cut, grad_parts = lax.optimization_barrier((ortho_cut, grad_parts))
    ortho_parts = lax.all_to_all(ortho_cut, AXES, 0, 0, tiled=True)
    square_total = jnp.sum(grad_parts[:, 48, :2].astype(f32))

    step_value = step_count[0].astype(f32)
    decay = jnp.minimum(0.9999, (1.0 + step_value) / (10.0 + step_value))
    masters = (turned(w_square), turned(w_out), w_router, turned(w_up), turned(w_down))
    emas = (turned(ema_square), turned(ema_out), ema_router, turned(ema_up), turned(ema_down))
    updated = update(decay[None], grad_parts, ortho_parts, masters, moment_parts, emas)
    results = []
    for which in range(5):
        results += [
            array if which == 2 else turned(array) for array in updated[which::5]
        ]
    root_mean = jnp.sqrt(square_total / (6 * D) + 1e-05)
    master_bias = b_ada - RATE_VECTOR * state_bias / root_mean
    average_bias = decay * ema_bias + (1.0 - decay) * master_bias
    return (output, grad_in, *results, state_bias, master_bias, average_bias)


def solution(mesh):
    placed = (
        P((WIDE, NARROW), None),
        P((WIDE, NARROW), None),
        P((WIDE, NARROW), None),
        P((WIDE, NARROW)),
        P(),
        P((WIDE, NARROW), None),
        P(None, NARROW, WIDE),
        P(NARROW, WIDE),
        P(NARROW, WIDE),
        P(None, NARROW, WIDE),
        P(None, NARROW, WIDE),
        P((WIDE, NARROW)),
        P(None, NARROW, WIDE),
        P(NARROW, WIDE),
        P(NARROW, WIDE),
        P(None, NARROW, WIDE),
        P(None, NARROW, WIDE),
        P((WIDE, NARROW)),
        P(None, NARROW, WIDE),
        P(NARROW, WIDE),
        P(NARROW, WIDE),
        P(None, NARROW, WIDE),
        P(None, NARROW, WIDE),
        P((WIDE, NARROW)),
    )
    device_body = fast_device if dict(mesh.shape) == {WIDE: 8, NARROW: 4} else on_device
    return jax.shard_map(
        device_body,
        mesh=mesh,
        in_specs=placed,
        out_specs=(
            P((WIDE, NARROW), None),
            P((WIDE, NARROW), None),
            P(None, NARROW, WIDE),
            P(None, NARROW, WIDE),
            P(None, NARROW, WIDE),
            P(NARROW, WIDE),
            P(NARROW, WIDE),
            P(NARROW, WIDE),
            P(NARROW, WIDE),
            P(NARROW, WIDE),
            P(NARROW, WIDE),
            P(None, NARROW, WIDE),
            P(None, NARROW, WIDE),
            P(None, NARROW, WIDE),
            P(None, NARROW, WIDE),
            P(None, NARROW, WIDE),
            P(None, NARROW, WIDE),
            P((WIDE, NARROW)),
            P((WIDE, NARROW)),
            P((WIDE, NARROW)),
        ),
        check_vma=False,
    )
```

```python
from functools import partial

import jax
import jax.numpy as jnp
from jax import lax
from jax.experimental import pallas as pl
from jax.experimental.pallas import tpu as pltpu
from jax.sharding import PartitionSpec as P

WIDE, NARROW = "wide", "narrow"
D = 384
HEADS = 6
HEAD = 64
FF = 1536
TOP = 2
ROUTED = 8
SHORT = 256
LONG = 1024
CAP = 384


PRECISE = lax.Precision.HIGHEST
EPSILON = 1e-06
NS_FIRST = 3.4445
NS_SECOND = -4.775
NS_THIRD = 2.0315
MOMENTUM = 0.95
MOMENTUM_VECTOR = 0.5
RATE = 0.25
RATE_VECTOR = 0.05


def as_sent(array):

    def short(part):
        return part.astype(jnp.bfloat16) if part.dtype == jnp.float32 else part

    return jax.tree.map(short, array)


def modulate(seg_rows, shift_by, scale_by):
    center = seg_rows - jnp.mean(seg_rows, axis=-1, keepdims=True)
    normed = center * lax.rsqrt(jnp.mean(center * center, axis=-1, keepdims=True) + EPSILON)
    return normed * (1.0 + scale_by) + shift_by


def gelu_tanh(values):
    return jax.nn.gelu(values, approximate=True)


def gelu_grad(pre_act, upstream):
    _, pull_back = jax.vjp(gelu_tanh, pre_act)
    return pull_back(upstream)[0]


def slot_table(route_rows):
    flat_routes = route_rows.reshape(-1)
    hot_table = (flat_routes[:, None] == jnp.arange(ROUTED, dtype=jnp.int32)[None, :]).astype(
        jnp.int32
    )
    earlier = jnp.cumsum(hot_table, axis=0, dtype=jnp.int32) - hot_table
    place_in = jnp.sum(earlier * hot_table, axis=1, dtype=jnp.int32)
    slot_ids = flat_routes * CAP + place_in
    sources = jnp.arange(slot_ids.shape[0], dtype=jnp.int32) // TOP
    slot_owner = jnp.zeros((ROUTED * CAP,), jnp.int32).at[slot_ids].set(sources)
    return (slot_ids, slot_owner)


def attend(projected, length):
    image_count = projected.shape[1] // length
    split_parts = projected.reshape(3, image_count, length, HEADS, HEAD)
    scores = jnp.einsum(
        "bqhe,bkhe->bhqk", split_parts[0], split_parts[1], preferred_element_type=jnp.float32
    ) * HEAD ** (-0.5)
    highest = jnp.max(scores, axis=-1, keepdims=True)
    expo = jnp.exp(scores - highest)
    totals = jnp.sum(expo, axis=-1, keepdims=True)
    weights_low = (expo / totals).astype(jnp.bfloat16)
    mixed_heads = jnp.einsum(
        "bhqk,bkhe->bqhe", weights_low, split_parts[2], preferred_element_type=jnp.float32
    )
    log_total = (highest + jnp.log(totals))[..., 0]
    return (
        mixed_heads.reshape(-1, D).astype(jnp.bfloat16),
        jnp.transpose(log_total, (0, 2, 1)).reshape(-1, HEADS),
    )


def attend_back(projected, log_total, d_attended, length):
    image_count = projected.shape[1] // length
    split_parts = projected.reshape(3, image_count, length, HEADS, HEAD)
    scale_qk = HEAD ** (-0.5)
    scores = (
        jnp.einsum(
            "bqhe,bkhe->bhqk", split_parts[0], split_parts[1], preferred_element_type=jnp.float32
        )
        * scale_qk
    )
    log_four = jnp.transpose(log_total.reshape(image_count, length, HEADS), (0, 2, 1))[..., None]
    probs = jnp.exp(scores - log_four)
    weights_low = probs.astype(jnp.bfloat16)
    d_heads = d_attended.reshape(image_count, length, HEADS, HEAD)
    d_weights = jnp.einsum(
        "bqhe,bkhe->bhqk", d_heads, split_parts[2], preferred_element_type=jnp.float32
    )
    d_values = jnp.einsum(
        "bhqk,bqhe->bkhe", weights_low, d_heads, preferred_element_type=jnp.float32
    )
    d_scores = (probs * (d_weights - jnp.sum(d_weights * probs, axis=-1, keepdims=True))).astype(
        jnp.bfloat16
    )
    d_queries = (
        jnp.einsum("bhqk,bkhe->bqhe", d_scores, split_parts[1], preferred_element_type=jnp.float32)
        * scale_qk
    )
    d_keys = (
        jnp.einsum("bhqk,bqhe->bkhe", d_scores, split_parts[0], preferred_element_type=jnp.float32)
        * scale_qk
    )
    return jnp.stack([d_queries, d_keys, d_values]).reshape(3, -1, D).astype(jnp.bfloat16)


def on_device(
    tokens,
    conditions,
    routes,
    resolution,
    step_count,
    cotangent,
    w_square,
    w_out,
    w_router,
    w_up,
    w_down,
    b_ada,
    moment_square,
    moment_out,
    moment_router,
    moment_up,
    moment_down,
    moment_bias,
    ema_square,
    ema_out,
    ema_router,
    ema_up,
    ema_down,
    ema_bias,
):
    bf_type = jnp.bfloat16
    fl_type = jnp.float32
    row_pieces = (
        lax.all_gather(w_square.astype(bf_type), NARROW, axis=1, tiled=True),
        lax.all_gather(w_out.astype(bf_type), NARROW, axis=0, tiled=True),
        lax.all_gather(w_router.astype(bf_type), NARROW, axis=0, tiled=True),
        lax.all_gather(w_up.astype(bf_type), NARROW, axis=1, tiled=True),
        lax.all_gather(w_down.astype(bf_type), NARROW, axis=1, tiled=True),
        lax.all_gather(b_ada.astype(bf_type), NARROW, axis=0, tiled=True),
    )
    whole_low = (
        lax.all_gather(row_pieces[0], WIDE, axis=2, tiled=True),
        lax.all_gather(row_pieces[1], WIDE, axis=1, tiled=True),
        lax.all_gather(row_pieces[2], WIDE, axis=1, tiled=True),
        lax.all_gather(row_pieces[3], WIDE, axis=2, tiled=True),
        lax.all_gather(row_pieces[4], WIDE, axis=2, tiled=True),
        lax.all_gather(row_pieces[5], WIDE, axis=0, tiled=True),
    )
    square_low, out_low, router_low, up_low, down_low, bias_low = whole_low
    res_group = resolution[0]
    token_f = tokens.astype(fl_type)
    segments = tokens.shape[0] // SHORT
    seg_ratio = LONG // SHORT
    first_seg = jnp.arange(segments, dtype=jnp.int32) // seg_ratio * seg_ratio
    chosen = jnp.where(res_group == 1, conditions[first_seg], conditions)
    cond_low = jax.nn.silu(chosen.astype(fl_type)).astype(bf_type)
    modulation = jnp.einsum(
        "sd,jde->sje", cond_low, square_low[3:], preferred_element_type=fl_type
    ) + bias_low.astype(fl_type).reshape(6, D)
    seg_rows = token_f.reshape(segments, SHORT, D)
    first_mod, first_back = jax.vjp(modulate, seg_rows, modulation[:, 0:1], modulation[:, 1:2])
    hidden_one = first_mod.reshape(-1, D).astype(bf_type)
    projected = jnp.einsum(
        "td,jde->jte", hidden_one, square_low[:3], preferred_element_type=fl_type
    ).astype(bf_type)
    attended, log_total = lax.cond(
        res_group == 1, partial(attend, length=LONG), partial(attend, length=SHORT), projected
    )
    attn_out = jnp.dot(attended, out_low, preferred_element_type=fl_type)
    mid_state = token_f + (attn_out.reshape(segments, SHORT, D) * modulation[:, 2:3]).reshape(-1, D)
    second_mod, second_back = jax.vjp(
        modulate, mid_state.reshape(segments, SHORT, D), modulation[:, 3:4], modulation[:, 4:5]
    )
    hidden_two = second_mod.reshape(-1, D).astype(bf_type)
    logits = jnp.einsum("td,rd->tr", hidden_two, router_low, preferred_element_type=fl_type)
    gate_probs = jax.nn.softmax(jnp.take_along_axis(logits, routes, axis=1), axis=1)
    slot_ids, slot_owner = slot_table(routes)
    inputs = hidden_two[slot_owner].reshape(ROUTED, CAP, D)
    pre_act = jnp.einsum("ecd,efd->ecf", inputs, up_low[:ROUTED], preferred_element_type=fl_type)
    act_low = gelu_tanh(pre_act).astype(bf_type)
    produced = jnp.einsum(
        "ecf,efd->ecd", act_low, down_low[:ROUTED], preferred_element_type=fl_type
    ).reshape(-1, D)
    chosen_out = produced[slot_ids].reshape(-1, TOP, D)
    routed = jnp.sum(chosen_out * gate_probs[:, :, None], axis=1)
    shared_pre = jnp.einsum(
        "td,sfd->stf", hidden_two, up_low[ROUTED:], preferred_element_type=fl_type
    )
    shared_act = gelu_tanh(shared_pre).astype(bf_type)
    shared_out = jnp.einsum(
        "stf,sfd->std", shared_act, down_low[ROUTED:], preferred_element_type=fl_type
    )
    mixture = routed + jnp.sum(shared_out, axis=0)
    output = (
        mid_state + (mixture.reshape(segments, SHORT, D) * modulation[:, 5:6]).reshape(-1, D)
    ).astype(bf_type)
    again_rows = (
        lax.all_gather(w_square.astype(bf_type), NARROW, axis=1, tiled=True),
        lax.all_gather(w_out.astype(bf_type), NARROW, axis=0, tiled=True),
        lax.all_gather(w_router.astype(bf_type), NARROW, axis=0, tiled=True),
        lax.all_gather(w_up.astype(bf_type), NARROW, axis=1, tiled=True),
        lax.all_gather(w_down.astype(bf_type), NARROW, axis=1, tiled=True),
    )
    again_whole = (
        lax.all_gather(again_rows[0], WIDE, axis=2, tiled=True),
        lax.all_gather(again_rows[1], WIDE, axis=1, tiled=True),
        lax.all_gather(again_rows[2], WIDE, axis=1, tiled=True),
        lax.all_gather(again_rows[3], WIDE, axis=2, tiled=True),
        lax.all_gather(again_rows[4], WIDE, axis=2, tiled=True),
    )
    square_low, out_low, router_low, up_low, down_low = again_whole
    grad_out = cotangent.astype(fl_type)
    grad_seg = grad_out.reshape(segments, SHORT, D)
    d_gate_two = jnp.sum(grad_seg * mixture.reshape(segments, SHORT, D), axis=1)
    d_mixture = (grad_seg * modulation[:, 5:6]).reshape(-1, D)
    d_shared = d_mixture.astype(bf_type)
    d_shared_act = jnp.einsum(
        "td,sfd->stf", d_shared, down_low[ROUTED:], preferred_element_type=fl_type
    )
    d_shared_pre = gelu_grad(shared_pre, d_shared_act).astype(bf_type)
    g_shared_down = jnp.einsum("stf,td->sfd", shared_act, d_shared, preferred_element_type=fl_type)
    g_shared_up = jnp.einsum(
        "stf,td->sfd", d_shared_pre, hidden_two, preferred_element_type=fl_type
    )
    d_hidden = jnp.einsum(
        "stf,sfd->td", d_shared_pre, up_low[ROUTED:], preferred_element_type=fl_type
    )
    d_gates = jnp.sum(d_mixture[:, None, :] * chosen_out, axis=2)
    gate_slot = jnp.zeros((ROUTED * CAP,), fl_type).at[slot_ids].set(gate_probs.reshape(-1))
    d_produced = (
        (gate_slot[:, None] * d_mixture[slot_owner]).astype(bf_type).reshape(ROUTED, CAP, D)
    )
    d_act = jnp.einsum(
        "ecd,efd->ecf", d_produced, down_low[:ROUTED], preferred_element_type=fl_type
    )
    d_pre = gelu_grad(pre_act, d_act).astype(bf_type)
    g_routed_down = jnp.einsum("ecf,ecd->efd", act_low, d_produced, preferred_element_type=fl_type)
    g_routed_up = jnp.einsum("ecf,ecd->efd", d_pre, inputs, preferred_element_type=fl_type)
    d_inputs = jnp.einsum(
        "ecf,efd->ecd", d_pre, up_low[:ROUTED], preferred_element_type=fl_type
    ).reshape(-1, D)
    d_hidden = d_hidden + jnp.sum(d_inputs[slot_ids].reshape(-1, TOP, D), axis=1)
    d_picked = gate_probs * (d_gates - jnp.sum(gate_probs * d_gates, axis=1, keepdims=True))
    route_hot = (routes[:, :, None] == jnp.arange(ROUTED, dtype=jnp.int32)[None, None, :]).astype(
        fl_type
    )
    d_logits = jnp.sum(route_hot * d_picked[:, :, None], axis=1).astype(bf_type)
    g_router = jnp.einsum("tr,td->rd", d_logits, hidden_two, preferred_element_type=fl_type)
    d_hidden = d_hidden + jnp.einsum(
        "tr,rd->td", d_logits, router_low, preferred_element_type=fl_type
    )
    d_mid_norm, d_shift_two, d_scale_two = second_back(d_hidden.reshape(segments, SHORT, D))
    d_mid = grad_out + d_mid_norm.reshape(-1, D)
    d_gate_one = jnp.sum(
        d_mid.reshape(segments, SHORT, D) * attn_out.reshape(segments, SHORT, D), axis=1
    )
    d_attn = (d_mid.reshape(segments, SHORT, D) * modulation[:, 2:3]).reshape(-1, D).astype(bf_type)
    g_out = jnp.einsum("td,te->de", attended, d_attn, preferred_element_type=fl_type)
    d_attended = jnp.einsum("te,de->td", d_attn, out_low, preferred_element_type=fl_type).astype(
        bf_type
    )
    d_projected = lax.cond(
        res_group == 1,
        partial(attend_back, length=LONG),
        partial(attend_back, length=SHORT),
        projected,
        log_total,
        d_attended,
    )
    g_qkv = jnp.einsum("td,jte->jde", hidden_one, d_projected, preferred_element_type=fl_type)
    d_hidden_one = jnp.einsum(
        "jte,jde->td", d_projected, square_low[:3], preferred_element_type=fl_type
    )
    d_rows, d_shift_one, d_scale_one = first_back(d_hidden_one.reshape(segments, SHORT, D))
    grad_in = d_mid + d_rows.reshape(-1, D)
    d_modulation = jnp.stack(
        [
            d_shift_one[:, 0],
            d_scale_one[:, 0],
            d_gate_one,
            d_shift_two[:, 0],
            d_scale_two[:, 0],
            d_gate_two,
        ],
        axis=1,
    )
    g_ada = jnp.einsum("sd,sje->jde", cond_low.astype(fl_type), d_modulation, precision=PRECISE)
    g_bias = jnp.sum(d_modulation, axis=0).reshape(-1)
    g_square = jnp.concatenate([g_qkv, g_ada], axis=0)
    g_up = jnp.concatenate([g_routed_up, g_shared_up], axis=0)
    g_down = jnp.concatenate([g_routed_down, g_shared_down], axis=0)
    by_columns = (
        lax.psum_scatter(g_square, WIDE, scatter_dimension=2, tiled=True),
        lax.psum_scatter(g_out, WIDE, scatter_dimension=1, tiled=True),
        lax.psum_scatter(g_router, WIDE, scatter_dimension=1, tiled=True),
        lax.psum_scatter(g_up, WIDE, scatter_dimension=2, tiled=True),
        lax.psum_scatter(g_down, WIDE, scatter_dimension=2, tiled=True),
        lax.psum_scatter(g_bias, WIDE, scatter_dimension=0, tiled=True),
    )
    summed = (
        lax.psum_scatter(by_columns[0], NARROW, scatter_dimension=1, tiled=True),
        lax.psum_scatter(by_columns[1], NARROW, scatter_dimension=0, tiled=True),
        lax.psum_scatter(by_columns[2], NARROW, scatter_dimension=0, tiled=True),
        lax.psum_scatter(by_columns[3], NARROW, scatter_dimension=1, tiled=True),
        lax.psum_scatter(by_columns[4], NARROW, scatter_dimension=1, tiled=True),
        lax.psum_scatter(by_columns[5], NARROW, scatter_dimension=0, tiled=True),
    )
    state_square = MOMENTUM * moment_square + summed[0]
    state_out = MOMENTUM * moment_out + summed[1]
    state_router = MOMENTUM * moment_router + summed[2]
    state_up = MOMENTUM * moment_up + summed[3]
    state_down = MOMENTUM * moment_down + summed[4]
    local_rows = w_up.shape[1]

    def padded(block):
        return jnp.pad(block, ((0, 0), (0, local_rows - block.shape[1]), (0, 0)))

    stacked = jnp.concatenate(
        [
            padded(state_square),
            padded(state_out[None]),
            padded(state_router[None]),
            state_up,
            state_down,
        ],
        axis=0,
    )
    wide_count = lax.axis_size(WIDE)
    matrices = stacked.shape[0]
    per_owner = -(-matrices // wide_count)
    stacked = jnp.pad(stacked, ((0, per_owner * wide_count - matrices), (0, 0), (0, 0)))
    current = lax.all_to_all(stacked, WIDE, split_axis=0, concat_axis=2, tiled=True)
    for sweep_num in range(5):
        gram_mat = lax.psum(
            jnp.einsum("mrc,mrd->mcd", current, current, precision=PRECISE).astype(jnp.bfloat16),
            NARROW,
        ).astype(jnp.float32)
        if sweep_num == 0:
            factor = 1.0 / (jnp.sqrt(jnp.trace(gram_mat, axis1=1, axis2=2)) + 1e-07)
            current = current * factor[:, None, None]
            gram_mat = gram_mat * (factor * factor)[:, None, None]
        polynomial = NS_SECOND * gram_mat + NS_THIRD * jnp.einsum(
            "mcd,mde->mce", gram_mat, gram_mat, precision=PRECISE
        )
        current = NS_FIRST * current + jnp.einsum(
            "mrc,mcd->mrd", current, polynomial, precision=PRECISE
        )
    spread_back = lax.all_to_all(
        as_sent(current), WIDE, split_axis=2, concat_axis=0, tiled=True
    ).astype(current.dtype)[:matrices]
    expert_total = w_up.shape[0]
    small_factor = RATE * 0.2 * D**0.5
    large_factor = RATE * 0.2 * FF**0.5
    master_square = w_square - small_factor * spread_back[0:9, : w_square.shape[1]]
    master_out = w_out - small_factor * spread_back[9, : w_out.shape[0]]
    master_router = w_router - small_factor * spread_back[10, : w_router.shape[0]]
    master_up = w_up - large_factor * spread_back[11 : 11 + expert_total]
    master_down = w_down - large_factor * spread_back[11 + expert_total : 11 + 2 * expert_total]
    state_bias = MOMENTUM_VECTOR * moment_bias + summed[5]
    square_total = lax.psum(jnp.sum(state_bias * state_bias), (WIDE, NARROW))
    root_mean = jnp.sqrt(square_total / (6 * D) + 1e-05)
    master_bias = b_ada - RATE_VECTOR * state_bias / root_mean
    step_value = step_count[0].astype(fl_type)
    decay = jnp.minimum(0.9999, (1.0 + step_value) / (10.0 + step_value))
    average_square = decay * ema_square + (1.0 - decay) * master_square
    average_out = decay * ema_out + (1.0 - decay) * master_out
    average_router = decay * ema_router + (1.0 - decay) * master_router
    average_up = decay * ema_up + (1.0 - decay) * master_up
    average_down = decay * ema_down + (1.0 - decay) * master_down
    average_bias = decay * ema_bias + (1.0 - decay) * master_bias
    return (
        output,
        grad_in,
        state_square,
        master_square,
        average_square,
        state_out,
        master_out,
        average_out,
        state_router,
        master_router,
        average_router,
        state_up,
        master_up,
        average_up,
        state_down,
        master_down,
        average_down,
        state_bias,
        master_bias,
        average_bias,
    )


bf = jnp.bfloat16
f32 = jnp.float32
TOK = 1024
UNITS = 768
NN = (((1,), (0,)), ((), ()))
NT = (((1,), (1,)), ((), ()))
TN = (((0,), (0,)), ((), ()))


def dot(a, b, dims=NN):
    return lax.dot_general(a, b, dims, preferred_element_type=f32)


def gelu_pair(pre):
    sq = pre * pre
    th = jnp.tanh(pre * (0.7978845608028654 + 0.035677408136300125 * sq))
    half = 0.5 * th + 0.5
    act = pre * half
    slope = half + act * (1.0 - half) * (1.5957691216057308 + 0.21406444881780075 * sq)
    return act, slope


def units(xs, ds, up_ref, down_ref, g_up_ref, g_down_ref, count):
    out = jnp.zeros(xs.shape, f32)
    dx = jnp.zeros(xs.shape, f32)
    for first in range(0, count, UNITS):
        lanes = slice(first, min(first + UNITS, count))
        act, slope = gelu_pair(dot(xs, up_ref[:, lanes]))
        act = act.astype(bf)
        d_pre = (slope * dot(ds, down_ref[:, lanes])).astype(bf)
        out = out + dot(act, down_ref[:, lanes], NT)
        dx = dx + dot(d_pre, up_ref[:, lanes], NT)
        g_up_ref[:, lanes] += dot(xs, d_pre, TN)
        g_down_ref[:, lanes] += dot(ds, act, TN)
    return out, dx


def start_all(copies):
    copies = [pltpu.make_async_copy(*copy) for copy in copies]
    for copy in copies:
        copy.start()
    return copies


def wait_all(copies):
    for copy in copies:
        copy.wait()


def routed_kernel(ids, *refs):
    hidden, d_mix, metas, priors = refs[0:4], refs[4:8], refs[8:12], refs[12:16]
    gathered, mix_out, dx_out, d_gate_out = refs[16], refs[17:21], refs[21:25], refs[25]
    g_send, g_keep, g_second, g_third = refs[26:30]
    tok, meta, up, down, g_up, g_down, acc, part, d_gate, stage = refs[30:40]
    tok_sem, w_sem, out_sem, g_sem = refs[40:]
    n, x = ids[0], ids[2]
    loads = []
    for w in range(8):
        for e in range(2):
            for k in range(4):
                where = (e, pl.ds(48 * w, 48), pl.ds(k * D, D))
                loads.append((gathered.at[w, k, 2 * e], up.at[where], w_sem.at[0]))
                loads.append((gathered.at[w, k, 2 * e + 1], down.at[where], w_sem.at[0]))
    token_loads = []
    for i in range(4):
        token_loads.append((hidden[i], tok.at[i, :, pl.ds(0, D)], tok_sem.at[i, 0]))
        token_loads.append((d_mix[i], tok.at[i, :, pl.ds(D, D)], tok_sem.at[i, 1]))
        token_loads.append((metas[i], meta.at[i], tok_sem.at[i, 2]))
        token_loads.append((priors[i], part.at[i], tok_sem.at[i, 3]))
    loads = start_all(loads)
    start_all(token_loads)
    g_up[...] = jnp.zeros_like(g_up)
    g_down[...] = jnp.zeros_like(g_down)
    wait_all(loads)

    def results(i):
        return [
            pltpu.make_async_copy(part.at[i, :, pl.ds(0, D)], mix_out[i], out_sem.at[i]),
            pltpu.make_async_copy(part.at[i, :, pl.ds(D, D)], dx_out[i], out_sem.at[5 + i]),
        ]

    def one_source(s, carry):
        pltpu.make_async_copy(hidden[0], tok.at[s, :, pl.ds(0, D)], tok_sem.at[s, 0]).wait()
        pltpu.make_async_copy(d_mix[0], tok.at[s, :, pl.ds(D, D)], tok_sem.at[s, 1]).wait()
        pltpu.make_async_copy(metas[0], meta.at[s], tok_sem.at[s, 2]).wait()
        pltpu.make_async_copy(priors[0], part.at[s], tok_sem.at[s, 3]).wait()
        acc[...] = part[s].astype(f32)

        def routed(e, carry):
            place = meta[s, pl.ds(2 * n + e, 1), :]
            gate = meta[s, pl.ds(8 + 2 * n + e, 1), :]
            slot = lax.broadcasted_iota(jnp.int32, (CAP, TOK), 0).astype(f32)
            hit = slot == place
            hot = hit.astype(f32).astype(bf)
            gates = jnp.sum(jnp.where(hit, gate, 0.0), axis=1, keepdims=True)
            rows = dot(hot, tok[s])
            d_rows = rows[:, D:]
            xs, ds = rows[:, :D].astype(bf), (d_rows * gates).astype(bf)
            out, dx = units(xs, ds, up.at[e], down.at[e], g_up.at[e], g_down.at[e], FF)
            d_slot = jnp.sum(out * d_rows, axis=1, keepdims=True)
            d_gate[s, pl.ds(e, 1), :] = jnp.sum(
                jnp.where(hit, d_slot, 0.0), axis=0, keepdims=True
            )
            both = jnp.concatenate([(out * gates).astype(bf), dx.astype(bf)], axis=1)
            acc[...] += dot(hot, both, TN)
            return carry

        lax.fori_loop(0, 2, routed, 0)
        part[s] = acc[...].astype(bf)
        for i in range(4):

            @pl.when(s == i)
            def _():
                for copy in results(i):
                    copy.start()

        return carry

    lax.fori_loop(0, 4, one_source, 0)
    outs = start_all([(d_gate, d_gate_out, out_sem.at[4])])
    for i in range(4):
        outs += results(i)
    for e in range(2):
        stage[2 * e] = g_up[e].astype(bf)
        stage[2 * e + 1] = g_down[e].astype(bf)

    @pl.when(x == 0)
    def _():
        wait_all(
            start_all([(stage.at[0], g_keep, g_sem.at[0]), (stage.at[3], g_send, g_sem.at[1])])
        )

    @pl.when(x != 0)
    def _():
        wait_all(
            start_all([(stage.at[3], g_keep, g_sem.at[0]), (stage.at[0], g_send, g_sem.at[1])])
        )

    outs += start_all(
        [(stage.at[1], g_second, g_sem.at[2]), (stage.at[2], g_third, g_sem.at[3])]
    )
    wait_all(outs)


def shared_kernel(*refs):
    hidden, d_mix, gathered, part_out, g_out = refs[0:4], refs[4:8], refs[8], refs[9:13], refs[13]
    tok, up, down, g_up, g_down, part, stage, tok_sem, w_sem, out_sem = refs[14:]
    loads = []
    for w in range(8):
        for s in range(2):
            where = (pl.ds(48 * w, 48), pl.ds(s * D, D))
            loads.append((gathered.at[w, 4, 2 * s], up.at[where], w_sem.at[0]))
            loads.append((gathered.at[w, 4, 2 * s + 1], down.at[where], w_sem.at[0]))
    loads = start_all(loads)
    token_loads = []
    for i in range(4):
        token_loads.append((hidden[i], tok.at[i, :, pl.ds(0, D)], tok_sem.at[i, 0]))
        token_loads.append((d_mix[i], tok.at[i, :, pl.ds(D, D)], tok_sem.at[i, 1]))
    start_all(token_loads)
    g_up[...] = jnp.zeros_like(g_up)
    g_down[...] = jnp.zeros_like(g_down)
    wait_all(loads)
    def one_source(i, carry):
        pltpu.make_async_copy(hidden[0], tok.at[i, :, pl.ds(0, D)], tok_sem.at[i, 0]).wait()
        pltpu.make_async_copy(d_mix[0], tok.at[i, :, pl.ds(D, D)], tok_sem.at[i, 1]).wait()
        out, dx = units(tok[i, :, :D], tok[i, :, D:], up, down, g_up, g_down, 2 * D)
        part[i, :, :D] = out.astype(bf)
        part[i, :, D:] = dx.astype(bf)
        for k in range(4):

            @pl.when(i == k)
            def _():
                pltpu.make_async_copy(part.at[k], part_out[k], out_sem.at[k]).start()

        return carry

    lax.fori_loop(0, 4, one_source, 0)
    outs = [pltpu.make_async_copy(part.at[k], part_out[k], out_sem.at[k]) for k in range(4)]
    for s in range(2):
        stage[:, 2 * s * D : 2 * s * D + D] = g_up[:, s * D : s * D + D].astype(bf)
        stage[:, 2 * s * D + D : 2 * s * D + 2 * D] = g_down[:, s * D : s * D + D].astype(bf)
    wait_all(outs + start_all([(stage, g_out, w_sem.at[1])]))


def routed_experts(ids, hidden, d_mix, metas, priors, gathered):
    anyspec = pl.BlockSpec(memory_space=pl.ANY)
    hbm = pl.BlockSpec(memory_space=pltpu.HBM)
    whole = jax.ShapeDtypeStruct((D, FF), bf)
    shapes = [jax.ShapeDtypeStruct((TOK, D), bf)] * 8
    shapes += [jax.ShapeDtypeStruct((4, 8, TOK), f32)] + [whole] * 4
    return pl.pallas_call(
        routed_kernel,
        out_shape=shapes,
        in_specs=[pl.BlockSpec(memory_space=pltpu.SMEM)] + [anyspec] * 17,
        out_specs=[hbm] * len(shapes),
        scratch_shapes=[
            pltpu.VMEM((4, TOK, 2 * D), bf),
            pltpu.VMEM((4, 16, TOK), f32),
            pltpu.VMEM((2, D, FF), bf),
            pltpu.VMEM((2, D, FF), bf),
            pltpu.VMEM((2, D, FF), f32),
            pltpu.VMEM((2, D, FF), f32),
            pltpu.VMEM((TOK, 2 * D), f32),
            pltpu.VMEM((4, TOK, 2 * D), bf),
            pltpu.VMEM((4, 8, TOK), f32),
            pltpu.VMEM((4, D, FF), bf),
            pltpu.SemaphoreType.DMA((4, 4)),
            pltpu.SemaphoreType.DMA((1,)),
            pltpu.SemaphoreType.DMA((9,)),
            pltpu.SemaphoreType.DMA((4,)),
        ],
        compiler_params=pltpu.CompilerParams(vmem_limit_bytes=58 * 1024 * 1024),
        name="routed_experts",
    )(ids, *hidden, *d_mix, *metas, *priors, gathered)


def shared_units(hidden, d_mix, gathered):
    anyspec = pl.BlockSpec(memory_space=pl.ANY)
    hbm = pl.BlockSpec(memory_space=pltpu.HBM)
    shapes = [jax.ShapeDtypeStruct((TOK, 2 * D), bf)] * 4 + [jax.ShapeDtypeStruct((D, FF), bf)]
    return pl.pallas_call(
        shared_kernel,
        out_shape=shapes,
        in_specs=[anyspec] * 9,
        out_specs=[hbm] * 5,
        scratch_shapes=[
            pltpu.VMEM((4, TOK, 2 * D), bf),
            pltpu.VMEM((D, 2 * D), bf),
            pltpu.VMEM((D, 2 * D), bf),
            pltpu.VMEM((D, 2 * D), f32),
            pltpu.VMEM((D, 2 * D), f32),
            pltpu.VMEM((4, TOK, 2 * D), bf),
            pltpu.VMEM((D, FF), bf),
            pltpu.SemaphoreType.DMA((4, 2)),
            pltpu.SemaphoreType.DMA((2,)),
            pltpu.SemaphoreType.DMA((4,)),
        ],
        compiler_params=pltpu.CompilerParams(vmem_limit_bytes=58 * 1024 * 1024),
        name="shared_units",
    )(*hidden, *d_mix, gathered)


def head_only(block, head):
    lane = lax.broadcasted_iota(jnp.int32, block.shape, 1)
    return jnp.where((lane >= 64) == (head == 1), block, jnp.zeros_like(block))


def attend_kernel(res, q_ref, k_ref, v_ref, o_ref, lse_ref, vt_ref):
    qb = pl.program_id(1)

    @pl.when(qb == 0)
    def _():
        vt_ref[...] = v_ref[...].T

    def work(rows):
        q = q_ref[...] * 0.125
        outs = []
        for head in range(2):
            scores = dot(k_ref[rows, :], head_only(q, head), NT)
            top = jnp.max(scores, axis=0, keepdims=True)
            expo = jnp.exp(scores - top)
            total = jnp.sum(expo, axis=0, keepdims=True)
            weights = (expo * (1.0 / total)).astype(bf)
            outs.append(dot(vt_ref[head * 64 : head * 64 + 64, rows], weights))
            lse_ref[0, head : head + 1, :] = top + jnp.log(total)
        o_ref[...] = jnp.concatenate(outs, axis=0).T.astype(bf)

    @pl.when(res[0] == 1)
    def _():
        work(pl.ds(0, TOK))

    @pl.when(res[0] != 1)
    def _():
        work(pl.ds(pl.multiple_of(qb * 256, 256), 256))


def attend_fast(resolution, projected):
    return pl.pallas_call(
        attend_kernel,
        grid_spec=pltpu.PrefetchScalarGridSpec(
            num_scalar_prefetch=1,
            grid=(3, 4),
            in_specs=[
                pl.BlockSpec((256, 128), lambda h, i, r: (i, h)),
                pl.BlockSpec((TOK, 128), lambda h, i, r: (0, 3 + h)),
                pl.BlockSpec((TOK, 128), lambda h, i, r: (0, 6 + h)),
            ],
            out_specs=[
                pl.BlockSpec((256, 128), lambda h, i, r: (i, h)),
                pl.BlockSpec((1, 8, 256), lambda h, i, r: (h, 0, i)),
            ],
            scratch_shapes=[pltpu.VMEM((128, TOK), bf)],
        ),
        out_shape=(
            jax.ShapeDtypeStruct((TOK, D), bf),
            jax.ShapeDtypeStruct((3, 8, TOK), f32),
        ),
        compiler_params=pltpu.CompilerParams(vmem_limit_bytes=48 * 1024 * 1024),
        name="attend_fast",
    )(resolution, projected, projected, projected)


def attend_back_kernel(
    res, q_ref, k_ref, v_ref, do_ref, lse_ref, dq_ref, dk_ref, dv_ref, kt_ref, dk_acc, dv_acc
):
    qb = pl.program_id(1)

    @pl.when(qb == 0)
    def _():
        kt_ref[...] = k_ref[...].T

    def work(rows, whole):
        q = q_ref[...] * 0.125
        grads = []
        dk = dv = None
        for head in range(2):
            qh = head_only(q, head)
            doh = head_only(do_ref[...], head)
            scores = dot(k_ref[rows, :], qh, NT)
            probs = jnp.exp(scores - lse_ref[0, head : head + 1, :])
            d_weights = dot(v_ref[rows, :], doh, NT)
            delta = jnp.sum(d_weights * probs, axis=0, keepdims=True)
            d_scores = (probs * (d_weights - delta)).astype(bf)
            dv_one = dot(probs.astype(bf), doh)
            dk_one = dot(d_scores, qh)
            dv = dv_one if dv is None else dv + dv_one
            dk = dk_one if dk is None else dk + dk_one
            grads.append(dot(kt_ref[head * 64 : head * 64 + 64, rows], d_scores))
        dq_ref[...] = (jnp.concatenate(grads, axis=0).T * 0.125).astype(bf)
        if not whole:
            dk_ref[rows, :] = dk.astype(bf)
            dv_ref[rows, :] = dv.astype(bf)
            return

        @pl.when(qb == 0)
        def _():
            dk_acc[...] = dk
            dv_acc[...] = dv

        @pl.when(qb != 0)
        def _():
            dk_acc[...] += dk
            dv_acc[...] += dv

        @pl.when(qb == 3)
        def _():
            dk_ref[...] = dk_acc[...].astype(bf)
            dv_ref[...] = dv_acc[...].astype(bf)

    @pl.when(res[0] == 1)
    def _():
        work(pl.ds(0, TOK), True)

    @pl.when(res[0] != 1)
    def _():
        work(pl.ds(pl.multiple_of(qb * 256, 256), 256), False)


def attend_back_fast(resolution, projected, lse, d_attended):
    return pl.pallas_call(
        attend_back_kernel,
        grid_spec=pltpu.PrefetchScalarGridSpec(
            num_scalar_prefetch=1,
            grid=(3, 4),
            in_specs=[
                pl.BlockSpec((256, 128), lambda h, i, r: (i, h)),
                pl.BlockSpec((TOK, 128), lambda h, i, r: (0, 3 + h)),
                pl.BlockSpec((TOK, 128), lambda h, i, r: (0, 6 + h)),
                pl.BlockSpec((256, 128), lambda h, i, r: (i, h)),
                pl.BlockSpec((1, 8, 256), lambda h, i, r: (h, 0, i)),
            ],
            out_specs=[
                pl.BlockSpec((256, 128), lambda h, i, r: (i, h)),
                pl.BlockSpec((TOK, 128), lambda h, i, r: (0, h)),
                pl.BlockSpec((TOK, 128), lambda h, i, r: (0, h)),
            ],
            scratch_shapes=[
                pltpu.VMEM((128, TOK), bf),
                pltpu.VMEM((TOK, 128), f32),
                pltpu.VMEM((TOK, 128), f32),
            ],
        ),
        out_shape=[jax.ShapeDtypeStruct((TOK, D), bf)] * 3,
        compiler_params=pltpu.CompilerParams(vmem_limit_bytes=48 * 1024 * 1024),
        name="attend_back_fast",
    )(resolution, projected, projected, projected, d_attended, lse)


def halves(value):
    high = value.astype(bf)
    return high, (value - high.astype(f32)).astype(bf)


def dot_three(a, b, dims=NN):
    return dot(a[0], b[0], dims) + dot(a[0], b[1], dims) + dot(a[1], b[0], dims)


def up_owner(e):
    return (24 if e % 2 else 0) + e // 2 if e < 8 else 20 + 2 * (e - 8)


def down_owner(e):
    return (4 if e % 2 else 16) + e // 2 if e < 8 else 21 + 2 * (e - 8)


def square_owner(j):
    return 8 + j if j < 3 else (9 + j if j < 7 else 21 + j)


OUT_OWNER, ROUTER_OWNER = 11, 30


def pack_kernel(square, out, router, up, down, packed):
    for e in range(10):
        packed[up_owner(e)] = up[e]
        packed[down_owner(e)] = down[e]
    rest = jnp.zeros((48, D - 96), f32)
    for j in range(9):
        packed[square_owner(j)] = jnp.concatenate([square[j], rest], axis=1)
    packed[OUT_OWNER] = jnp.concatenate([out[...], rest], axis=1)
    packed[ROUTER_OWNER] = router[...]
    packed[31] = jnp.zeros((48, D), f32)


def pack_owned(square, out, router, up, down):
    vmem = pl.BlockSpec(memory_space=pltpu.VMEM)
    return pl.pallas_call(
        pack_kernel,
        out_shape=jax.ShapeDtypeStruct((32, 48, D), f32),
        in_specs=[vmem] * 5,
        out_specs=vmem,
        name="pack_owned",
    )(square, out, router, up, down)


def owned_grad_kernel(ids, *refs):
    pieces = refs[:6]
    dense, small, extra, full_out, cut_out, buf, sems = refs[6:]
    n, z, x = ids[0], ids[1], ids[2]
    is_small = (z == 1) | ((z == 3) & (x == 1))
    for group, owner in enumerate((0, 2, 3)):

        @pl.when((z == owner) & jnp.logical_not(is_small))
        def _():
            copies = [
                pltpu.make_async_copy(pieces[2 * group + i], buf.at[i], sems.at[i])
                for i in range(2)
            ]
            for copy in copies:
                copy.start()
            for copy in copies:
                copy.wait()

    @pl.when(jnp.logical_not(is_small))
    def _():
        for k in range(4):
            lanes = slice(k * D, k * D + D)
            full_out[k] = buf[0, :, lanes].astype(f32) + buf[1, :, lanes].astype(f32)

    @pl.when(is_small)
    def _():
        rows = small[...].reshape(32, 8, 512)

        def place(matrix, width):
            rest = jnp.zeros((D, D - width), f32)
            for m in range(4):
                part = matrix[:, m * width : m * width + width]
                full_out[m ^ n] = jnp.concatenate([part, rest], axis=1)

        @pl.when(z == 1)
        def _():
            @pl.when(x == 0)
            def _():
                place(dense[...], 96)

        @pl.when(jnp.logical_not((z == 1) & (x == 0)))
        def _():
            is_router = (z == 3) & (n == 2)

            @pl.when(is_router)
            def _():
                summed = jnp.sum(rows[:, :, :D], axis=0)
                place(jnp.concatenate([summed, jnp.zeros((120, D), f32)], axis=0).T[:, :8], 2)

            @pl.when(jnp.logical_not(is_router))
            def _():
                first = (lax.broadcasted_iota(jnp.int32, (256, D), 0) % 8) < 4
                both = small[:, :D]
                mods = jnp.where(first, both, 0.0)
                conds = pltpu.roll(both, 252, 0)
                conds = jnp.where(first, conds, 0.0)
                place(dot_three(halves(mods), halves(conds), TN), 96)

    for w in range(8):
        for m in range(4):
            cut_out[4 * w + m, :48] = full_out[m ^ n, 48 * w : 48 * w + 48, :].astype(bf)
            cut_out[4 * w + m, 48:] = extra[...]


def owned_grad(ids, pieces, dense, small, extra):
    anyspec, vmem = pl.BlockSpec(memory_space=pltpu.HBM), pl.BlockSpec(memory_space=pltpu.VMEM)
    return pl.pallas_call(
        owned_grad_kernel,
        out_shape=(
            jax.ShapeDtypeStruct((4, D, D), f32),
            jax.ShapeDtypeStruct((32, 56, D), bf),
        ),
        in_specs=[pl.BlockSpec(memory_space=pltpu.SMEM)] + [anyspec] * 6 + [vmem] * 3,
        out_specs=[vmem, vmem],
        scratch_shapes=[pltpu.VMEM((2, D, FF), bf), pltpu.SemaphoreType.DMA((2,))],
        compiler_params=pltpu.CompilerParams(vmem_limit_bytes=40 * 1024 * 1024),
        name="owned_grad",
    )(ids, *pieces, dense, small, extra)


def ortho_kernel(ids, grad, moment, cut_out, cur, high, low, cross):
    n = ids[0]
    for k in range(4):
        cur[k] = grad[k]
    for w in range(8):
        rows = slice(48 * w, 48 * w + 48)
        for m in range(4):
            cur[m ^ n, rows, :] += MOMENTUM * moment[4 * w + m]
    total = jnp.zeros((1, D), f32)
    for k in range(4):
        total = total + jnp.sum(cur[k] * cur[k], axis=0, keepdims=True)
    factor = 1.0 / (jnp.sqrt(jnp.sum(total, axis=1, keepdims=True)) + 1e-07)

    def keep(k, value):
        cur[k] = value
        high[:, k * D : k * D + D], low[:, k * D : k * D + D] = halves(value)

    for k in range(4):
        keep(k, cur[k] * factor)

    def sweep(_, carry):
        cross[...] = dot(high[...], low[...], NT)
        gram = dot(high[...], high[...], NT) + (cross[...] + cross[...].T)
        gram_high, gram_low = halves(gram)
        cross[...] = dot(gram_high, gram_low)
        square = dot(gram_high, gram_high) + (cross[...] + cross[...].T)
        poly = halves(NS_SECOND * gram + NS_THIRD * square)
        for pair in range(0, 4, 4):
            lanes = slice(pair * D, pair * D + 4 * D)
            step = dot_three(poly, (high[:, lanes], low[:, lanes]))
            for k in range(4):
                keep(pair + k, NS_FIRST * cur[pair + k] + step[:, k * D : k * D + D])
        return carry

    lax.fori_loop(0, 5, sweep, 0)
    for w in range(8):
        for m in range(4):
            cut_out[4 * w + m] = cur[m ^ n, 48 * w : 48 * w + 48, :].astype(bf)


def ortho_owned(ids, grad, moment):
    vmem = pl.BlockSpec(memory_space=pltpu.VMEM)
    return pl.pallas_call(
        ortho_kernel,
        out_shape=jax.ShapeDtypeStruct((32, 48, D), bf),
        in_specs=[pl.BlockSpec(memory_space=pltpu.SMEM), vmem, vmem],
        out_specs=vmem,
        scratch_shapes=[
            pltpu.VMEM((4, D, D), f32),
            pltpu.VMEM((D, FF), bf),
            pltpu.VMEM((D, FF), bf),
            pltpu.VMEM((D, D), f32),
        ],
        compiler_params=pltpu.CompilerParams(vmem_limit_bytes=40 * 1024 * 1024),
        name="ortho_owned",
    )(ids, grad, moment)


def update_kernel(decay_ref, grads, orthos, *refs):
    decay = decay_ref[0]
    weights, moments, emas = refs[0:5], refs[5:10], refs[10:15]
    states, masters, averages = refs[15:20], refs[20:25], refs[25:30]
    small_rate, large_rate = RATE * 0.2 * D**0.5, RATE * 0.2 * FF**0.5

    def step(which, at, grad, ortho, rate):
        states[which][at] = MOMENTUM * moments[which][at] + grad.astype(f32)
        master = weights[which][at] - rate * ortho.astype(f32)
        masters[which][at] = master
        averages[which][at] = decay * emas[which][at] + (1.0 - decay) * master

    for j in range(9):
        own = square_owner(j)
        step(0, j, grads[own, :48, :96], orthos[own, :48, :96], small_rate)
    step(1, slice(None), grads[OUT_OWNER, :48, :96], orthos[OUT_OWNER, :48, :96], small_rate)

    def router_rows(source):
        return source[ROUTER_OWNER, :48, :128].astype(f32).T[:2]

    step(2, slice(None), router_rows(grads), router_rows(orthos), small_rate)
    for e in range(10):
        step(3, e, grads[up_owner(e), :48], orthos[up_owner(e), :48], large_rate)
        step(4, e, grads[down_owner(e), :48], orthos[down_owner(e), :48], large_rate)


def update(decay, grads, orthos, weights, moments, emas):
    vmem = pl.BlockSpec(memory_space=pltpu.VMEM)
    shapes = [jax.ShapeDtypeStruct(weight.shape, f32) for weight in weights]
    return pl.pallas_call(
        update_kernel,
        out_shape=shapes * 3,
        in_specs=[pl.BlockSpec(memory_space=pltpu.SMEM)] + [vmem] * 17,
        out_specs=[vmem] * 15,
        compiler_params=pltpu.CompilerParams(vmem_limit_bytes=48 * 1024 * 1024),
        name="update",
    )(decay, grads, orthos, *weights, *moments, *emas)


def first_back_kernel(
    ids, dq, dk, dv, hidden, tokens, d_mid, maps, scales, g_out, mods, cond, g_router, *refs
):
    grad_in, keep, out_send, payload, g_acc, sums = refs
    i = pl.program_id(0)
    heads = (dq, dk, dv)
    d_hidden = jnp.zeros((SHORT, D), f32)
    for j in range(3):
        d_hidden = d_hidden + dot(heads[j][...], maps[j * D : j * D + D, :])

    @pl.when(i == 0)
    def _():
        for j in range(3):
            g_acc[j] = dot(heads[j][...], hidden[...], TN)

    @pl.when(i != 0)
    def _():
        for j in range(3):
            g_acc[j] += dot(heads[j][...], hidden[...], TN)

    rows = tokens[...].astype(f32)
    center = rows - jnp.mean(rows, axis=1, keepdims=True)
    inverse = lax.rsqrt(jnp.mean(center * center, axis=1, keepdims=True) + EPSILON)
    normed = center * inverse
    d_normed = d_hidden * (1.0 + scales[pl.ds(i, 1), :])
    inner = d_normed - jnp.mean(d_normed, axis=1, keepdims=True)
    inner = inner - normed * jnp.mean(d_normed * normed, axis=1, keepdims=True)
    grad_in[...] = d_mid[...] + inverse * inner
    sums[0, pl.ds(i, 1), :] = jnp.sum(d_hidden, axis=0, keepdims=True)
    sums[1, pl.ds(i, 1), :] = jnp.sum(d_hidden * normed, axis=0, keepdims=True)

    @pl.when(i == 3)
    def _():
        c = lax.rem(ids[0], 2)
        for m in range(4):

            def total(m=m):
                return g_acc[m] if m < 3 else g_out[...]

            @pl.when(c == m % 2)
            def _():
                keep[m // 2] = total()

            @pl.when(c != m % 2)
            def _():
                out_send[m // 2] = total().astype(bf)

        rows = [sums[0, :4, :], sums[1, :4, :]] + [mods[j] for j in range(4)]
        payload[...] = jnp.zeros_like(payload)
        for j, slot in enumerate((12, 13, 14, 15, 28, 29)):
            payload[slot, :4, :D] = rows[j]
            payload[slot, 4:, :D] = cond[...]
        payload[30, :, :D] = g_router[...]
        bias = jnp.concatenate([jnp.sum(row, axis=0, keepdims=True) for row in rows], axis=1)
        for slot in range(32):
            payload[slot, 0:1, D : D + 72] = bias[:, slot * 72 : slot * 72 + 72]


def first_back_fast(ids, d_heads, hidden, tokens, d_mid, maps, scales, g_out, mods, cond, g_router):
    block = pl.BlockSpec((SHORT, D), lambda i: (i, 0))

    def whole(*shape):
        return pl.BlockSpec(shape, lambda i: (0,) * len(shape))

    return pl.pallas_call(
        first_back_kernel,
        grid=(4,),
        out_shape=(
            jax.ShapeDtypeStruct((TOK, D), f32),
            jax.ShapeDtypeStruct((2, D, D), f32),
            jax.ShapeDtypeStruct((2, D, D), bf),
            jax.ShapeDtypeStruct((32, 8, 512), f32),
        ),
        in_specs=[pl.BlockSpec(memory_space=pltpu.SMEM)]
        + [block] * 6
        + [
            whole(3 * D, D),
            whole(4, D),
            whole(D, D),
            whole(4, 4, D),
            whole(4, D),
            whole(8, D),
        ],
        out_specs=[block, whole(2, D, D), whole(2, D, D), whole(32, 8, 512)],
        scratch_shapes=[pltpu.VMEM((3, D, D), f32), pltpu.VMEM((2, 8, D), f32)],
        compiler_params=pltpu.CompilerParams(vmem_limit_bytes=40 * 1024 * 1024),
        name="first_back",
    )(ids, *d_heads, hidden, tokens, d_mid, maps, scales, g_out, mods, cond, g_router)


AXES = (WIDE, NARROW)


def route_pairs(move):
    pairs = []
    for index in range(32):
        w, n = divmod(index, 4)
        target = move(w // 2, w % 2, n // 2, n % 2)
        if target is not None:
            z, x, y, c = target
            pairs.append((index, (z * 2 + x) * 4 + y * 2 + c))
    return pairs


def send(array, move):
    return lax.ppermute(array, AXES, route_pairs(move))


def to_core(z, x, y, c):
    return (z, x, y, 1 - c)


def to_y(z, x, y, c):
    return (z, x, 1 - y, c)


def to_diag(z, x, y, c):
    return (z, x, 1 - y, 1 - c)


def to_x(z, x, y, c):
    return (z, 1 - x, y, c)


def to_z(step):
    return lambda z, x, y, c: ((z + step) % 4, x, y, c)


NARROW_MOVES = (None, to_core, to_y, to_diag)


def pick(array, index, axis=0):
    return lax.dynamic_index_in_dim(array, index, axis, keepdims=False)


def in_order(mine, other, flag):
    return jnp.where(flag == 0, mine, other), jnp.where(flag == 0, other, mine)


def xor_blocks(array, axis, y, c):
    parts = [lax.index_in_dim(array, i, axis, keepdims=True) for i in range(4)]
    parts = [jnp.where(c == 0, parts[i], parts[i ^ 1]) for i in range(4)]
    parts = [jnp.where(y == 0, parts[i], parts[i ^ 2]) for i in range(4)]
    return jnp.concatenate(parts, axis=axis)


def gather_z(rows, z):
    ring = jnp.stack([send(rows, to_z(step)) for step in (3, 2, 1)] + [rows])
    return lax.dynamic_slice_in_dim(jnp.concatenate([ring, ring]), (3 - z) % 4, 4, 0)


def gather_core(by_z, received, x, c):
    by_zx = jnp.stack(in_order(by_z, received, x), axis=1)
    return jnp.stack(in_order(by_zx, send(by_zx, to_core), c), axis=2)


def lanes_to(block, width):
    return jnp.pad(block, [(0, 0)] * (block.ndim - 1) + [(0, width - block.shape[-1])])


def turned(array):
    return jnp.swapaxes(array, -1, -2)


def fast_device(
    tokens,
    conditions,
    routes,
    resolution,
    step_count,
    cotangent,
    w_square,
    w_out,
    w_router,
    w_up,
    w_down,
    b_ada,
    moment_square,
    moment_out,
    moment_router,
    moment_up,
    moment_down,
    moment_bias,
    ema_square,
    ema_out,
    ema_router,
    ema_up,
    ema_down,
    ema_bias,
):
    wide = lax.axis_index(WIDE)
    narrow = lax.axis_index(NARROW)
    z, x = wide // 2, wide % 2
    y, c = narrow // 2, narrow % 2

    up_t = turned(w_up).astype(bf)
    down_t = turned(w_down).astype(bf)
    routed_t = jnp.stack([up_t[:8], down_t[:8]], axis=1).reshape(4, 4, 48, D)
    shared_t = jnp.stack([up_t[8:], down_t[8:]], axis=1).reshape(4, 48, D)
    square_t = turned(w_square).astype(bf)
    out_t = turned(w_out).astype(bf)[None]
    misc = jnp.concatenate(
        [
            lanes_to(b_ada.astype(bf)[None], 96),
            lanes_to(w_router.astype(bf), 96),
            jnp.zeros((5, 96), bf),
        ]
    )
    flat = jnp.concatenate(
        [
            square_t[:5].reshape(-1, 96),
            misc,
            square_t[5:].reshape(-1, 96),
            out_t.reshape(-1, 96),
        ]
    )
    lanes = jnp.stack([flat] + [send(flat, move) for move in NARROW_MOVES[1:]])
    rows = jnp.concatenate(list(xor_blocks(lanes, 0, y, c)), axis=1)

    moment_parts = (
        turned(moment_square),
        turned(moment_out),
        moment_router,
        turned(moment_up),
        turned(moment_down),
    )
    router_block = lanes_to(turned(moment_router), D)
    moments = pack_owned(*moment_parts[:2], router_block, *moment_parts[3:])

    def my_half(block):
        return pick(block.reshape(5, 2, 24, D), c, 1).reshape(120, D)

    mine = [pick(routed_t, narrow)]
    mine += [send(pick(routed_t, narrow ^ k), NARROW_MOVES[k]) for k in (1, 2, 3)]
    first_rows = jnp.concatenate([my_half(rows[:240]), rows[240:248]])
    first_z = gather_z(first_rows, z)
    first_z, blocks = lax.optimization_barrier((first_z, jnp.stack(mine + [shared_t])))
    gathered = lax.all_gather(blocks, WIDE)
    first_x = send(first_z, to_x)
    first_x, second_rows, moments = lax.optimization_barrier((first_x, rows[248:], moments))
    second_z = gather_z(my_half(second_rows), z)
    first_all = gather_core(first_z, first_x, x, c)
    second_all = gather_core(second_z, send(second_z, to_x), x, c)

    def assemble(gathered):
        parts = gathered[..., :120, :].reshape(8, 2, 5, 24, D)
        return jnp.transpose(parts, (2, 0, 1, 3, 4)).reshape(5, D, D)

    first_maps = assemble(first_all)
    second_maps = assemble(second_all)
    misc_all = first_all[:, :, 0, 120:, :].reshape(8, 8, 4, 96)
    bias_low = misc_all[:, 0, :, :72].reshape(-1)
    router_low = jnp.transpose(misc_all[:, 1:3, :, :48], (2, 1, 0, 3)).reshape(ROUTED, D)

    res_group = resolution[0]
    token_f = tokens.astype(f32)
    segments = tokens.shape[0] // SHORT
    seg_ratio = LONG // SHORT
    first_seg = jnp.arange(segments, dtype=jnp.int32) // seg_ratio * seg_ratio
    chosen = jnp.where(res_group == 1, conditions[first_seg], conditions)
    cond_low = jax.nn.silu(chosen.astype(f32)).astype(bf)
    bias_rows = bias_low.astype(f32).reshape(6, D)

    def modulation_of(maps, bias):
        return dot(cond_low, maps.reshape(-1, D), NT).reshape(segments, -1, D) + bias

    first_two = modulation_of(first_maps[3:], bias_rows[:2])
    last_four = modulation_of(second_maps[:4], bias_rows[2:])
    out_map = second_maps[4]
    seg_rows = token_f.reshape(segments, SHORT, D)
    first_mod = modulate(seg_rows, first_two[:, 0:1], first_two[:, 1:2])
    hidden_one = first_mod.reshape(-1, D).astype(bf)
    query_maps = first_maps[:3].reshape(3 * D, D)
    projected = dot(hidden_one, query_maps, NT).astype(bf)
    gate_one, gate_two = last_four[:, 0:1], last_four[:, 3:4]
    grad_out = cotangent.astype(f32)
    grad_seg = grad_out.reshape(segments, SHORT, D)
    d_mixture = (grad_seg * gate_two).reshape(-1, D).astype(bf)
    d_mix_core = send(d_mixture, to_core)
    d_mix_y = send(d_mixture, to_y)
    attended, log_total = attend_fast(resolution, projected)
    attended, d_mix_y = lax.optimization_barrier((attended, d_mix_y))
    d_mix_diag = send(d_mix_y, to_core)
    attn_out = dot(attended, out_map, NT)
    mid_state = token_f + (attn_out.reshape(segments, SHORT, D) * gate_one).reshape(-1, D)
    second_mod, second_back = jax.vjp(
        modulate, mid_state.reshape(segments, SHORT, D), last_four[:, 1:2], last_four[:, 2:3]
    )
    hidden_two = second_mod.reshape(-1, D).astype(bf)

    logits = dot(router_low, hidden_two, NT)
    experts = jnp.arange(ROUTED, dtype=jnp.int32)[:, None]
    named = (routes[:, 0][None] == experts) | (routes[:, 1][None] == experts)
    index = jnp.arange(TOK, dtype=jnp.int32)
    earlier = (index[:, None] < index[None, :]).astype(bf)
    place = jnp.dot(named.astype(bf), earlier, preferred_element_type=f32)
    masked = jnp.where(named, logits, -jnp.inf)
    expo = jnp.where(named, jnp.exp(logits - jnp.max(masked, axis=0, keepdims=True)), 0.0)
    gates = expo / jnp.sum(expo, axis=0, keepdims=True)
    meta = jnp.concatenate([jnp.where(named, place, -1.0), gates])

    hidden_core, meta_core = send(hidden_two, to_core), send(meta, to_core)
    hidden_y, meta_y = send(hidden_two, to_y), send(meta, to_y)
    meta_diag = send(meta, to_diag)
    hidden_y, meta_y, meta_core, meta_diag = lax.optimization_barrier(
        (hidden_y, meta_y, meta_core, meta_diag)
    )
    hidden_diag = send(hidden_y, to_core)
    place_ids = jnp.stack([narrow, z, x]).astype(jnp.int32)
    hiddens = (hidden_two, hidden_core, hidden_y, hidden_diag)
    d_mixes = (d_mixture, d_mix_core, d_mix_y, d_mix_diag)
    metas = (meta, meta_core, meta_y, meta_diag)
    hiddens, d_mixes, metas, gathered, moments = lax.optimization_barrier(
        (hiddens, d_mixes, metas, gathered, moments)
    )
    moments = lax.all_to_all(moments, AXES, 0, 0, tiled=True)
    *priors, g_shared = shared_units(hiddens, d_mixes, gathered)

    def back_x(z_, x_, y_, c_):
        return (z_, 0, y_, c_) if x_ == 1 else None

    def forth_x(z_, x_, y_, c_):
        return (z_, 1, y_, c_) if x_ == 0 else None

    def along_z(hops, sides=(0, 1)):
        table = dict(hops)

        def move(z_, x_, y_, c_):
            return (table[z_], x_, y_, c_) if z_ in table and x_ in sides else None

        return move

    def added(kept, other):
        return (kept.astype(f32) + other.astype(f32)).astype(bf)

    def shared_part(k):
        return lax.dynamic_slice_in_dim(g_shared, (narrow ^ k) * D, D, 1)

    def over_core(parts):
        over = (parts[2].astype(f32) + send(parts[3], to_core).astype(f32)).astype(bf)
        return parts[0].astype(f32) + send(parts[1], to_core).astype(f32), over

    gate = lax.optimization_barrier
    shared_parts = [shared_part(0)]
    shared_parts += [send(shared_part(k), NARROW_MOVES[k]) for k in (1, 2, 3)]
    *routed_outs, d_gate_rows, g_send, g_keep, g_second, g_third = routed_experts(
        place_ids, hiddens, d_mixes, metas, priors, gathered
    )
    routed_outs, shared_parts, moments, d_gate_rows, g_send = gate(
        (routed_outs, shared_parts, moments, d_gate_rows, g_send)
    )
    pairs_one, pairs_two, pairs_three = ((3, 2), (1, 0)), ((0, 1), (3, 2)), ((0, 1), (2, 3))
    received_one = send(g_send, to_x)
    step_three = send(g_third, along_z(pairs_three))
    d_rows = [d_gate_rows[0, :2]]
    d_rows += [send(d_gate_rows[k, :2], NARROW_MOVES[k]) for k in (1, 2, 3)]
    own_hidden, over_hidden = over_core(routed_outs[4:])
    own_hidden, over_hidden, mix_outs, shared_parts, g_keep, g_second, d_rows = gate(
        (own_hidden, over_hidden, routed_outs[:4], shared_parts, g_keep, g_second, d_rows)
    )
    far_hidden = send(over_hidden, to_y)
    shared_grad = jnp.concatenate(shared_parts, axis=1)
    received_second = send(g_second, back_x)
    received_shared = send(shared_grad, forth_x)
    own_mix, over_mix = over_core(mix_outs)
    d_gates = xor_blocks(jnp.stack(d_rows), 0, y, c).reshape(ROUTED, TOK)
    far_hidden, own_mix, over_mix, received_one, step_three, shared_grad, d_gates = gate(
        (far_hidden, own_mix, over_mix, received_one, step_three, shared_grad, d_gates)
    )
    held_one = added(g_keep, received_one)
    held_three = added(g_third, step_three)
    d_hidden = own_hidden + far_hidden.astype(f32)

    d_logits = gates * (d_gates - jnp.sum(gates * d_gates, axis=0, keepdims=True))
    d_logits = d_logits.astype(bf)
    g_router = jnp.dot(d_logits, hidden_two, preferred_element_type=f32)
    d_hidden = d_hidden + dot(d_logits, router_low, TN)
    d_mid_norm, d_shift_two, d_scale_two = second_back(d_hidden.reshape(segments, SHORT, D))
    d_mid = grad_out + d_mid_norm.reshape(-1, D)
    d_mid_seg = d_mid.reshape(segments, SHORT, D)
    d_gate_one = jnp.sum(d_mid_seg * attn_out.reshape(segments, SHORT, D), axis=1)
    d_attn = (d_mid_seg * gate_one).reshape(-1, D).astype(bf)
    g_out = dot(d_attn, attended, TN)
    d_attended = jnp.dot(d_attn, out_map, preferred_element_type=f32).astype(bf)
    d_attended, held_one, held_three, over_mix = gate(
        (d_attended, held_one, held_three, over_mix)
    )
    step_one = send(held_one, along_z(pairs_one))
    last_three = send(held_three, along_z(((1, 3),)))
    far_mix = send(over_mix, to_y)
    d_heads = attend_back_fast(resolution, projected, log_total, d_attended)
    d_heads, step_one, last_three, received_second, received_shared, far_mix = gate(
        (d_heads, step_one, last_three, received_second, received_shared, far_mix)
    )
    held_two = added(
        jnp.where(x == 0, g_second, shared_grad), jnp.where(x == 0, received_second, received_shared)
    )
    held_one = added(held_one, step_one)
    held_three = added(held_three, last_three)
    d_heads, held_one, held_two, held_three = gate((d_heads, held_one, held_two, held_three))

    def cross_x(z_, x_, y_, c_):
        return (z_, 0, y_, c_) if x_ == 1 and z_ == 3 else None

    step_two = send(held_two, along_z(pairs_two))
    last_one = send(held_one, along_z(((2, 0),)))
    cross_three = send(held_three, cross_x)
    mixture = own_mix + far_mix.astype(f32)
    output = (
        mid_state + (mixture.reshape(segments, SHORT, D) * gate_two).reshape(-1, D)
    ).astype(bf)
    d_gate_two = jnp.sum(grad_seg * mixture.reshape(segments, SHORT, D), axis=1)
    mods = jnp.stack([d_gate_one, d_shift_two[:, 0], d_scale_two[:, 0], d_gate_two])
    grad_in, dense_keep, dense_send, small = first_back_fast(
        place_ids,
        d_heads,
        hidden_one,
        tokens,
        d_mid,
        query_maps,
        first_two[:, 1],
        g_out,
        mods,
        cond_low.astype(f32),
        g_router,
    )

    dense_recv = send(dense_send, to_core)
    small, dense_recv = gate((small, dense_recv))
    dense = dense_keep + dense_recv.astype(f32)
    dense_far = send(pick(dense, 1 - y).astype(bf), to_y)
    small = lax.all_to_all(small, AXES, 0, 0, tiled=True)
    g_bias = jnp.sum(small[:, 0, D : D + 72], axis=0)
    dense_far, step_two = gate((dense_far, step_two))
    held_two = added(held_two, step_two)
    last_two = send(held_two, along_z(((1, 2),)))
    dense = pick(dense, y) + dense_far.astype(f32)
    dense_side = send(dense.astype(bf), back_x)
    pieces = (held_one, last_one, held_two, last_two, held_three, cross_three)
    dense = dense + dense_side.astype(f32)
    dense = dense + send(dense.astype(bf), along_z(pairs_two, (0,))).astype(f32)
    dense = dense + send(dense.astype(bf), along_z(((2, 1),), (0,))).astype(f32)

    state_bias = MOMENTUM_VECTOR * moment_bias + g_bias
    part_sum = jnp.sum(state_bias * state_bias)
    sum_high = part_sum.astype(bf)
    sum_low = (part_sum - sum_high.astype(f32)).astype(bf)

    extra = jnp.pad(jnp.stack([sum_high, sum_low])[None], ((0, 7), (0, D - 2)))
    grad_full, grad_cut = owned_grad(place_ids, pieces, dense, small.reshape(256, 512), extra)
    grad_parts = lax.all_to_all(grad_cut, AXES, 0, 0, tiled=True)

    ortho_cut = ortho_owned(place_ids, grad_full, moments)
    ortho_cut, grad_parts = lax.optimization_barrier((ortho_cut, grad_parts))
    ortho_parts = lax.all_to_all(ortho_cut, AXES, 0, 0, tiled=True)
    square_total = jnp.sum(grad_parts[:, 48, :2].astype(f32))

    step_value = step_count[0].astype(f32)
    decay = jnp.minimum(0.9999, (1.0 + step_value) / (10.0 + step_value))
    masters = (turned(w_square), turned(w_out), w_router, turned(w_up), turned(w_down))
    emas = (turned(ema_square), turned(ema_out), ema_router, turned(ema_up), turned(ema_down))
    updated = update(decay[None], grad_parts, ortho_parts, masters, moment_parts, emas)
    results = []
    for which in range(5):
        results += [
            array if which == 2 else turned(array) for array in updated[which::5]
        ]
    root_mean = jnp.sqrt(square_total / (6 * D) + 1e-05)
    master_bias = b_ada - RATE_VECTOR * state_bias / root_mean
    average_bias = decay * ema_bias + (1.0 - decay) * master_bias
    return (output, grad_in, *results, state_bias, master_bias, average_bias)


def solution(mesh):
    placed = (
        P((WIDE, NARROW), None),
        P((WIDE, NARROW), None),
        P((WIDE, NARROW), None),
        P((WIDE, NARROW)),
        P(),
        P((WIDE, NARROW), None),
        P(None, NARROW, WIDE),
        P(NARROW, WIDE),
        P(NARROW, WIDE),
        P(None, NARROW, WIDE),
        P(None, NARROW, WIDE),
        P((WIDE, NARROW)),
        P(None, NARROW, WIDE),
        P(NARROW, WIDE),
        P(NARROW, WIDE),
        P(None, NARROW, WIDE),
        P(None, NARROW, WIDE),
        P((WIDE, NARROW)),
        P(None, NARROW, WIDE),
        P(NARROW, WIDE),
        P(NARROW, WIDE),
        P(None, NARROW, WIDE),
        P(None, NARROW, WIDE),
        P((WIDE, NARROW)),
    )
    device_body = fast_device if dict(mesh.shape) == {WIDE: 8, NARROW: 4} else on_device
    return jax.shard_map(
        device_body,
        mesh=mesh,
        in_specs=placed,
        out_specs=(
            P((WIDE, NARROW), None),
            P((WIDE, NARROW), None),
            P(None, NARROW, WIDE),
            P(None, NARROW, WIDE),
            P(None, NARROW, WIDE),
            P(NARROW, WIDE),
            P(NARROW, WIDE),
            P(NARROW, WIDE),
            P(NARROW, WIDE),
            P(NARROW, WIDE),
            P(NARROW, WIDE),
            P(None, NARROW, WIDE),
            P(None, NARROW, WIDE),
            P(None, NARROW, WIDE),
            P(None, NARROW, WIDE),
            P(None, NARROW, WIDE),
            P(None, NARROW, WIDE),
            P((WIDE, NARROW)),
            P((WIDE, NARROW)),
            P((WIDE, NARROW)),
        ),
        check_vma=False,
    )
```
